32 devices in a mesh: seq: 16 (over z, y, core), head: 2 (over x).
Axes of the slice: x: 2, y: 2, z: 4, core: 2. Of those that a mesh axis runs over, the one named last changes fastest.
Arguments:
- attn_out: bfloat16 [2, 32, 64, 5120], P(None, 'seq', None, 'head'), may hold values from -40 to 40
- w_proj: bfloat16 [5120, 64], P('head'), may hold values from -0.078125 to 0.078125
- norm_gain: float32 [384], replicated, may hold values from 0.1 to 1.9
- entry_weight: bfloat16 [384, 3, 3, 3, 16], replicated, may hold values from -0.3125 to 0.3125
- conv_weight: bfloat16 [384, 3, 3, 3, 384], P('head'), may hold values from -0.0625 to 0.0625
- cotangent: bfloat16 [384, 2, 64, 128], P('head', None, 'seq'), may hold values from -0.09375 to 0.09375
Outputs:
- decoded: bfloat16 [384, 2, 64, 128], P('head', None, 'seq')
- weight_grad: float32 [384, 3, 3, 3, 384], P('head')
The draws below stay inside these ranges and needn't reach their ends.
All inputs are finite; a program needn't handle non-finite values.
Results may differ from the reference program's by a relative error of at most 0.0058.
Values may be sent and summed in bfloat16 or wider, within the bound.
No kernel may reach another device: no remote copies, remote signals or barrier semaphores. Data moves between devices by JAX's collectives and lax.ppermute only.
A program may use at most 64 MiB of HBM per device.

```python
import math
import jax
import jax.numpy as jnp
from jax import lax

DM = 5120
LAT = 16
CMID = 384
FRAMES = 2
WT = 64
NR = 32
NH = 64
NW = 128


def draw_attn_out(key, part):
    first_key, second_key, third_key = jax.random.split(key, 3)
    row_scale = jnp.exp(jax.random.uniform(second_key, (FRAMES, NR, WT, 1), minval=0.0, maxval=math.log(10.0)))
    col_scale = jnp.exp(jax.random.uniform(third_key, (1, 1, 1, DM), minval=0.0, maxval=math.log(10.0)))
    values = jnp.clip(jax.random.normal(first_key, (FRAMES, NR, WT, DM)), -4.0, 4.0)
    return jnp.clip(values * row_scale * col_scale / 10.0, -40.0, 40.0).astype(jnp.bfloat16)


def shard_levels(stream_key, dims, cuts, smallest, high):
    level, own = 1.0, jax.random.fold_in(stream_key, 6)
    for position, parts in cuts:
        draws = jnp.exp(jax.random.uniform(jax.random.fold_in(own, position), (parts,), jnp.float32, smallest / len(cuts), high / len(cuts)))
        level = level * jnp.repeat(draws, dims[position] // parts).reshape([-1 if axis == position else 1 for axis in range(len(dims))])
    return level


def centred(rng, extent, width, limit, cuts=(), kind=jnp.bfloat16):
    values = width * jax.random.normal(rng, extent, jnp.float32)
    if cuts:
        values = values * shard_levels(rng, extent, cuts, -0.22, 0.18)
    return jnp.clip(values, -limit, limit).astype(kind)


def setup_inputs(seed: int = 0) -> dict:
    arg_keys = jax.random.split(jax.random.key(seed), 7)
    attn_out = draw_attn_out(jax.random.fold_in(arg_keys[6], 71), 0)
    w_proj = centred(arg_keys[1], (DM, 4 * LAT), DM ** -0.5, 0.078125, ((0, 2),))
    norm_gain = jnp.clip(1.0 + 0.18 * jax.random.normal(arg_keys[2], (CMID,), jnp.float32), 0.1, 1.9)
    entry_weight = centred(arg_keys[3], (CMID, 3, 3, 3, LAT), (27 * LAT) ** -0.5, 0.3125)
    conv_weight = centred(arg_keys[4], (CMID, 3, 3, 3, CMID), (27 * CMID) ** -0.5, 0.0625, ((0, 2),))
    cotangent = centred(arg_keys[5], (CMID, FRAMES, NH, NW), 0.006, 0.09375, ((0, 2), (2, 16)))
    return {"attn_out": attn_out, "w_proj": w_proj, "norm_gain": norm_gain, "entry_weight": entry_weight, "conv_weight": conv_weight, "cotangent": cotangent}


def convolve_causal(inputs, weight):
    kernel = weight.transpose(0, 4, 1, 2, 3)
    result = lax.conv_general_dilated(inputs[None], kernel, (1, 1, 1), ((2, 0), (0, 0), (1, 1)), dimension_numbers=('NCDHW', 'OIDHW', 'NCDHW'), preferred_element_type=jnp.float32)
    return result[0]

def activate(hidden, norm_gain):
    inverse_rms = lax.rsqrt(lax.optimization_barrier(jnp.mean(hidden * hidden, axis=0, keepdims=True)) + 1e-06)
    return jax.nn.silu(hidden * inverse_rms * norm_gain[:, None, None, None]).astype(jnp.bfloat16)

def unpatchify(features, frames, tok_rows, tok_cols, latent_width):
    grid = features.astype(jnp.bfloat16).reshape(2, 2, latent_width, frames, tok_rows, tok_cols)
    grid = grid.transpose(2, 3, 4, 0, 5, 1)
    return grid.reshape(latent_width, frames, 2 * tok_rows, 2 * tok_cols)

def reference(attn_out, w_proj, norm_gain, entry_weight, conv_weight, cotangent):
    frames, tok_rows, tok_cols, model_width = attn_out.shape
    latent_width = entry_weight.shape[4]
    channels = entry_weight.shape[0]
    out_channels = conv_weight.shape[0]
    flattened = attn_out.reshape(frames * tok_rows * tok_cols, model_width)
    features = lax.dot_general(w_proj, flattened, (((0,), (1,)), ((), ())), preferred_element_type=jnp.float32)
    latent = unpatchify(features, frames, tok_rows, tok_cols, latent_width)
    heights = 2 * tok_rows
    widths = 2 * tok_cols
    latent_rows = jnp.pad(latent, ((0, 0), (0, 0), (1, 1), (0, 0)))
    act = activate(convolve_causal(latent_rows, entry_weight), norm_gain)
    act_rows = jnp.pad(act, ((0, 0), (0, 0), (1, 1), (0, 0)))
    decoded = convolve_causal(act_rows, conv_weight).astype(jnp.bfloat16)
    padded = jnp.pad(act_rows, ((0, 0), (2, 0), (0, 0), (1, 1)))
    upstream = cotangent.reshape(out_channels, frames * heights * widths)
    tap_grads = []
    for kernel_tap in range(27):
        depth_tap = kernel_tap // 9
        row_tap = kernel_tap // 3 % 3
        col_tap = kernel_tap % 3
        window = padded[:, depth_tap:depth_tap + frames, row_tap:row_tap + heights, col_tap:col_tap + widths].reshape(channels, -1)
        tap_grads.append(lax.dot_general(upstream, window, (((1,), (1,)), ((), ())), preferred_element_type=jnp.float32))
    weight_grad = jnp.stack(tap_grads, axis=1).reshape(conv_weight.shape)
    return (decoded, weight_grad)
```

```python
import functools

import jax
import jax.numpy as jnp
from jax import lax
from jax.experimental import pallas as pl
from jax.experimental.pallas import tpu as pltpu
from jax.sharding import PartitionSpec as P

LANES = 128
VMEM_LIMIT = 56 * 1024 * 1024
F32 = jnp.float32
BF16 = jnp.bfloat16


def params():
    return pltpu.CompilerParams(vmem_limit_bytes=VMEM_LIMIT)


def vmem():
    return pl.BlockSpec(memory_space=pltpu.VMEM)


def smem():
    return pl.BlockSpec(memory_space=pltpu.SMEM)


def xor_permute(x, axis, mask):
    return lax.ppermute(x, axis, [(i, i ^ mask) for i in range(lax.axis_size(axis))])


def dot(a, b):
    return lax.dot_general(a, b, (((1,), (0,)), ((), ())), preferred_element_type=F32)


def dot_t(a, b):
    return lax.dot_general(a, b, (((1,), (1,)), ((), ())), preferred_element_type=F32)


def unpatchify_kernel(frames, tok_rows, tok_cols, own_ref, other_ref, out_ref):
    latent_width = out_ref.shape[0]
    features = (own_ref[...] + other_ref[...]).astype(BF16)
    width = 2 * tok_cols
    span = tok_rows * tok_cols
    source = lax.broadcasted_iota(jnp.int32, (span, tok_rows * width), 0)
    target = lax.broadcasted_iota(jnp.int32, (span, tok_rows * width), 1)
    same_row = source // tok_cols == target // width
    column = source % tok_cols
    even = (same_row & (target % width == 2 * column)).astype(BF16)
    odd = (same_row & (target % width == 2 * column + 1)).astype(BF16)
    for frame in range(frames):
        tokens = features[:, frame * span : (frame + 1) * span]
        left = dot(tokens, even)
        right = dot(tokens, odd)
        for row in range(tok_rows):
            cols = slice(row * width, (row + 1) * width)
            for half in range(2):
                base = half * 2 * latent_width
                cells = (
                    left[base : base + latent_width, cols]
                    + right[base + latent_width : base + 2 * latent_width, cols]
                )
                at = (frame * 2 * tok_rows + 2 * row + half) * width
                out_ref[:, at : at + width] = cells.astype(BF16)


def shifted(tile, shift):
    if shift == 1:
        return tile
    lane = lax.broadcasted_iota(jnp.int32, tile.shape, 1)
    if shift == 0:
        return jnp.where(lane == 0, 0.0, pltpu.roll(tile, 1, 1))
    return jnp.where(lane == LANES - 1, 0.0, pltpu.roll(tile, LANES - 1, 1))


def place_latent(lat_ref, stack_ref, me, masks, frames, rows):
    latent_width = lat_ref.shape[1]
    total = stack_ref.shape[2]
    zeros = jnp.zeros((stack_ref.shape[1], 2 * LANES), BF16)
    for frame in range(frames):
        stack_ref[frame, :, 0 : 2 * LANES] = zeros
        stack_ref[frame, :, total - 2 * LANES : total] = zeros
    for index, mask in enumerate(masks):
        slab = me ^ mask
        for frame in range(frames):
            for row in range(rows):
                at = (frame * rows + row) * LANES
                tile = lat_ref[index, :, at : at + LANES].astype(F32)
                to = pl.multiple_of((slab * rows + row + 2) * LANES, LANES)
                for shift in range(3):
                    stack_ref[
                        frame,
                        shift * latent_width : (shift + 1) * latent_width,
                        pl.ds(to, LANES),
                    ] = shifted(tile, shift).astype(BF16)


def activation(stack_ref, weight_refs, gain, frame, first, count, height):
    pieces = []
    for source in range(max(0, frame - 2), frame + 1):
        for row_tap in range(3):
            at = pl.multiple_of((first + row_tap) * LANES, LANES)
            pieces.append(stack_ref[source, :, pl.ds(at, count * LANES)])
    patches = jnp.concatenate(pieces, axis=0)
    hidden = dot(weight_refs[frame][...], patches)
    mean = jnp.sum(hidden * hidden, axis=0, keepdims=True) * (1.0 / hidden.shape[0])
    row = first - 1 + lax.broadcasted_iota(jnp.int32, mean.shape, 1) // LANES
    inside = (row >= 0) & (row < height)
    inverse = jnp.where(inside, lax.rsqrt(mean + 1e-6), 0.0)
    half = hidden * inverse * (0.5 * gain)
    return (half + half * jnp.tanh(half)).astype(BF16)


def cotangent_kernel(
    frames, rows, half_rows, chips, pad_channels, me_ref, own_ref, other_ref, out_ref, flat_ref
):
    me = me_ref[0]
    first_slab = (me & 1) * (half_rows // rows)
    channels = own_ref.shape[1]
    group = 3 * pad_channels
    padded = -(-3 * group // 16) * 16
    lanes = (half_rows + 2) * LANES
    for frame in range(frames):
        for edge in (0, half_rows + 2):
            flat_ref[frame, :, edge * LANES : (edge + 2) * LANES] = jnp.zeros((group, 2 * LANES), F32)
    for index in range(half_rows // rows):
        relative = (first_slab + index) ^ me
        chip = relative >> 1
        core = relative & 1
        block = jnp.where(core == 0, own_ref[chip].astype(F32), other_ref[chip].astype(F32))
        for frame in range(frames):
            for row in range(rows):
                at = (frame * rows + row) * LANES
                tile = block[:, at : at + LANES]
                if pad_channels != channels:
                    tile = jnp.concatenate(
                        [tile, jnp.zeros((pad_channels - channels, LANES), F32)], axis=0
                    )
                to = (index * rows + row + 2) * LANES
                for tap in range(3):
                    flat_ref[frame, tap * pad_channels : (tap + 1) * pad_channels, to : to + LANES] = (
                        shifted(tile, 2 - tap)
                    )
    filler = [jnp.zeros((padded - 3 * group, LANES), F32)] if padded != 3 * group else []
    for frame in range(frames):
        for row in range(half_rows + 2):
            taps = [flat_ref[frame, :, (row + 2 - tap) * LANES : (row + 3 - tap) * LANES] for tap in range(3)]
            out_ref[frame * padded : (frame + 1) * padded, row * LANES : (row + 1) * LANES] = (
                jnp.concatenate(taps + filler, axis=0).astype(BF16)
            )


def gradient_kernel(
    frames, rows, half_rows, height, masks, real_rows, step_rows,
    me_ref, lat_ref, cot_ref, gain_ref, *refs,
):
    weight_refs = refs[:frames]
    keep_ref, send_ref, stack_ref, act_ref, sum_ref = refs[frames:]
    me = me_ref[0]
    core = me & 1
    place_latent(lat_ref, stack_ref, me, masks, frames, rows)
    gain = gain_ref[...]
    padded = cot_ref.shape[0] // frames
    start = core * half_rows
    steps = (half_rows + 2) // step_rows
    width = step_rows * LANES
    sum_ref[...] = jnp.zeros_like(sum_ref)
    for frame in range(frames):

        def fill(step, carry):
            at = pl.multiple_of(step * width, LANES)
            act_ref[:, pl.ds(at, width)] = activation(
                stack_ref, weight_refs, gain, frame, start + step * step_rows, step_rows, height
            )
            return carry

        lax.fori_loop(0, steps, fill, 0)
        last = min(frames, frame + 3)
        count = (last - frame) * padded

        def add(step, carry):
            at = pl.multiple_of(step * width, LANES)
            sum_ref[0:count, :] += dot_t(
                cot_ref[frame * padded : last * padded, pl.ds(at, width)],
                act_ref[:, pl.ds(at, width)],
            )
            return carry

        lax.fori_loop(0, steps, add, 0)
    keep_at = pl.multiple_of(core * padded, 16)
    send_at = pl.multiple_of((1 - core) * padded, 16)
    keep_ref[...] = sum_ref[pl.ds(keep_at, padded), :][:real_rows]
    send_ref[...] = sum_ref[pl.ds(send_at, padded), :][:real_rows].astype(BF16)


def decode_kernel(frames, rows, height, masks, me_ref, lat_ref, gain_ref, conv_ref, *refs):
    weight_refs = refs[:frames]
    out_ref, stack_ref, act_ref = refs[frames:]
    me = me_ref[0]
    place_latent(lat_ref, stack_ref, me, masks, frames, rows)
    gain = gain_ref[...]
    live = min(3, frames)
    ext = rows + 2
    for frame in range(frames):
        act = activation(stack_ref, weight_refs, gain, frame, me * rows, ext, height)
        for row in range(ext):
            tile = act[:, row * LANES : (row + 1) * LANES].astype(F32)
            for tap in range(3):
                act_ref[frame, tap, :, row * LANES : (row + 1) * LANES] = shifted(tile, tap).astype(BF16)
    for frame in range(frames):
        total = None
        for depth in range(max(0, 2 - frame), 3):
            source = frame + depth - 2
            for row_tap in range(3):
                for col_tap in range(3):
                    term = dot(
                        conv_ref[(depth - (3 - live)) * 9 + row_tap * 3 + col_tap],
                        act_ref[source, col_tap, :, row_tap * LANES : (row_tap + rows) * LANES],
                    )
                    total = term if total is None else total + term
        out_ref[:, frame * rows * LANES : (frame + 1) * rows * LANES] = total.astype(BF16)


def finish_kernel(live, masks, channels, me_ref, *refs):
    block_refs = refs[:-1]
    out_ref = refs[-1]
    me = me_ref[0]
    chip = me >> 1
    core = me & 1
    depth = pl.program_id(0)
    plane = 2 - depth

    @pl.when(depth < 3 - live)
    def _():
        out_ref[...] = jnp.zeros_like(out_ref)

    @pl.when(depth >= 3 - live)
    def _():
        for index, mask in enumerate(masks):
            at = pl.multiple_of((chip ^ mask) * channels, 8)
            mine = block_refs[0]
            other = block_refs[1]
            for tap in range(out_ref.shape[1]):

                @pl.when(plane == core)
                def _():
                    out_ref[0, tap, pl.ds(at, channels), :] = mine[index, tap].astype(F32)

                @pl.when(plane != core)
                def _():
                    out_ref[0, tap, pl.ds(at, channels), :] = other[index, tap].astype(F32)


def per_device(attn_out, w_proj, norm_gain, entry_weight, conv_weight, cotangent):
    frames, tok_rows, tok_cols, model_width = attn_out.shape
    latent_width = entry_weight.shape[4]
    channels = entry_weight.shape[0]
    out_channels = conv_weight.shape[0]
    slabs = lax.axis_size("seq")
    heads = lax.axis_size("head")
    chips = slabs // 2
    rows = 2 * tok_rows
    width = 2 * tok_cols
    height = rows * slabs
    half_rows = height // 2
    chip_channels = out_channels // chips
    pad_channels = -(-chip_channels // 8) * 8
    real_rows = 9 * pad_channels
    live = min(3, frames)
    me_index = lax.axis_index("seq")
    me = me_index.astype(jnp.int32).reshape(1)
    chip_bits = [b for b in (4, 8, 16, 32, 64, 128) if b < slabs] + [2]

    flat = cotangent.reshape(chips, chip_channels, frames * rows * width)
    chip = me_index // 2
    relative = jnp.stack(
        [lax.dynamic_index_in_dim(flat, chip ^ d, 0, keepdims=False) for d in range(chips)]
    )
    pieces = {(d, 0): relative[d] for d in range(chips)}
    for bit in chip_bits:
        step = bit // 2
        sends = sorted(k for k in pieces if k[0] & step)
        got = xor_permute(jnp.stack([pieces[k] for k in sends]), "seq", bit)
        kept = {k: v for k, v in pieces.items() if not k[0] & step}
        for position, (d, s) in enumerate(sends):
            kept[(d ^ step, s ^ step)] = got[position]
        pieces = kept
    own_cot = jnp.stack([pieces[(0, s)] for s in range(chips)])
    other_cot = xor_permute(own_cot, "seq", 1)
    padded = -(-real_rows // 16) * 16
    lanes = (half_rows + 2) * width
    cot = pl.pallas_call(
        functools.partial(cotangent_kernel, frames, rows, half_rows, chips, pad_channels),
        out_shape=jax.ShapeDtypeStruct((frames * padded, lanes), BF16),
        in_specs=[smem(), vmem(), vmem()],
        out_specs=vmem(),
        scratch_shapes=[pltpu.VMEM((frames, 3 * pad_channels, (half_rows + 4) * width), F32)],
        compiler_params=params(),
        name="cotangent",
    )(me, own_cot, other_cot)

    flattened = attn_out.reshape(frames * tok_rows * tok_cols, model_width)
    partial_sum = lax.dot_general(
        w_proj, flattened, (((0,), (1,)), ((), ())), preferred_element_type=F32
    )
    step = heads // 2
    other = jnp.zeros_like(partial_sum)
    while step >= 1:
        other = xor_permute(partial_sum, "head", step)
        if step > 1:
            partial_sum = partial_sum + other
        step //= 2
    latent = pl.pallas_call(
        functools.partial(unpatchify_kernel, frames, tok_rows, tok_cols),
        out_shape=jax.ShapeDtypeStruct((latent_width, frames * rows * width), BF16),
        in_specs=[vmem(), vmem()],
        out_specs=vmem(),
        compiler_params=params(),
        name="unpatchify",
    )(partial_sum, other)

    masks = [0]
    gathered = latent[None]
    for bit in chip_bits + [1]:
        gathered = jnp.concatenate([gathered, xor_permute(gathered, "seq", bit)], axis=0)
        masks = masks + [m ^ bit for m in masks]

    entry = entry_weight.reshape(channels, 3, 9 * latent_width)
    entries = [
        entry[:, max(0, 2 - f) :].reshape(channels, -1) for f in range(frames)
    ]
    gain = norm_gain.reshape(channels, 1)
    step_rows = 2
    keep, send = pl.pallas_call(
        functools.partial(
            gradient_kernel, frames, rows, half_rows, height, masks, real_rows, step_rows
        ),
        out_shape=(
            jax.ShapeDtypeStruct((real_rows, channels), F32),
            jax.ShapeDtypeStruct((real_rows, channels), BF16),
        ),
        in_specs=[smem(), vmem(), vmem(), vmem()] + [vmem()] * frames,
        out_specs=(vmem(), vmem()),
        scratch_shapes=[
            pltpu.VMEM((frames, 3 * latent_width, (height + 4) * width), BF16),
            pltpu.VMEM((channels, lanes), BF16),
            pltpu.VMEM((live * padded, channels), F32),
        ],
        compiler_params=params(),
        name="gradient",
    )(me, gathered, cot, gain, *entries)

    block = (keep + xor_permute(send, "seq", 1).astype(F32)).astype(BF16)

    far = [b for b in chip_bits if b != 2]
    far_masks = [0]
    for b in far:
        far_masks = far_masks + [m ^ b for m in far_masks]
    parts = [block] + [xor_permute(block, "seq", m) for m in far_masks[1:]]
    mine = jnp.stack(parts + [xor_permute(p, "seq", 2) for p in parts])
    chip_masks = [m // 2 for m in far_masks] + [(m ^ 2) // 2 for m in far_masks]
    theirs = xor_permute(mine, "seq", 1)
    shape = (chips, 9, pad_channels, channels)

    conv = conv_weight.transpose(1, 2, 3, 0, 4).reshape(27, out_channels, channels)
    decoded = pl.pallas_call(
        functools.partial(decode_kernel, frames, rows, height, masks),
        grid=(1,),
        out_shape=jax.ShapeDtypeStruct((out_channels, frames * rows * width), BF16),
        in_specs=[smem(), vmem(), vmem(), vmem()] + [vmem()] * frames,
        out_specs=vmem(),
        scratch_shapes=[
            pltpu.VMEM((frames, 3 * latent_width, (height + 4) * width), BF16),
            pltpu.VMEM((frames, 3, channels, (rows + 2) * width), BF16),
        ],
        compiler_params=params(),
        name="decode",
    )(me, gathered, gain, conv[(3 - live) * 9 :], *entries)

    grad = pl.pallas_call(
        functools.partial(finish_kernel, live, chip_masks, pad_channels),
        grid=(3, 3),
        out_shape=jax.ShapeDtypeStruct((3, 9, chips * pad_channels, channels), F32),
        in_specs=[smem()]
        + [
            pl.BlockSpec((chips, 3, pad_channels, channels), lambda a, b: (0, b, 0, 0)),
            pl.BlockSpec((chips, 3, pad_channels, channels), lambda a, b: (0, b, 0, 0)),
        ],
        out_specs=pl.BlockSpec((1, 3, chips * pad_channels, channels), lambda a, b: (a, b, 0, 0)),
        compiler_params=params(),
        name="finish",
    )(me, mine.reshape(shape), theirs.reshape(shape))
    if pad_channels != chip_channels:
        grad = grad.reshape(27, chips, pad_channels, channels)[:, :, :chip_channels]
    grad = grad.reshape(3, 3, 3, out_channels, channels).transpose(3, 0, 1, 2, 4)
    return decoded.reshape(out_channels, frames, rows, width), grad


def solution(mesh):
    return jax.shard_map(
        per_device,
        mesh=mesh,
        in_specs=(
            P(None, "seq", None, "head"),
            P("head", None),
            P(),
            P(),
            P("head", None, None, None, None),
            P("head", None, "seq", None),
        ),
        out_specs=(P("head", None, "seq", None), P("head", None, None, None, None)),
        check_vma=False,
    )
```

```python
import functools

import jax
import jax.numpy as jnp
from jax import lax
from jax.experimental import pallas as pl
from jax.experimental.pallas import tpu as pltpu
from jax.sharding import PartitionSpec as P

LANES = 128
VMEM_LIMIT = 56 * 1024 * 1024
F32 = jnp.float32
BF16 = jnp.bfloat16


def params():
    return pltpu.CompilerParams(vmem_limit_bytes=VMEM_LIMIT)


def vmem():
    return pl.BlockSpec(memory_space=pltpu.VMEM)


def smem():
    return pl.BlockSpec(memory_space=pltpu.SMEM)


def xor_permute(x, axis, mask):
    return lax.ppermute(x, axis, [(i, i ^ mask) for i in range(lax.axis_size(axis))])


def dot(a, b):
    return lax.dot_general(a, b, (((1,), (0,)), ((), ())), preferred_element_type=F32)


def dot_t(a, b):
    return lax.dot_general(a, b, (((1,), (1,)), ((), ())), preferred_element_type=F32)


def unpatchify_kernel(frames, tok_rows, tok_cols, own_ref, other_ref, out_ref):
    latent_width = out_ref.shape[0]
    features = (own_ref[...] + other_ref[...]).astype(BF16)
    width = 2 * tok_cols
    span = tok_rows * tok_cols
    source = lax.broadcasted_iota(jnp.int32, (span, tok_rows * width), 0)
    target = lax.broadcasted_iota(jnp.int32, (span, tok_rows * width), 1)
    same_row = source // tok_cols == target // width
    column = source % tok_cols
    even = (same_row & (target % width == 2 * column)).astype(BF16)
    odd = (same_row & (target % width == 2 * column + 1)).astype(BF16)
    for frame in range(frames):
        tokens = features[:, frame * span : (frame + 1) * span]
        left = dot(tokens, even)
        right = dot(tokens, odd)
        for row in range(tok_rows):
            cols = slice(row * width, (row + 1) * width)
            for half in range(2):
                base = half * 2 * latent_width
                cells = (
                    left[base : base + latent_width, cols]
                    + right[base + latent_width : base + 2 * latent_width, cols]
                )
                at = (frame * 2 * tok_rows + 2 * row + half) * width
                out_ref[:, at : at + width] = cells.astype(BF16)


def shifted(tile, shift):
    if shift == 1:
        return tile
    lane = lax.broadcasted_iota(jnp.int32, tile.shape, 1)
    if shift == 0:
        return jnp.where(lane == 0, 0.0, pltpu.roll(tile, 1, 1))
    return jnp.where(lane == LANES - 1, 0.0, pltpu.roll(tile, LANES - 1, 1))


def place_latent(lat_refs, mask_lists, stack_ref, me, frames, rows):
    latent_width = lat_refs[0].shape[1]
    total = stack_ref.shape[2]
    zeros = jnp.zeros((stack_ref.shape[1], 2 * LANES), BF16)
    for frame in range(frames):
        stack_ref[frame, :, 0 : 2 * LANES] = zeros
        stack_ref[frame, :, total - 2 * LANES : total] = zeros
    for lat_ref, masks in zip(lat_refs, mask_lists):
        for index, mask in enumerate(masks):
            slab = me ^ mask
            for frame in range(frames):
                for row in range(rows):
                    at = (frame * rows + row) * LANES
                    tile = lat_ref[index, :, at : at + LANES].astype(F32)
                    to = pl.multiple_of((slab * rows + row + 2) * LANES, LANES)
                    for shift in range(3):
                        stack_ref[
                            frame,
                            shift * latent_width : (shift + 1) * latent_width,
                            pl.ds(to, LANES),
                        ] = shifted(tile, shift).astype(BF16)


def hidden_rows(stack_ref, weight_ref, frame, first, count):
    pieces = []
    for source in range(max(0, frame - 2), frame + 1):
        for row_tap in range(3):
            at = pl.multiple_of((first + row_tap) * LANES, LANES)
            pieces.append(stack_ref[source, :, pl.ds(at, count * LANES)])
    return dot(weight_ref[...], jnp.concatenate(pieces, axis=0))


def activate_rows(hidden_ref, gain_ref, act_ref, base, top_row, count, height):
    channels = hidden_ref.shape[0]
    block = 16
    for index in range(count):
        at = pl.multiple_of((base + index) * LANES, LANES)
        hidden = hidden_ref[:, pl.ds(at, LANES)]
        mean = jnp.sum(hidden * hidden, axis=0, keepdims=True) * (1.0 / channels)
        row = top_row + base + index
        inside = ((row >= 0) & (row < height)).astype(F32)
        inverse = jnp.broadcast_to(lax.rsqrt(mean + 1e-6) * inside, (block, LANES))
        for at_channel in range(0, channels, block):
            chunk = slice(at_channel, at_channel + block)
            half = hidden_ref[chunk, pl.ds(at, LANES)] * inverse * gain_ref[chunk, :]
            act_ref[chunk, pl.ds(at, LANES)] = (half + half * jnp.tanh(half)).astype(BF16)


def cotangent_kernel(
    frames, rows, half_rows, pad_channels, mask_lists, me_ref, *refs
):
    block_refs = refs[:-2]
    out_ref, flat_ref = refs[-2:]
    me = me_ref[0]
    slabs_half = half_rows // rows
    first_slab = (me & 1) * slabs_half
    channels = block_refs[0].shape[1]
    group = 3 * pad_channels
    padded = out_ref.shape[0] // frames
    for frame in range(frames):
        for edge in (0, half_rows + 2):
            flat_ref[frame, :, edge * LANES : (edge + 2) * LANES] = jnp.zeros((group, 2 * LANES), F32)
    for block_ref, masks in zip(block_refs, mask_lists):
        for position, mask in enumerate(masks):
            index = (me ^ mask) - first_slab

            @pl.when((index >= 0) & (index < slabs_half))
            def _(block_ref=block_ref, position=position, index=index):
                for frame in range(frames):
                    for row in range(rows):
                        at = (frame * rows + row) * LANES
                        tile = block_ref[position, :, at : at + LANES].astype(F32)
                        if pad_channels != channels:
                            tile = jnp.concatenate(
                                [tile, jnp.zeros((pad_channels - channels, LANES), F32)], axis=0
                            )
                        to = pl.multiple_of((index * rows + row + 2) * LANES, LANES)
                        for tap in range(3):
                            flat_ref[
                                frame, tap * pad_channels : (tap + 1) * pad_channels, pl.ds(to, LANES)
                            ] = shifted(tile, 2 - tap)

    filler = [jnp.zeros((padded - 3 * group, LANES), F32)] if padded != 3 * group else []
    for frame in range(frames):
        for row in range(half_rows + 2):
            taps = [flat_ref[frame, :, (row + 2 - tap) * LANES : (row + 3 - tap) * LANES] for tap in range(3)]
            out_ref[frame * padded : (frame + 1) * padded, row * LANES : (row + 1) * LANES] = (
                jnp.concatenate(taps + filler, axis=0).astype(BF16)
            )


def gradient_kernel(frames, rows, half_rows, height, mask_lists, real_rows, *refs):
    lat_count = len(mask_lists)
    me_ref, cot_hbm, gain_ref = refs[:3]
    weight_refs = refs[3 : 3 + frames]
    lat_refs = refs[3 + frames : 3 + frames + lat_count]
    keep_ref, send_ref = refs[3 + frames + lat_count : 5 + frames + lat_count]
    stack_ref, hid_a, hid_b, act_a, act_b, sum_ref, wide_gain, cot_ref, sem = refs[5 + frames + lat_count :]
    load = pltpu.make_async_copy(cot_hbm, cot_ref, sem)
    load.start()
    me = me_ref[0]
    core = me & 1
    place_latent(lat_refs, mask_lists, stack_ref, me, frames, rows)
    channels = sum_ref.shape[1]
    wide_gain[...] = jnp.broadcast_to(0.5 * gain_ref[...], wide_gain.shape)
    padded = cot_ref.shape[0] // frames
    start = core * half_rows
    ext = half_rows + 2
    count = max(d for d in range(1, 18) if ext % d == 0)
    width = count * LANES
    hidden = (hid_a, hid_b)
    acts = (act_a, act_b)
    hid_a[...] = hidden_rows(stack_ref, weight_refs[0], 0, start, ext)
    sum_ref[...] = jnp.zeros_like(sum_ref)
    for frame in range(frames):
        if frame == 1:
            load.wait()

        def chunk(step, carry):
            at = pl.multiple_of(step * width, LANES)
            if frame + 1 < frames:
                hidden[(frame + 1) % 2][:, pl.ds(at, width)] = hidden_rows(
                    stack_ref, weight_refs[frame + 1], frame + 1, start + step * count, count
                )
            if frame > 0:
                last = min(frames, frame + 2)
                sum_ref[0 : (last - frame + 1) * padded, :] += dot_t(
                    cot_ref[(frame - 1) * padded : last * padded, pl.ds(at, width)],
                    acts[(frame - 1) % 2][:, pl.ds(at, width)],
                )
            activate_rows(
                hidden[frame % 2], wide_gain, acts[frame % 2], step * count, start - 1, count, height
            )
            return carry

        lax.fori_loop(0, ext // count, chunk, 0)
    if frames == 1:
        load.wait()
    final = frames - 1
    sum_ref[0:padded, :] += dot_t(cot_ref[final * padded : frames * padded, :], acts[final % 2][...])
    keep_at = pl.multiple_of(core * padded, 16)
    send_at = pl.multiple_of((1 - core) * padded, 16)
    keep_ref[...] = sum_ref[pl.ds(keep_at, padded), :][:real_rows]
    send_ref[...] = sum_ref[pl.ds(send_at, padded), :][:real_rows].astype(BF16)


def decode_kernel(frames, rows, height, mask_lists, *refs):
    lat_count = len(mask_lists)
    me_ref, gain_ref, conv_hbm = refs[:3]
    weight_refs = refs[3 : 3 + frames]
    lat_refs = refs[3 + frames : 3 + frames + lat_count]
    out_ref, stack_ref, hid_ref, flat_ref, act_ref, wide_gain, conv_ref, sem = refs[3 + frames + lat_count :]
    live = conv_ref.shape[0] // 9
    load = pltpu.make_async_copy(conv_hbm.at[pl.ds((3 - live) * 9, live * 9)], conv_ref, sem)
    load.start()
    me = me_ref[0]
    place_latent(lat_refs, mask_lists, stack_ref, me, frames, rows)
    wide_gain[...] = jnp.broadcast_to(0.5 * gain_ref[...], wide_gain.shape)
    ext = rows + 2
    for frame in range(frames):
        hid_ref[...] = hidden_rows(stack_ref, weight_refs[frame], frame, me * rows, ext)
        activate_rows(hid_ref, wide_gain, flat_ref, 0, me * rows - 1, ext, height)
        for row in range(ext):
            tile = flat_ref[:, row * LANES : (row + 1) * LANES].astype(F32)
            for tap in range(3):
                act_ref[frame, tap, :, row * LANES : (row + 1) * LANES] = shifted(tile, tap).astype(BF16)
    load.wait()
    for frame in range(frames):
        total = None
        for depth in range(max(0, 2 - frame), 3):
            source = frame + depth - 2
            for row_tap in range(3):
                for col_tap in range(3):
                    term = dot(
                        conv_ref[(depth - (3 - live)) * 9 + row_tap * 3 + col_tap],
                        act_ref[source, col_tap, :, row_tap * LANES : (row_tap + rows) * LANES],
                    )
                    total = term if total is None else total + term
        out_ref[:, frame * rows * LANES : (frame + 1) * rows * LANES] = total.astype(BF16)


def finish_kernel(first, pieces, blank, me_ref, *refs):
    count = len(pieces)
    piece_refs = refs[:count]
    out_hbm, wide_ref, zero_ref, sems, zero_sem = refs[count + (0 if first else 1) :]
    me = me_ref[0]
    channels = wide_ref.shape[2]
    copies = []
    if first and blank:
        zero_ref[...] = jnp.zeros_like(zero_ref)
        for plane in range(blank):
            for tap in range(9):
                copies.append(
                    pltpu.make_async_copy(zero_ref, out_hbm.at[plane, tap], zero_sem.at[plane * 9 + tap])
                )
                copies[-1].start()
    for index, mask in enumerate(pieces):
        source = me ^ mask
        wide_ref[index] = piece_refs[index][...].astype(F32)
        at = pl.multiple_of((source >> 1) * channels, 8)
        copy = pltpu.make_async_copy(
            wide_ref.at[index], out_hbm.at[2 - (source & 1), :, pl.ds(at, channels), :], sems.at[index]
        )
        copy.start()
        copies.append(copy)
    for copy in copies:
        copy.wait()


def per_device(attn_out, w_proj, norm_gain, entry_weight, conv_weight, cotangent):
    frames, tok_rows, tok_cols, model_width = attn_out.shape
    latent_width = entry_weight.shape[4]
    channels = entry_weight.shape[0]
    out_channels = conv_weight.shape[0]
    slabs = lax.axis_size("seq")
    heads = lax.axis_size("head")
    chips = slabs // 2
    rows = 2 * tok_rows
    width = 2 * tok_cols
    height = rows * slabs
    half_rows = height // 2
    chip_channels = out_channels // chips
    pad_channels = -(-chip_channels // 8) * 8
    real_rows = 9 * pad_channels
    padded = -(-real_rows // 16) * 16
    lanes = (half_rows + 2) * width
    live = min(3, frames)
    me_index = lax.axis_index("seq")
    me = me_index.astype(jnp.int32).reshape(1)
    top = slabs // 2
    rest = [m for m in range(2, top, 2)]

    flat = cotangent.reshape(chips, chip_channels, frames * rows * width)
    chip = me_index // 2

    def wanted(side):
        return jnp.stack(
            [
                lax.dynamic_index_in_dim(flat, chip ^ ((m ^ side) // 2), 0, keepdims=False)
                for m in [0] + rest
            ]
        )

    near, far = wanted(0), wanted(top)
    got = xor_permute(far, "seq", top)
    cot_blocks = []
    cot_masks = []
    for position, mask in enumerate([0] + rest):
        pair = jnp.stack([near[position], got[position]])
        cot_blocks.append(pair if mask == 0 else xor_permute(pair, "seq", mask))
        cot_masks.append([mask, mask ^ top])
    cot_blocks = cot_blocks + [xor_permute(b, "seq", 1) for b in cot_blocks]
    cot_masks = cot_masks + [[m ^ 1 for m in masks] for masks in cot_masks]
    cot = pl.pallas_call(
        functools.partial(cotangent_kernel, frames, rows, half_rows, pad_channels, cot_masks),
        out_shape=jax.ShapeDtypeStruct((frames * padded, lanes), BF16),
        in_specs=[smem()] + [vmem()] * len(cot_blocks),
        out_specs=vmem(),
        scratch_shapes=[pltpu.VMEM((frames, 3 * pad_channels, (half_rows + 4) * width), F32)],
        compiler_params=params(),
        name="cotangent",
    )(me, *cot_blocks)

    flattened = attn_out.reshape(frames * tok_rows * tok_cols, model_width)
    partial_sum = lax.dot_general(
        w_proj, flattened, (((0,), (1,)), ((), ())), preferred_element_type=F32
    )
    step = heads // 2
    other = jnp.zeros_like(partial_sum)
    while step >= 1:
        other = xor_permute(partial_sum, "head", step)
        if step > 1:
            partial_sum = partial_sum + other
        step //= 2
    latent = pl.pallas_call(
        functools.partial(unpatchify_kernel, frames, tok_rows, tok_cols),
        out_shape=jax.ShapeDtypeStruct((latent_width, frames * rows * width), BF16),
        in_specs=[vmem(), vmem()],
        out_specs=vmem(),
        compiler_params=params(),
        name="unpatchify",
    )(partial_sum, other)

    pair = jnp.stack([latent, xor_permute(latent, "seq", top)])
    lats = [pair] + [xor_permute(pair, "seq", m) for m in rest]
    lat_masks = [[m, m ^ top] for m in [0] + rest]
    lats = lats + [xor_permute(b, "seq", 1) for b in lats]
    lat_masks = lat_masks + [[m ^ 1 for m in masks] for masks in lat_masks]

    entry = entry_weight.reshape(channels, 3, 9 * latent_width)
    entries = [entry[:, max(0, 2 - f) :].reshape(channels, -1) for f in range(frames)]
    gain = norm_gain.reshape(channels, 1)
    keep, send = pl.pallas_call(
        functools.partial(gradient_kernel, frames, rows, half_rows, height, lat_masks, real_rows),
        out_shape=(
            jax.ShapeDtypeStruct((real_rows, channels), F32),
            jax.ShapeDtypeStruct((real_rows, channels), BF16),
        ),
        in_specs=[smem(), pl.BlockSpec(memory_space=pl.ANY), vmem()]
        + [vmem()] * (frames + len(lats)),
        out_specs=(vmem(), vmem()),
        scratch_shapes=[
            pltpu.VMEM((frames, 3 * latent_width, (height + 4) * width), BF16),
            pltpu.VMEM((channels, lanes), F32),
            pltpu.VMEM((channels, lanes), F32),
            pltpu.VMEM((channels, lanes), BF16),
            pltpu.VMEM((channels, lanes), BF16),
            pltpu.VMEM((live * padded, channels), F32),
            pltpu.VMEM((channels, LANES), F32),
            pltpu.VMEM((frames * padded, lanes), BF16),
            pltpu.SemaphoreType.DMA(()),
        ],
        compiler_params=params(),
        name="gradient",
    )(me, cot, gain, *entries, *lats)
    block = (keep + xor_permute(send, "seq", 1).astype(F32)).astype(BF16)

    columns = [m for m in range(0, slabs, 4)]
    direct = [block] + [xor_permute(block, "seq", m) for m in columns[1:]]
    beside = xor_permute(block, "seq", 2)
    held = lax.optimization_barrier((block, *lats))[1:]
    conv = conv_weight.transpose(1, 2, 3, 0, 4).reshape(27, out_channels, channels)
    decoded = pl.pallas_call(
        functools.partial(decode_kernel, frames, rows, height, lat_masks),
        out_shape=jax.ShapeDtypeStruct((out_channels, frames * rows * width), BF16),
        in_specs=[smem(), vmem(), pl.BlockSpec(memory_space=pl.ANY)]
        + [vmem()] * (frames + len(lats)),
        out_specs=vmem(),
        scratch_shapes=[
            pltpu.VMEM((frames, 3 * latent_width, (height + 4) * width), BF16),
            pltpu.VMEM((channels, (rows + 2) * width), F32),
            pltpu.VMEM((channels, (rows + 2) * width), BF16),
            pltpu.VMEM((frames, 3, channels, (rows + 2) * width), BF16),
            pltpu.VMEM((channels, LANES), F32),
            pltpu.VMEM((live * 9, out_channels, channels), BF16),
            pltpu.SemaphoreType.DMA(()),
        ],
        compiler_params=params(),
        name="decode",
    )(me, gain, conv, *entries, *held)
    decoded = decoded.reshape(out_channels, frames, rows, width)

    blank = 3 - live
    shape = (9, pad_channels, channels)
    grad_shape = (3, 9, chips * pad_channels, channels)

    def finish(parts, masks, grad=None):
        first = grad is None
        return pl.pallas_call(
            functools.partial(finish_kernel, first, masks, blank),
            out_shape=jax.ShapeDtypeStruct(grad_shape, F32),
            in_specs=[smem()]
            + [vmem()] * len(parts)
            + ([] if first else [pl.BlockSpec(memory_space=pl.ANY)]),
            out_specs=pl.BlockSpec(memory_space=pl.ANY),
            scratch_shapes=[
                pltpu.VMEM((len(parts),) + shape, F32),
                pltpu.VMEM((chips * pad_channels, channels), F32),
                pltpu.SemaphoreType.DMA((len(parts),)),
                pltpu.SemaphoreType.DMA((max(1, 9 * blank),)),
            ],
            input_output_aliases={} if first else {len(parts) + 1: 0},
            compiler_params=params(),
            name="finish",
        )(me, *[p.reshape(shape) for p in parts], *([] if first else [grad]))

    early = [block, beside]
    early_masks = [0, 2]
    early = early + [xor_permute(p, "seq", 1) for p in early]
    early_masks = early_masks + [m ^ 1 for m in early_masks]
    grad = finish(early, early_masks)
    after = lax.optimization_barrier((decoded, grad, *direct[1:]))
    decoded, grad, late = after[0], after[1], list(after[2:])
    late_masks = columns[1:]
    late = late + [xor_permute(p, "seq", 2) for p in late]
    late_masks = late_masks + [m ^ 2 for m in late_masks]
    late = late + [xor_permute(p, "seq", 1) for p in late]
    late_masks = late_masks + [m ^ 1 for m in late_masks]
    grad = finish(late, late_masks, grad)
    if pad_channels != chip_channels:
        grad = grad.reshape(27, chips, pad_channels, channels)[:, :, :chip_channels]
    grad = grad.reshape(3, 3, 3, out_channels, channels).transpose(3, 0, 1, 2, 4)
    return decoded, grad


def solution(mesh):
    return jax.shard_map(
        per_device,
        mesh=mesh,
        in_specs=(
            P(None, "seq", None, "head"),
            P("head", None),
            P(),
            P(),
            P("head", None, None, None, None),
            P("head", None, "seq", None),
        ),
        out_specs=(P("head", None, "seq", None), P("head", None, None, None, None)),
        check_vma=False,
    )
```

```python
import functools

import jax
import jax.numpy as jnp
from jax import lax
from jax.experimental import pallas as pl
from jax.experimental.pallas import tpu as pltpu
from jax.sharding import PartitionSpec as P

LANES = 128
VMEM_LIMIT = 56 * 1024 * 1024
F32 = jnp.float32
BF16 = jnp.bfloat16


def params():
    return pltpu.CompilerParams(vmem_limit_bytes=VMEM_LIMIT)


def vmem():
    return pl.BlockSpec(memory_space=pltpu.VMEM)


def smem():
    return pl.BlockSpec(memory_space=pltpu.SMEM)


def xor_permute(x, axis, mask):
    return lax.ppermute(x, axis, [(i, i ^ mask) for i in range(lax.axis_size(axis))])


def dot(a, b):
    return lax.dot_general(a, b, (((1,), (0,)), ((), ())), preferred_element_type=F32)


def dot_t(a, b):
    return lax.dot_general(a, b, (((1,), (1,)), ((), ())), preferred_element_type=F32)


def unpatchify_kernel(frames, tok_rows, tok_cols, own_ref, other_ref, out_ref):
    latent_width = out_ref.shape[0]
    features = (own_ref[...] + other_ref[...]).astype(BF16)
    width = 2 * tok_cols
    span = tok_rows * tok_cols
    source = lax.broadcasted_iota(jnp.int32, (span, tok_rows * width), 0)
    target = lax.broadcasted_iota(jnp.int32, (span, tok_rows * width), 1)
    same_row = source // tok_cols == target // width
    column = source % tok_cols
    even = (same_row & (target % width == 2 * column)).astype(BF16)
    odd = (same_row & (target % width == 2 * column + 1)).astype(BF16)
    for frame in range(frames):
        tokens = features[:, frame * span : (frame + 1) * span]
        left = dot(tokens, even)
        right = dot(tokens, odd)
        for row in range(tok_rows):
            cols = slice(row * width, (row + 1) * width)
            for half in range(2):
                base = half * 2 * latent_width
                cells = (
                    left[base : base + latent_width, cols]
                    + right[base + latent_width : base + 2 * latent_width, cols]
                )
                at = (frame * 2 * tok_rows + 2 * row + half) * width
                out_ref[:, at : at + width] = cells.astype(BF16)


def shifted(tile, shift):
    if shift == 1:
        return tile
    lane = lax.broadcasted_iota(jnp.int32, tile.shape, 1)
    if shift == 0:
        return jnp.where(lane == 0, 0.0, pltpu.roll(tile, 1, 1))
    return jnp.where(lane == LANES - 1, 0.0, pltpu.roll(tile, LANES - 1, 1))


def fetch(piece_refs, mask_lists, slot_ref, sems):
    copies = []
    for index, (piece_ref, masks) in enumerate(zip(piece_refs, mask_lists)):
        for position, mask in enumerate(masks):
            copies.append(
                pltpu.make_async_copy(
                    piece_ref.at[position], slot_ref.at[mask], sems.at[index * len(masks) + position]
                )
            )
    for copy in copies:
        copy.start()
    return copies


def place_latent(slot_ref, stack_ref, me, first_slab, slab_count, frames, rows, slabs):
    latent_width = slot_ref.shape[1]
    for offset in range(-1, slab_count + 1):
        slab = first_slab + offset
        inside = ((slab >= 0) & (slab < slabs)).astype(F32)
        source = jnp.clip(slab, 0, slabs - 1) ^ me
        needed = range(rows)
        if offset == -1:
            needed = range(rows - 2, rows)
        if offset == slab_count:
            needed = range(2)
        for frame in range(frames):
            for row in needed:
                at = (frame * rows + row) * LANES
                tile = slot_ref[source, :, at : at + LANES].astype(F32)
                if offset in (-1, slab_count):
                    tile = tile * inside
                to = (offset * rows + row + 2) * LANES
                for shift in range(3):
                    stack_ref[
                        frame, shift * latent_width : (shift + 1) * latent_width, to : to + LANES
                    ] = shifted(tile, shift).astype(BF16)


def hidden_rows(stack_ref, weight_ref, frame, first, count):
    pieces = []
    for source in range(max(0, frame - 2), frame + 1):
        for row_tap in range(3):
            at = pl.multiple_of((first + row_tap) * LANES, LANES)
            pieces.append(stack_ref[source, :, pl.ds(at, count * LANES)])
    return dot(weight_ref[...], jnp.concatenate(pieces, axis=0))


def activate_rows(hidden_ref, gain_ref, act_ref, base, top_row, count, height):
    channels = hidden_ref.shape[0]
    block = 16
    for index in range(count):
        at = pl.multiple_of((base + index) * LANES, LANES)
        hidden = hidden_ref[:, pl.ds(at, LANES)]
        mean = jnp.sum(hidden * hidden, axis=0, keepdims=True) * (1.0 / channels)
        row = top_row + base + index
        inside = ((row >= 0) & (row < height)).astype(F32)
        inverse = jnp.broadcast_to(lax.rsqrt(mean + 1e-6) * inside, (block, LANES))
        for at_channel in range(0, channels, block):
            chunk = slice(at_channel, at_channel + block)
            half = hidden_ref[chunk, pl.ds(at, LANES)] * inverse * gain_ref[chunk, :]
            act_ref[chunk, pl.ds(at, LANES)] = (half + half * jnp.tanh(half)).astype(BF16)


def place_cotangent(slot_ref, flat_ref, out_ref, me, first_slab, slab_count, frames, rows, pad_channels):
    channels = slot_ref.shape[1]
    half_rows = slab_count * rows
    group = 3 * pad_channels
    padded = out_ref.shape[0] // frames
    for frame in range(frames):
        for edge in (0, half_rows + 2):
            flat_ref[frame, :, edge * LANES : (edge + 2) * LANES] = jnp.zeros((group, 2 * LANES), F32)
    for offset in range(slab_count):
        source = (first_slab + offset) ^ me
        for frame in range(frames):
            for row in range(rows):
                at = (frame * rows + row) * LANES
                tile = slot_ref[source, :, at : at + LANES].astype(F32)
                if pad_channels != channels:
                    tile = jnp.concatenate(
                        [tile, jnp.zeros((pad_channels - channels, LANES), F32)], axis=0
                    )
                to = (offset * rows + row + 2) * LANES
                for tap in range(3):
                    flat_ref[frame, tap * pad_channels : (tap + 1) * pad_channels, to : to + LANES] = (
                        shifted(tile, 2 - tap)
                    )
    filler = [jnp.zeros((padded - 3 * group, LANES), F32)] if padded != 3 * group else []
    for frame in range(frames):
        for row in range(half_rows + 2):
            taps = [flat_ref[frame, :, (row + 2 - tap) * LANES : (row + 3 - tap) * LANES] for tap in range(3)]
            out_ref[frame * padded : (frame + 1) * padded, row * LANES : (row + 1) * LANES] = (
                jnp.concatenate(taps + filler, axis=0).astype(BF16)
            )


def gradient_kernel(frames, rows, slabs, lat_masks, cot_masks, real_rows, pad_channels, *refs):
    me_ref, gain_ref = refs[:2]
    refs = refs[2:]
    weight_refs, refs = refs[:frames], refs[frames:]
    lat_refs, refs = refs[: len(lat_masks)], refs[len(lat_masks) :]
    cot_refs, refs = refs[: len(cot_masks)], refs[len(cot_masks) :]
    keep_ref, send_ref, lat_slots, cot_slots, stack_ref, flat_ref, cot_ref = refs[:7]
    hid_a, hid_b, act_a, act_b, sum_ref, wide_gain, lat_sems, cot_sems = refs[7:]
    lat_copies = fetch(lat_refs, lat_masks, lat_slots, lat_sems)
    cot_copies = fetch(cot_refs, cot_masks, cot_slots, cot_sems)
    me = me_ref[0]
    core = me & 1
    slab_count = slabs // 2
    half_rows = slab_count * rows
    height = slabs * rows
    first_slab = core * slab_count
    padded = cot_ref.shape[0] // frames
    top_row = core * half_rows - 1
    ext = half_rows + 2
    count = max(d for d in range(1, 18) if ext % d == 0)
    width = count * LANES
    hidden = (hid_a, hid_b)
    acts = (act_a, act_b)
    wide_gain[...] = jnp.broadcast_to(0.5 * gain_ref[...], wide_gain.shape)
    sum_ref[...] = jnp.zeros_like(sum_ref)
    for copy in lat_copies:
        copy.wait()
    place_latent(lat_slots, stack_ref, me, first_slab, slab_count, frames, rows, slabs)
    for copy in cot_copies:
        copy.wait()
    hid_a[...] = hidden_rows(stack_ref, weight_refs[0], 0, 0, ext)
    place_cotangent(
        cot_slots, flat_ref, cot_ref, me, first_slab, slab_count, frames, rows, pad_channels
    )
    for frame in range(frames):

        def chunk(step, carry):
            at = pl.multiple_of(step * width, LANES)
            if frame + 1 < frames:
                hidden[(frame + 1) % 2][:, pl.ds(at, width)] = hidden_rows(
                    stack_ref, weight_refs[frame + 1], frame + 1, step * count, count
                )
            if frame > 0:
                last = min(frames, frame + 2)
                sum_ref[0 : (last - frame + 1) * padded, :] += dot_t(
                    cot_ref[(frame - 1) * padded : last * padded, pl.ds(at, width)],
                    acts[(frame - 1) % 2][:, pl.ds(at, width)],
                )
            activate_rows(
                hidden[frame % 2], wide_gain, acts[frame % 2], step * count, top_row, count, height
            )
            return carry

        lax.fori_loop(0, ext // count, chunk, 0)
    final = frames - 1
    sum_ref[0:padded, :] += dot_t(cot_ref[final * padded : frames * padded, :], acts[final % 2][...])
    keep_at = pl.multiple_of(core * padded, 16)
    send_at = pl.multiple_of((1 - core) * padded, 16)
    keep_ref[...] = sum_ref[pl.ds(keep_at, padded), :][:real_rows]
    send_ref[...] = sum_ref[pl.ds(send_at, padded), :][:real_rows].astype(BF16)


def decode_kernel(frames, rows, slabs, lat_masks, *refs):
    me_ref, gain_ref, conv_hbm = refs[:3]
    refs = refs[3:]
    weight_refs, refs = refs[:frames], refs[frames:]
    lat_refs, refs = refs[: len(lat_masks)], refs[len(lat_masks) :]
    out_ref, lat_slots, stack_ref, hid_ref, flat_ref, act_ref, wide_gain, conv_ref, lat_sems, sem = refs
    live = conv_ref.shape[0] // 9
    load = pltpu.make_async_copy(conv_hbm.at[pl.ds((3 - live) * 9, live * 9)], conv_ref, sem)
    load.start()
    lat_copies = fetch(lat_refs, lat_masks, lat_slots, lat_sems)
    me = me_ref[0]
    height = slabs * rows
    wide_gain[...] = jnp.broadcast_to(0.5 * gain_ref[...], wide_gain.shape)
    for copy in lat_copies:
        copy.wait()
    place_latent(lat_slots, stack_ref, me, me, 1, frames, rows, slabs)
    ext = rows + 2
    for frame in range(frames):
        hid_ref[...] = hidden_rows(stack_ref, weight_refs[frame], frame, 0, ext)
        activate_rows(hid_ref, wide_gain, flat_ref, 0, me * rows - 1, ext, height)
        for row in range(ext):
            tile = flat_ref[:, row * LANES : (row + 1) * LANES].astype(F32)
            for tap in range(3):
                act_ref[frame, tap, :, row * LANES : (row + 1) * LANES] = shifted(tile, tap).astype(BF16)
    load.wait()
    for frame in range(frames):
        kernels = []
        inputs = []
        for depth in range(max(0, 2 - frame), 3):
            for row_tap in range(3):
                for col_tap in range(3):
                    kernels.append(conv_ref[(depth - (3 - live)) * 9 + row_tap * 3 + col_tap])
                    inputs.append(
                        act_ref[frame + depth - 2, col_tap, :, row_tap * LANES : (row_tap + rows) * LANES]
                    )
        total = dot(jnp.concatenate(kernels, axis=1), jnp.concatenate(inputs, axis=0))
        out_ref[:, frame * rows * LANES : (frame + 1) * rows * LANES] = total.astype(BF16)


def finish_kernel(first, pieces, blank, me_ref, *refs):
    count = len(pieces)
    piece_refs = refs[:count]
    out_hbm, wide_ref, zero_ref, sems, zero_sem = refs[count + (0 if first else 1) :]
    me = me_ref[0]
    channels = wide_ref.shape[2]
    copies = []
    if first and blank:
        zero_ref[...] = jnp.zeros_like(zero_ref)
        for plane in range(blank):
            for tap in range(9):
                copies.append(
                    pltpu.make_async_copy(zero_ref, out_hbm.at[plane, tap], zero_sem.at[plane * 9 + tap])
                )
                copies[-1].start()
    for index, mask in enumerate(pieces):
        source = me ^ mask
        wide_ref[index] = piece_refs[index][...].astype(F32)
        at = pl.multiple_of((source >> 1) * channels, 8)
        copy = pltpu.make_async_copy(
            wide_ref.at[index], out_hbm.at[2 - (source & 1), :, pl.ds(at, channels), :], sems.at[index]
        )
        copy.start()
        copies.append(copy)
    for copy in copies:
        copy.wait()


def per_device(attn_out, w_proj, norm_gain, entry_weight, conv_weight, cotangent):
    frames, tok_rows, tok_cols, model_width = attn_out.shape
    latent_width = entry_weight.shape[4]
    channels = entry_weight.shape[0]
    out_channels = conv_weight.shape[0]
    slabs = lax.axis_size("seq")
    heads = lax.axis_size("head")
    chips = slabs // 2
    rows = 2 * tok_rows
    width = 2 * tok_cols
    height = rows * slabs
    half_rows = height // 2
    chip_channels = out_channels // chips
    pad_channels = -(-chip_channels // 8) * 8
    real_rows = 9 * pad_channels
    padded = -(-real_rows // 16) * 16
    lanes = (half_rows + 2) * width
    live = min(3, frames)
    me_index = lax.axis_index("seq")
    me = me_index.astype(jnp.int32).reshape(1)
    top = slabs // 2
    rest = [m for m in range(2, top, 2)]

    flat = cotangent.reshape(chips, chip_channels, frames * rows * width)
    chip = me_index // 2

    def wanted(side):
        return jnp.stack(
            [
                lax.dynamic_index_in_dim(flat, chip ^ ((m ^ side) // 2), 0, keepdims=False)
                for m in [0] + rest
            ]
        )

    near, far = wanted(0), wanted(top)
    got = xor_permute(far, "seq", top)
    cot_blocks = []
    cot_masks = []
    for position, mask in enumerate([0] + rest):
        pair = jnp.stack([near[position], got[position]])
        cot_blocks.append(pair if mask == 0 else xor_permute(pair, "seq", mask))
        cot_masks.append([mask, mask ^ top])
    cot_blocks = cot_blocks + [xor_permute(b, "seq", 1) for b in cot_blocks]
    cot_masks = cot_masks + [[m ^ 1 for m in masks] for masks in cot_masks]
    attn_out = lax.optimization_barrier((attn_out, far))[0]
    flattened = attn_out.reshape(frames * tok_rows * tok_cols, model_width)
    partial_sum = lax.dot_general(
        w_proj, flattened, (((0,), (1,)), ((), ())), preferred_element_type=F32
    )
    step = heads // 2
    other = jnp.zeros_like(partial_sum)
    while step >= 1:
        other = xor_permute(partial_sum, "head", step)
        if step > 1:
            partial_sum = partial_sum + other
        step //= 2
    latent = pl.pallas_call(
        functools.partial(unpatchify_kernel, frames, tok_rows, tok_cols),
        out_shape=jax.ShapeDtypeStruct((latent_width, frames * rows * width), BF16),
        in_specs=[vmem(), vmem()],
        out_specs=vmem(),
        compiler_params=params(),
        name="unpatchify",
    )(partial_sum, other)

    pair = jnp.stack([latent, xor_permute(latent, "seq", top)])
    lats = [pair] + [xor_permute(pair, "seq", m) for m in rest]
    lat_masks = [[m, m ^ top] for m in [0] + rest]
    lats = lats + [xor_permute(b, "seq", 1) for b in lats]
    lat_masks = lat_masks + [[m ^ 1 for m in masks] for masks in lat_masks]

    entry = entry_weight.reshape(channels, 3, 9 * latent_width)
    entries = [entry[:, max(0, 2 - f) :].reshape(channels, -1) for f in range(frames)]
    gain = norm_gain.reshape(channels, 1)
    hbm = pl.BlockSpec(memory_space=pl.ANY)
    keep, send = pl.pallas_call(
        functools.partial(
            gradient_kernel, frames, rows, slabs, lat_masks, cot_masks, real_rows, pad_channels
        ),
        out_shape=(
            jax.ShapeDtypeStruct((real_rows, channels), F32),
            jax.ShapeDtypeStruct((real_rows, channels), BF16),
        ),
        in_specs=[smem(), vmem()] + [vmem()] * frames + [hbm] * (len(lats) + len(cot_blocks)),
        out_specs=(vmem(), vmem()),
        scratch_shapes=[
            pltpu.VMEM((slabs, latent_width, frames * rows * width), BF16),
            pltpu.VMEM((slabs, chip_channels, frames * rows * width), BF16),
            pltpu.VMEM((frames, 3 * latent_width, (half_rows + 4) * width), BF16),
            pltpu.VMEM((frames, 3 * pad_channels, (half_rows + 4) * width), F32),
            pltpu.VMEM((frames * padded, lanes), BF16),
            pltpu.VMEM((channels, lanes), F32),
            pltpu.VMEM((channels, lanes), F32),
            pltpu.VMEM((channels, lanes), BF16),
            pltpu.VMEM((channels, lanes), BF16),
            pltpu.VMEM((live * padded, channels), F32),
            pltpu.VMEM((channels, LANES), F32),
            pltpu.SemaphoreType.DMA((slabs,)),
            pltpu.SemaphoreType.DMA((slabs,)),
        ],
        compiler_params=params(),
        name="gradient",
    )(me, gain, *entries, *lats, *cot_blocks)
    block = (keep + xor_permute(send, "seq", 1).astype(F32)).astype(BF16)

    columns = [m for m in range(0, slabs, 4)]
    direct = [block] + [xor_permute(block, "seq", m) for m in columns[1:]]
    beside = xor_permute(block, "seq", 2)
    held = lax.optimization_barrier((block, *lats))[1:]
    conv = conv_weight.transpose(1, 2, 3, 0, 4).reshape(27, out_channels, channels)
    decoded = pl.pallas_call(
        functools.partial(decode_kernel, frames, rows, slabs, lat_masks),
        out_shape=jax.ShapeDtypeStruct((out_channels, frames * rows * width), BF16),
        in_specs=[smem(), vmem(), hbm] + [vmem()] * frames + [hbm] * len(lats),
        out_specs=vmem(),
        scratch_shapes=[
            pltpu.VMEM((slabs, latent_width, frames * rows * width), BF16),
            pltpu.VMEM((frames, 3 * latent_width, (rows + 4) * width), BF16),
            pltpu.VMEM((channels, (rows + 2) * width), F32),
            pltpu.VMEM((channels, (rows + 2) * width), BF16),
            pltpu.VMEM((frames, 3, channels, (rows + 2) * width), BF16),
            pltpu.VMEM((channels, LANES), F32),
            pltpu.VMEM((live * 9, out_channels, channels), BF16),
            pltpu.SemaphoreType.DMA((slabs,)),
            pltpu.SemaphoreType.DMA(()),
        ],
        compiler_params=params(),
        name="decode",
    )(me, gain, conv, *entries, *held)
    decoded = decoded.reshape(out_channels, frames, rows, width)

    blank = 3 - live
    shape = (9, pad_channels, channels)
    grad_shape = (3, 9, chips * pad_channels, channels)

    def finish(parts, masks, grad=None):
        first = grad is None
        return pl.pallas_call(
            functools.partial(finish_kernel, first, masks, blank),
            out_shape=jax.ShapeDtypeStruct(grad_shape, F32),
            in_specs=[smem()]
            + [vmem()] * len(parts)
            + ([] if first else [pl.BlockSpec(memory_space=pl.ANY)]),
            out_specs=pl.BlockSpec(memory_space=pl.ANY),
            scratch_shapes=[
                pltpu.VMEM((len(parts),) + shape, F32),
                pltpu.VMEM((chips * pad_channels, channels), F32),
                pltpu.SemaphoreType.DMA((len(parts),)),
                pltpu.SemaphoreType.DMA((max(1, 9 * blank),)),
            ],
            input_output_aliases={} if first else {len(parts) + 1: 0},
            compiler_params=params(),
            name="finish",
        )(me, *[p.reshape(shape) for p in parts], *([] if first else [grad]))

    early = [block, beside]
    early_masks = [0, 2]
    early = early + [xor_permute(p, "seq", 1) for p in early]
    early_masks = early_masks + [m ^ 1 for m in early_masks]
    grad = finish(early, early_masks)
    after = lax.optimization_barrier((decoded, *direct[1:]))
    decoded = after[0]
    groups = [([], []), ([], [])]
    for mask, piece in zip(columns[1:], after[1:]):
        across = xor_permute(piece, "seq", 2)
        parts, masks = groups[0 if mask == 4 else 1]
        for part, m in ((piece, mask), (across, mask ^ 2)):
            parts += [part, xor_permute(part, "seq", 1)]
            masks += [m, m ^ 1]
    for parts, masks in groups:
        if parts:
            grad = finish(parts, masks, grad)
    if pad_channels != chip_channels:
        grad = grad.reshape(27, chips, pad_channels, channels)[:, :, :chip_channels]
    grad = grad.reshape(3, 3, 3, out_channels, channels).transpose(3, 0, 1, 2, 4)
    return decoded, grad


def solution(mesh):
    return jax.shard_map(
        per_device,
        mesh=mesh,
        in_specs=(
            P(None, "seq", None, "head"),
            P("head", None),
            P(),
            P(),
            P("head", None, None, None, None),
            P("head", None, "seq", None),
        ),
        out_specs=(P("head", None, "seq", None), P("head", None, None, None, None)),
        check_vma=False,
    )
```

```python
import functools

import jax
import jax.numpy as jnp
from jax import lax
from jax.experimental import pallas as pl
from jax.experimental.pallas import tpu as pltpu
from jax.sharding import PartitionSpec as P

LANES = 128
VMEM_LIMIT = 56 * 1024 * 1024
F32 = jnp.float32
BF16 = jnp.bfloat16


def params():
    return pltpu.CompilerParams(vmem_limit_bytes=VMEM_LIMIT)


def cost(flops, size):
    return pl.CostEstimate(flops=flops, transcendentals=0, bytes_accessed=size)


def vmem():
    return pl.BlockSpec(memory_space=pltpu.VMEM)


def smem():
    return pl.BlockSpec(memory_space=pltpu.SMEM)


def xor_permute(x, axis, mask):
    return lax.ppermute(x, axis, [(i, i ^ mask) for i in range(lax.axis_size(axis))])


def dot(a, b):
    return lax.dot_general(a, b, (((1,), (0,)), ((), ())), preferred_element_type=F32)


def dot_t(a, b):
    return lax.dot_general(a, b, (((1,), (1,)), ((), ())), preferred_element_type=F32)


def unpatchify_kernel(frames, tok_rows, tok_cols, own_ref, other_ref, out_ref):
    latent_width = out_ref.shape[0]
    features = (own_ref[...] + other_ref[...]).astype(BF16)
    width = 2 * tok_cols
    span = tok_rows * tok_cols
    source = lax.broadcasted_iota(jnp.int32, (span, tok_rows * width), 0)
    target = lax.broadcasted_iota(jnp.int32, (span, tok_rows * width), 1)
    same_row = source // tok_cols == target // width
    column = source % tok_cols
    even = (same_row & (target % width == 2 * column)).astype(BF16)
    odd = (same_row & (target % width == 2 * column + 1)).astype(BF16)
    for frame in range(frames):
        tokens = features[:, frame * span : (frame + 1) * span]
        left = dot(tokens, even)
        right = dot(tokens, odd)
        for row in range(tok_rows):
            cols = slice(row * width, (row + 1) * width)
            for half in range(2):
                base = half * 2 * latent_width
                cells = (
                    left[base : base + latent_width, cols]
                    + right[base + latent_width : base + 2 * latent_width, cols]
                )
                at = (frame * 2 * tok_rows + 2 * row + half) * width
                out_ref[:, at : at + width] = cells.astype(BF16)


def shifted(tile, shift):
    if shift == 1:
        return tile
    lane = lax.broadcasted_iota(jnp.int32, tile.shape, 1)
    if shift == 0:
        return jnp.where(lane == 0, 0.0, pltpu.roll(tile, 1, 1))
    return jnp.where(lane == LANES - 1, 0.0, pltpu.roll(tile, LANES - 1, 1))


def fetch(piece_refs, mask_lists, slot_ref, sems):
    copies = []
    for index, (piece_ref, masks) in enumerate(zip(piece_refs, mask_lists)):
        for position, mask in enumerate(masks):
            copies.append(
                pltpu.make_async_copy(
                    piece_ref.at[position], slot_ref.at[mask], sems.at[index * len(masks) + position]
                )
            )
    for copy in copies:
        copy.start()
    return copies


def place_latent(slot_ref, stack_ref, me, first_slab, slab_count, frames, rows, slabs):
    latent_width = stack_ref.shape[1] // 3
    for offset in range(-1, slab_count + 1):
        slab = first_slab + offset
        inside = ((slab >= 0) & (slab < slabs)).astype(F32)
        source = jnp.clip(slab, 0, slabs - 1) ^ me
        needed = range(rows)
        if offset == -1:
            needed = range(rows - 2, rows)
        if offset == slab_count:
            needed = range(2)
        for frame in range(frames):
            for row in needed:
                at = (frame * rows + row) * LANES
                tile = slot_ref[source, :latent_width, at : at + LANES].astype(F32)
                if offset in (-1, slab_count):
                    tile = tile * inside
                to = (offset * rows + row + 2) * LANES
                for shift in range(3):
                    stack_ref[
                        frame, shift * latent_width : (shift + 1) * latent_width, to : to + LANES
                    ] = shifted(tile, shift).astype(BF16)


def hidden_rows(stack_ref, weight_ref, frame, first, count):
    pieces = []
    for source in range(max(0, frame - 2), frame + 1):
        for row_tap in range(3):
            at = pl.multiple_of((first + row_tap) * LANES, LANES)
            pieces.append(stack_ref[source, :, pl.ds(at, count * LANES)])
    return dot(weight_ref[...], jnp.concatenate(pieces, axis=0))


def activate_rows(hidden_ref, gain_ref, act_ref, base, top_row, count, height):
    channels = hidden_ref.shape[0]
    block = 16
    for index in range(count):
        at = pl.multiple_of((base + index) * LANES, LANES)
        hidden = hidden_ref[:, pl.ds(at, LANES)]
        mean = jnp.sum(hidden * hidden, axis=0, keepdims=True) * (1.0 / channels)
        row = top_row + base + index
        inside = ((row >= 0) & (row < height)).astype(F32)
        inverse = jnp.broadcast_to(lax.rsqrt(mean + 1e-6) * inside, (block, LANES))
        for at_channel in range(0, channels, block):
            chunk = slice(at_channel, at_channel + block)
            half = hidden_ref[chunk, pl.ds(at, LANES)] * inverse * gain_ref[chunk, :]
            act_ref[chunk, pl.ds(at, LANES)] = (half + half * jnp.tanh(half)).astype(BF16)


def place_cotangent(
    slot_ref, flat_ref, out_ref, me, first_slab, slab_count, frames, rows, pad_channels, skip
):
    channels = slot_ref.shape[1] - skip
    half_rows = slab_count * rows
    group = 3 * pad_channels
    padded = out_ref.shape[0] // frames
    for frame in range(frames):
        for edge in (0, half_rows + 2):
            flat_ref[frame, :, edge * LANES : (edge + 2) * LANES] = jnp.zeros((group, 2 * LANES), F32)
    for offset in range(slab_count):
        source = (first_slab + offset) ^ me
        for frame in range(frames):
            for row in range(rows):
                at = (frame * rows + row) * LANES
                tile = slot_ref[source, skip:, at : at + LANES].astype(F32)
                if pad_channels != channels:
                    tile = jnp.concatenate(
                        [tile, jnp.zeros((pad_channels - channels, LANES), F32)], axis=0
                    )
                to = (offset * rows + row + 2) * LANES
                for tap in range(3):
                    flat_ref[frame, tap * pad_channels : (tap + 1) * pad_channels, to : to + LANES] = (
                        shifted(tile, 2 - tap)
                    )
    filler = [jnp.zeros((padded - 3 * group, LANES), F32)] if padded != 3 * group else []
    for frame in range(frames):
        for row in range(half_rows + 2):
            taps = [flat_ref[frame, :, (row + 2 - tap) * LANES : (row + 3 - tap) * LANES] for tap in range(3)]
            out_ref[frame * padded : (frame + 1) * padded, row * LANES : (row + 1) * LANES] = (
                jnp.concatenate(taps + filler, axis=0).astype(BF16)
            )


def gradient_kernel(frames, rows, slabs, masks, real_rows, pad_channels, *refs):
    me_ref, gain_ref = refs[:2]
    refs = refs[2:]
    weight_refs, refs = refs[:frames], refs[frames:]
    piece_refs, refs = refs[: len(masks)], refs[len(masks) :]
    keep_ref, send_ref, slots, stack_ref, flat_ref, cot_ref = refs[:6]
    hid_a, hid_b, act_a, act_b, sum_ref, wide_gain, sems = refs[6:]
    copies = fetch(piece_refs, masks, slots, sems)
    me = me_ref[0]
    core = me & 1
    slab_count = slabs // 2
    half_rows = slab_count * rows
    height = slabs * rows
    first_slab = core * slab_count
    padded = cot_ref.shape[0] // frames
    top_row = core * half_rows - 1
    ext = half_rows + 2
    count = max(d for d in range(1, 18) if ext % d == 0)
    width = count * LANES
    hidden = (hid_a, hid_b)
    acts = (act_a, act_b)
    wide_gain[...] = jnp.broadcast_to(0.5 * gain_ref[...], wide_gain.shape)
    sum_ref[...] = jnp.zeros_like(sum_ref)
    for copy in copies:
        copy.wait()
    place_latent(slots, stack_ref, me, first_slab, slab_count, frames, rows, slabs)
    hid_a[...] = hidden_rows(stack_ref, weight_refs[0], 0, 0, ext)
    place_cotangent(
        slots, flat_ref, cot_ref, me, first_slab, slab_count, frames, rows, pad_channels,
        stack_ref.shape[1] // 3,
    )
    for frame in range(frames):

        def chunk(step, carry):
            at = pl.multiple_of(step * width, LANES)
            if frame + 1 < frames:
                hidden[(frame + 1) % 2][:, pl.ds(at, width)] = hidden_rows(
                    stack_ref, weight_refs[frame + 1], frame + 1, step * count, count
                )
            if frame > 0:
                last = min(frames, frame + 2)
                sum_ref[0 : (last - frame + 1) * padded, :] += dot_t(
                    cot_ref[(frame - 1) * padded : last * padded, pl.ds(at, width)],
                    acts[(frame - 1) % 2][:, pl.ds(at, width)],
                )
            activate_rows(
                hidden[frame % 2], wide_gain, acts[frame % 2], step * count, top_row, count, height
            )
            return carry

        lax.fori_loop(0, ext // count, chunk, 0)
    final = frames - 1
    sum_ref[0:padded, :] += dot_t(cot_ref[final * padded : frames * padded, :], acts[final % 2][...])
    keep_at = pl.multiple_of(core * padded, 16)
    send_at = pl.multiple_of((1 - core) * padded, 16)
    keep_ref[...] = sum_ref[pl.ds(keep_at, padded), :][:real_rows]
    send_ref[...] = sum_ref[pl.ds(send_at, padded), :][:real_rows].astype(BF16)


def decode_kernel(frame, frames, rows, slabs, masks, me_ref, gain_ref, conv_hbm, *refs):
    first_source = max(0, frame - 2)
    sources = range(first_source, frame + 1)
    weight_refs, refs = refs[: len(sources)], refs[len(sources) :]
    piece_refs, refs = refs[: len(masks)], refs[len(masks) :]
    out_ref, slots, stack_ref, hid_ref, flat_ref, act_ref, wide_gain, conv_ref, sems, sem = refs
    taps = conv_ref.shape[0]
    load = pltpu.make_async_copy(conv_hbm.at[pl.ds(27 - taps, taps)], conv_ref, sem)
    load.start()
    copies = fetch(piece_refs, masks, slots, sems)
    me = me_ref[0]
    height = slabs * rows
    wide_gain[...] = jnp.broadcast_to(0.5 * gain_ref[...], wide_gain.shape)
    for copy in copies:
        copy.wait()
    place_latent(slots, stack_ref, me, me, 1, frames, rows, slabs)
    ext = rows + 2
    kernels = []
    inputs = []
    for position, source in enumerate(sources):
        hid_ref[...] = hidden_rows(stack_ref, weight_refs[position], source, 0, ext)
        activate_rows(hid_ref, wide_gain, flat_ref, 0, me * rows - 1, ext, height)
        for row in range(ext):
            tile = flat_ref[:, row * LANES : (row + 1) * LANES].astype(F32)
            for tap in range(3):
                act_ref[position, tap, :, row * LANES : (row + 1) * LANES] = shifted(tile, tap).astype(BF16)
    load.wait()
    for position, source in enumerate(sources):
        plane = position * 9
        for row_tap in range(3):
            for col_tap in range(3):
                kernels.append(conv_ref[plane + row_tap * 3 + col_tap])
                inputs.append(act_ref[position, col_tap, :, row_tap * LANES : (row_tap + rows) * LANES])
    total = dot(jnp.concatenate(kernels, axis=1), jnp.concatenate(inputs, axis=0))
    out_ref[...] = total.astype(BF16)


def blank_kernel(blank, out_hbm, zero_ref, sems):
    zero_ref[...] = jnp.zeros_like(zero_ref)
    copies = [
        pltpu.make_async_copy(zero_ref, out_hbm.at[plane, tap], sems.at[plane * 9 + tap])
        for plane in range(blank)
        for tap in range(9)
    ]
    for copy in copies:
        copy.start()
    for copy in copies:
        copy.wait()


def finish_kernel(pieces, me_ref, *refs):
    count = len(pieces)
    piece_refs = refs[:count]
    out_hbm, wide_ref, sems = refs[count + 1 :]
    me = me_ref[0]
    channels = wide_ref.shape[2]
    copies = []
    for index, mask in enumerate(pieces):
        source = me ^ mask
        wide_ref[index] = piece_refs[index][...].astype(F32)
        at = pl.multiple_of((source >> 1) * channels, 8)
        copy = pltpu.make_async_copy(
            wide_ref.at[index], out_hbm.at[2 - (source & 1), :, pl.ds(at, channels), :], sems.at[index]
        )
        copy.start()
        copies.append(copy)
    for copy in copies:
        copy.wait()


def per_device(attn_out, w_proj, norm_gain, entry_weight, conv_weight, cotangent):
    frames, tok_rows, tok_cols, model_width = attn_out.shape
    latent_width = entry_weight.shape[4]
    channels = entry_weight.shape[0]
    out_channels = conv_weight.shape[0]
    slabs = lax.axis_size("seq")
    heads = lax.axis_size("head")
    chips = slabs // 2
    rows = 2 * tok_rows
    width = 2 * tok_cols
    height = rows * slabs
    half_rows = height // 2
    chip_channels = out_channels // chips
    pad_channels = -(-chip_channels // 8) * 8
    real_rows = 9 * pad_channels
    padded = -(-real_rows // 16) * 16
    lanes = (half_rows + 2) * width
    live = min(3, frames)
    me_index = lax.axis_index("seq")
    me = me_index.astype(jnp.int32).reshape(1)
    top = slabs // 2
    rest = [m for m in range(2, top, 2)]

    flat = cotangent.reshape(chips, chip_channels, frames * rows * width)
    chip = me_index // 2

    def wanted(side):
        return jnp.stack(
            [
                lax.dynamic_index_in_dim(flat, chip ^ ((m ^ side) // 2), 0, keepdims=False)
                for m in [0] + rest
            ]
        )

    near, far = wanted(0), wanted(top)
    got = xor_permute(far, "seq", top)

    attn_out = lax.optimization_barrier((attn_out, far))[0]
    flattened = attn_out.reshape(frames * tok_rows * tok_cols, model_width)
    partial_sum = lax.dot_general(
        w_proj, flattened, (((0,), (1,)), ((), ())), preferred_element_type=F32
    )
    step = heads // 2
    other = jnp.zeros_like(partial_sum)
    while step >= 1:
        other = xor_permute(partial_sum, "head", step)
        if step > 1:
            partial_sum = partial_sum + other
        step //= 2
    entry = entry_weight.reshape(channels, 3, 9 * latent_width)
    entries = [entry[:, max(0, 2 - f) :].reshape(channels, -1) for f in range(frames)]
    gain = norm_gain.reshape(channels, 1)
    other, gain, *entries = lax.optimization_barrier((other, gain, *entries))
    latent = pl.pallas_call(
        functools.partial(unpatchify_kernel, frames, tok_rows, tok_cols),
        out_shape=jax.ShapeDtypeStruct((latent_width, frames * rows * width), BF16),
        in_specs=[vmem(), vmem()],
        out_specs=vmem(),
        compiler_params=params(),
        name="unpatchify",
    )(partial_sum, other)

    blank = 3 - live
    hbm = pl.BlockSpec(memory_space=pl.ANY)
    grad_shape = (3, 9, chips * pad_channels, channels)
    grad = pl.pallas_call(
        functools.partial(blank_kernel, blank),
        out_shape=jax.ShapeDtypeStruct(grad_shape, F32),
        out_specs=hbm,
        scratch_shapes=[
            pltpu.VMEM((chips * pad_channels, channels), F32),
            pltpu.SemaphoreType.DMA((max(1, 9 * blank),)),
        ],
        compiler_params=params(),
        cost_estimate=cost(0, blank * 9 * out_channels * channels * 4),
        name="blank",
    )()

    across = xor_permute(latent, "seq", top)
    across, grad = lax.optimization_barrier((across, grad))
    latents = jnp.stack([latent, across])
    pieces = []
    masks = []
    for position, mask in enumerate([0] + rest):
        both = jnp.concatenate([latents, jnp.stack([near[position], got[position]])], axis=1)
        pieces.append(both if mask == 0 else xor_permute(both, "seq", mask))
        masks.append([mask, mask ^ top])
    pieces = pieces + [xor_permute(p, "seq", 1) for p in pieces]
    masks = masks + [[m ^ 1 for m in pair] for pair in masks]
    slot_shape = (slabs, latent_width + chip_channels, frames * rows * width)

    keep, send = pl.pallas_call(
        functools.partial(gradient_kernel, frames, rows, slabs, masks, real_rows, pad_channels),
        out_shape=(
            jax.ShapeDtypeStruct((real_rows, channels), F32),
            jax.ShapeDtypeStruct((real_rows, channels), BF16),
        ),
        in_specs=[smem(), vmem()] + [vmem()] * frames + [hbm] * len(pieces),
        out_specs=(vmem(), vmem()),
        scratch_shapes=[
            pltpu.VMEM(slot_shape, BF16),
            pltpu.VMEM((frames, 3 * latent_width, (half_rows + 4) * width), BF16),
            pltpu.VMEM((frames, 3 * pad_channels, (half_rows + 4) * width), F32),
            pltpu.VMEM((frames * padded, lanes), BF16),
            pltpu.VMEM((channels, lanes), F32),
            pltpu.VMEM((channels, lanes), F32),
            pltpu.VMEM((channels, lanes), BF16),
            pltpu.VMEM((channels, lanes), BF16),
            pltpu.VMEM((live * padded, channels), F32),
            pltpu.VMEM((channels, LANES), F32),
            pltpu.SemaphoreType.DMA((slabs,)),
        ],
        compiler_params=params(),
        name="gradient",
    )(me, gain, *entries, *pieces)
    block = (keep + xor_permute(send, "seq", 1).astype(F32)).astype(BF16)

    columns = [m for m in range(4, slabs, 4)]
    direct = [xor_permute(block, "seq", m) for m in columns]
    beside = xor_permute(block, "seq", 2)
    conv = conv_weight.transpose(1, 2, 3, 0, 4).reshape(27, out_channels, channels)

    def decode(frame, pieces):
        first = max(0, frame - 2)
        count = frame + 1 - first
        return pl.pallas_call(
            functools.partial(decode_kernel, frame, frames, rows, slabs, masks),
            out_shape=jax.ShapeDtypeStruct((out_channels, rows * width), BF16),
            in_specs=[smem(), vmem(), hbm] + [vmem()] * count + [hbm] * len(pieces),
            out_specs=vmem(),
            scratch_shapes=[
                pltpu.VMEM(slot_shape, BF16),
                pltpu.VMEM((frames, 3 * latent_width, (rows + 4) * width), BF16),
                pltpu.VMEM((channels, (rows + 2) * width), F32),
                pltpu.VMEM((channels, (rows + 2) * width), BF16),
                pltpu.VMEM((count, 3, channels, (rows + 2) * width), BF16),
                pltpu.VMEM((channels, LANES), F32),
                pltpu.VMEM((count * 9, out_channels, channels), BF16),
                pltpu.SemaphoreType.DMA((slabs,)),
                pltpu.SemaphoreType.DMA(()),
            ],
            compiler_params=params(),
            cost_estimate=cost(
                count * 18 * out_channels * channels * rows * width,
                count * 18 * out_channels * channels,
            ),
            name="decode",
        )(me, gain, conv, *entries[first : frame + 1], *pieces)

    gate = block
    decoded = []
    across = []
    for frame in range(frames):
        held = lax.optimization_barrier((gate, *pieces))
        result = decode(frame, held[1:])
        decoded.append(result)
        gate = result
        ready = columns[frame:] if frame == frames - 1 else columns[frame : frame + 1]
        for mask in ready:
            position = columns.index(mask)
            gated = lax.optimization_barrier((direct[position], result))[0]
            across.append(xor_permute(gated, "seq", 2))
    decoded = jnp.stack([d.reshape(out_channels, rows, width) for d in decoded], axis=1)

    shape = (9, pad_channels, channels)

    def finish(parts, sources, grad):
        return pl.pallas_call(
            functools.partial(finish_kernel, sources),
            out_shape=jax.ShapeDtypeStruct(grad_shape, F32),
            in_specs=[smem()] + [vmem()] * len(parts) + [hbm],
            out_specs=hbm,
            scratch_shapes=[
                pltpu.VMEM((len(parts),) + shape, F32),
                pltpu.SemaphoreType.DMA((len(parts),)),
            ],
            input_output_aliases={len(parts) + 1: 0},
            compiler_params=params(),
            cost_estimate=cost(0, len(parts) * real_rows * channels * 6),
            name="finish",
        )(me, *[p.reshape(shape) for p in parts], grad)

    groups = [[(block, 0), (beside, 2)], []]
    for position, mask in enumerate(columns):
        groups[0 if position == 0 else 1] += [(direct[position], mask), (across[position], mask ^ 2)]
    for group in groups:
        parts = [p for p, _ in group] + [xor_permute(p, "seq", 1) for p, _ in group]
        sources = [m for _, m in group] + [m ^ 1 for _, m in group]
        if parts:
            grad = finish(parts, sources, grad)
    if pad_channels != chip_channels:
        grad = grad.reshape(27, chips, pad_channels, channels)[:, :, :chip_channels]
    grad = grad.reshape(3, 3, 3, out_channels, channels).transpose(3, 0, 1, 2, 4)
    return decoded, grad


def solution(mesh):
    return jax.shard_map(
        per_device,
        mesh=mesh,
        in_specs=(
            P(None, "seq", None, "head"),
            P("head", None),
            P(),
            P(),
            P("head", None, None, None, None),
            P("head", None, "seq", None),
        ),
        out_specs=(P("head", None, "seq", None), P("head", None, None, None, None)),
        check_vma=False,
    )
```

```python
import functools

import jax
import jax.numpy as jnp
from jax import lax
from jax.experimental import pallas as pl
from jax.experimental.pallas import tpu as pltpu
from jax.sharding import PartitionSpec as P

LANES = 128
VMEM_LIMIT = 56 * 1024 * 1024
F32 = jnp.float32
BF16 = jnp.bfloat16


def params():
    return pltpu.CompilerParams(vmem_limit_bytes=VMEM_LIMIT)


def cost(flops, size):
    return pl.CostEstimate(flops=flops, transcendentals=0, bytes_accessed=size)


def vmem():
    return pl.BlockSpec(memory_space=pltpu.VMEM)


def smem():
    return pl.BlockSpec(memory_space=pltpu.SMEM)


def xor_permute(x, axis, mask):
    return lax.ppermute(x, axis, [(i, i ^ mask) for i in range(lax.axis_size(axis))])


def dot(a, b):
    return lax.dot_general(a, b, (((1,), (0,)), ((), ())), preferred_element_type=F32)


def dot_t(a, b):
    return lax.dot_general(a, b, (((1,), (1,)), ((), ())), preferred_element_type=F32)


def unpatchify_kernel(frames, tok_rows, tok_cols, own_ref, other_ref, out_ref):
    latent_width = out_ref.shape[0]
    features = (own_ref[...] + other_ref[...]).astype(BF16)
    width = 2 * tok_cols
    span = tok_rows * tok_cols
    source = lax.broadcasted_iota(jnp.int32, (span, tok_rows * width), 0)
    target = lax.broadcasted_iota(jnp.int32, (span, tok_rows * width), 1)
    same_row = source // tok_cols == target // width
    column = source % tok_cols
    even = (same_row & (target % width == 2 * column)).astype(BF16)
    odd = (same_row & (target % width == 2 * column + 1)).astype(BF16)
    for frame in range(frames):
        tokens = features[:, frame * span : (frame + 1) * span]
        left = dot(tokens, even)
        right = dot(tokens, odd)
        for row in range(tok_rows):
            cols = slice(row * width, (row + 1) * width)
            for half in range(2):
                base = half * 2 * latent_width
                cells = (
                    left[base : base + latent_width, cols]
                    + right[base + latent_width : base + 2 * latent_width, cols]
                )
                at = (frame * 2 * tok_rows + 2 * row + half) * width
                out_ref[:, at : at + width] = cells.astype(BF16)


def shifted(tile, shift):
    if shift == 1:
        return tile
    lane = lax.broadcasted_iota(jnp.int32, tile.shape, 1)
    if shift == 0:
        return jnp.where(lane == 0, 0.0, pltpu.roll(tile, 1, 1))
    return jnp.where(lane == LANES - 1, 0.0, pltpu.roll(tile, LANES - 1, 1))


def fetch(piece_refs, mask_lists, slot_ref, sems):
    copies = []
    for index, (piece_ref, masks) in enumerate(zip(piece_refs, mask_lists)):
        for position, mask in enumerate(masks):
            copies.append(
                pltpu.make_async_copy(
                    piece_ref.at[position], slot_ref.at[mask], sems.at[index * len(masks) + position]
                )
            )
    for copy in copies:
        copy.start()
    return copies


def place_latent(slot_ref, stack_ref, me, first_slab, slab_count, frames, rows, slabs):
    latent_width = stack_ref.shape[1] // 3
    for offset in range(-1, slab_count + 1):
        slab = first_slab + offset
        inside = ((slab >= 0) & (slab < slabs)).astype(F32)
        source = jnp.clip(slab, 0, slabs - 1) ^ me
        needed = range(rows)
        if offset == -1:
            needed = range(rows - 2, rows)
        if offset == slab_count:
            needed = range(2)
        for frame in range(frames):
            for row in needed:
                at = (frame * rows + row) * LANES
                tile = slot_ref[source, :latent_width, at : at + LANES].astype(F32)
                if offset in (-1, slab_count):
                    tile = tile * inside
                to = (offset * rows + row + 2) * LANES
                for shift in range(3):
                    stack_ref[
                        frame, shift * latent_width : (shift + 1) * latent_width, to : to + LANES
                    ] = shifted(tile, shift).astype(BF16)


def hidden_rows(stack_ref, weight_ref, frame, first, count):
    pieces = []
    for source in range(max(0, frame - 2), frame + 1):
        for row_tap in range(3):
            at = pl.multiple_of((first + row_tap) * LANES, LANES)
            pieces.append(stack_ref[source, :, pl.ds(at, count * LANES)])
    return dot(weight_ref[...], jnp.concatenate(pieces, axis=0))


def load_entry(entry_ref, gain_ref, weight_refs, wide_gain):
    for weight_ref in weight_refs:
        depth = weight_ref.shape[1]
        start = entry_ref.shape[0] - depth
        weight_ref[...] = jnp.transpose(entry_ref[start:, :].astype(F32)).astype(BF16)
    wide_gain[...] = jnp.transpose(jnp.broadcast_to(0.5 * gain_ref[...], wide_gain.shape[::-1]))


def activate_rows(hidden_ref, gain_ref, act_ref, base, top_row, count, height):
    channels = hidden_ref.shape[0]
    block = 16
    for index in range(count):
        at = pl.multiple_of((base + index) * LANES, LANES)
        hidden = hidden_ref[:, pl.ds(at, LANES)]
        mean = jnp.sum(hidden * hidden, axis=0, keepdims=True) * (1.0 / channels)
        row = top_row + base + index
        inside = ((row >= 0) & (row < height)).astype(F32)
        inverse = jnp.broadcast_to(lax.rsqrt(mean + 1e-6) * inside, (block, LANES))
        for at_channel in range(0, channels, block):
            chunk = slice(at_channel, at_channel + block)
            half = hidden_ref[chunk, pl.ds(at, LANES)] * inverse * gain_ref[chunk, :]
            act_ref[chunk, pl.ds(at, LANES)] = (half + half * jnp.tanh(half)).astype(BF16)


def place_cotangent(
    slot_ref, flat_ref, out_ref, me, first_slab, slab_count, frames, rows, pad_channels, skip
):
    channels = slot_ref.shape[1] - skip
    half_rows = slab_count * rows
    group = 3 * pad_channels
    padded = out_ref.shape[0] // frames
    for frame in range(frames):
        for edge in (0, half_rows + 2):
            flat_ref[frame, :, edge * LANES : (edge + 2) * LANES] = jnp.zeros((group, 2 * LANES), F32)
    for offset in range(slab_count):
        source = (first_slab + offset) ^ me
        for frame in range(frames):
            for row in range(rows):
                at = (frame * rows + row) * LANES
                tile = slot_ref[source, skip:, at : at + LANES].astype(F32)
                if pad_channels != channels:
                    tile = jnp.concatenate(
                        [tile, jnp.zeros((pad_channels - channels, LANES), F32)], axis=0
                    )
                to = (offset * rows + row + 2) * LANES
                for tap in range(3):
                    flat_ref[frame, tap * pad_channels : (tap + 1) * pad_channels, to : to + LANES] = (
                        shifted(tile, 2 - tap)
                    )
    filler = [jnp.zeros((padded - 3 * group, LANES), F32)] if padded != 3 * group else []
    for frame in range(frames):
        for row in range(half_rows + 2):
            taps = [flat_ref[frame, :, (row + 2 - tap) * LANES : (row + 3 - tap) * LANES] for tap in range(3)]
            out_ref[frame * padded : (frame + 1) * padded, row * LANES : (row + 1) * LANES] = (
                jnp.concatenate(taps + filler, axis=0).astype(BF16)
            )


def gradient_kernel(frames, rows, slabs, masks, real_rows, pad_channels, *refs):
    me_ref, gain_ref, entry_ref = refs[:3]
    refs = refs[3:]
    piece_refs, refs = refs[: len(masks)], refs[len(masks) :]
    keep_ref, send_ref, slots, stack_ref, flat_ref, cot_ref = refs[:6]
    hid_a, hid_b, act_a, act_b, sum_ref, wide_gain, sems = refs[6:13]
    weight_refs = refs[13:]
    copies = fetch(piece_refs, masks, slots, sems)
    me = me_ref[0]
    core = me & 1
    slab_count = slabs // 2
    half_rows = slab_count * rows
    height = slabs * rows
    first_slab = core * slab_count
    padded = cot_ref.shape[0] // frames
    top_row = core * half_rows - 1
    ext = half_rows + 2
    count = max(d for d in range(1, 18) if ext % d == 0)
    width = count * LANES
    hidden = (hid_a, hid_b)
    acts = (act_a, act_b)
    load_entry(entry_ref, gain_ref, weight_refs, wide_gain)
    sum_ref[...] = jnp.zeros_like(sum_ref)
    for copy in copies:
        copy.wait()
    place_latent(slots, stack_ref, me, first_slab, slab_count, frames, rows, slabs)
    hid_a[...] = hidden_rows(stack_ref, weight_refs[0], 0, 0, ext)
    place_cotangent(
        slots, flat_ref, cot_ref, me, first_slab, slab_count, frames, rows, pad_channels,
        stack_ref.shape[1] // 3,
    )
    for frame in range(frames):

        def chunk(step, carry):
            at = pl.multiple_of(step * width, LANES)
            if frame + 1 < frames:
                hidden[(frame + 1) % 2][:, pl.ds(at, width)] = hidden_rows(
                    stack_ref, weight_refs[frame + 1], frame + 1, step * count, count
                )
            if frame > 0:
                last = min(frames, frame + 2)
                sum_ref[0 : (last - frame + 1) * padded, :] += dot_t(
                    cot_ref[(frame - 1) * padded : last * padded, pl.ds(at, width)],
                    acts[(frame - 1) % 2][:, pl.ds(at, width)],
                )
            activate_rows(
                hidden[frame % 2], wide_gain, acts[frame % 2], step * count, top_row, count, height
            )
            return carry

        lax.fori_loop(0, ext // count, chunk, 0)
    final = frames - 1
    sum_ref[0:padded, :] += dot_t(cot_ref[final * padded : frames * padded, :], acts[final % 2][...])
    keep_at = pl.multiple_of(core * padded, 16)
    send_at = pl.multiple_of((1 - core) * padded, 16)
    keep_ref[...] = sum_ref[pl.ds(keep_at, padded), :][:real_rows]
    send_ref[...] = sum_ref[pl.ds(send_at, padded), :][:real_rows].astype(BF16)


def decode_kernel(frames, rows, slabs, masks, me_ref, gain_ref, entry_ref, conv_hbm, *refs):
    piece_refs, refs = refs[: len(masks)], refs[len(masks) :]
    out_ref, slots, stack_ref, hid_ref, flat_ref, act_ref, wide_gain, conv_ref, sems, sem = refs[:10]
    weight_refs = refs[10:]
    live = conv_ref.shape[0] // 9
    load = pltpu.make_async_copy(conv_hbm.at[pl.ds((3 - live) * 9, live * 9)], conv_ref, sem)
    load.start()
    copies = fetch(piece_refs, masks, slots, sems)
    me = me_ref[0]
    height = slabs * rows
    load_entry(entry_ref, gain_ref, weight_refs, wide_gain)
    for copy in copies:
        copy.wait()
    place_latent(slots, stack_ref, me, me, 1, frames, rows, slabs)
    ext = rows + 2
    for frame in range(frames):
        hid_ref[...] = hidden_rows(stack_ref, weight_refs[frame], frame, 0, ext)
        activate_rows(hid_ref, wide_gain, flat_ref, 0, me * rows - 1, ext, height)
        for row in range(ext):
            tile = flat_ref[:, row * LANES : (row + 1) * LANES].astype(F32)
            for tap in range(3):
                act_ref[frame, tap, :, row * LANES : (row + 1) * LANES] = shifted(tile, tap).astype(BF16)
    load.wait()
    for frame in range(frames):
        kernels = []
        inputs = []
        for depth in range(max(0, 2 - frame), 3):
            for row_tap in range(3):
                for col_tap in range(3):
                    kernels.append(conv_ref[(depth - (3 - live)) * 9 + row_tap * 3 + col_tap])
                    inputs.append(
                        act_ref[frame + depth - 2, col_tap, :, row_tap * LANES : (row_tap + rows) * LANES]
                    )
        total = dot(jnp.concatenate(kernels, axis=1), jnp.concatenate(inputs, axis=0))
        for row in range(rows):
            out_ref[:, frame, row, :] = total[:, row * LANES : (row + 1) * LANES].astype(BF16)


def blank_kernel(blank, out_hbm, zero_ref, sems):
    zero_ref[...] = jnp.zeros_like(zero_ref)
    copies = [
        pltpu.make_async_copy(zero_ref, out_hbm.at[plane, tap], sems.at[plane * 9 + tap])
        for plane in range(blank)
        for tap in range(9)
    ]
    for copy in copies:
        copy.start()
    for copy in copies:
        copy.wait()


def finish_kernel(pieces, me_ref, *refs):
    count = len(pieces)
    piece_refs = refs[:count]
    out_hbm, wide_ref, sems = refs[count + 1 :]
    me = me_ref[0]
    channels = wide_ref.shape[2]
    copies = []
    for index, mask in enumerate(pieces):
        source = me ^ mask
        wide_ref[index] = piece_refs[index][...].astype(F32)
        at = pl.multiple_of((source >> 1) * channels, 8)
        copy = pltpu.make_async_copy(
            wide_ref.at[index], out_hbm.at[2 - (source & 1), :, pl.ds(at, channels), :], sems.at[index]
        )
        copy.start()
        copies.append(copy)
    for copy in copies:
        copy.wait()


def per_device(attn_out, w_proj, norm_gain, entry_weight, conv_weight, cotangent):
    frames, tok_rows, tok_cols, model_width = attn_out.shape
    latent_width = entry_weight.shape[4]
    channels = entry_weight.shape[0]
    out_channels = conv_weight.shape[0]
    slabs = lax.axis_size("seq")
    heads = lax.axis_size("head")
    chips = slabs // 2
    rows = 2 * tok_rows
    width = 2 * tok_cols
    height = rows * slabs
    half_rows = height // 2
    chip_channels = out_channels // chips
    pad_channels = -(-chip_channels // 8) * 8
    real_rows = 9 * pad_channels
    padded = -(-real_rows // 16) * 16
    lanes = (half_rows + 2) * width
    live = min(3, frames)
    me_index = lax.axis_index("seq")
    me = me_index.astype(jnp.int32).reshape(1)
    top = slabs // 2
    rest = [m for m in range(2, top, 2)]

    flat = cotangent.reshape(chips, chip_channels, frames * rows * width)
    chip = me_index // 2

    def wanted(side):
        return jnp.stack(
            [
                lax.dynamic_index_in_dim(flat, chip ^ ((m ^ side) // 2), 0, keepdims=False)
                for m in [0] + rest
            ]
        )

    near, far = wanted(0), wanted(top)
    got = xor_permute(far, "seq", top)

    attn_out = lax.optimization_barrier((attn_out, far))[0]
    flattened = attn_out.reshape(frames * tok_rows * tok_cols, model_width)
    partial_sum = lax.dot_general(
        w_proj, flattened, (((0,), (1,)), ((), ())), preferred_element_type=F32
    )
    step = heads // 2
    other = jnp.zeros_like(partial_sum)
    while step >= 1:
        other = xor_permute(partial_sum, "head", step)
        if step > 1:
            partial_sum = partial_sum + other
        step //= 2
    entry = entry_weight.transpose(1, 2, 3, 4, 0).reshape(27 * latent_width, channels)
    gain = norm_gain.reshape(1, channels)
    weights = [
        pltpu.VMEM((channels, min(3, f + 1) * 9 * latent_width), BF16) for f in range(frames)
    ]
    latent = pl.pallas_call(
        functools.partial(unpatchify_kernel, frames, tok_rows, tok_cols),
        out_shape=jax.ShapeDtypeStruct((latent_width, frames * rows * width), BF16),
        in_specs=[vmem(), vmem()],
        out_specs=vmem(),
        compiler_params=params(),
        name="unpatchify",
    )(partial_sum, other)

    blank = 3 - live
    hbm = pl.BlockSpec(memory_space=pl.ANY)
    grad_shape = (3, 9, chips * pad_channels, channels)
    grad = pl.pallas_call(
        functools.partial(blank_kernel, blank),
        out_shape=jax.ShapeDtypeStruct(grad_shape, F32),
        out_specs=hbm,
        scratch_shapes=[
            pltpu.VMEM((chips * pad_channels, channels), F32),
            pltpu.SemaphoreType.DMA((max(1, 9 * blank),)),
        ],
        compiler_params=params(),
        cost_estimate=cost(0, blank * 9 * out_channels * channels * 4),
        name="blank",
    )()

    across = xor_permute(latent, "seq", top)
    across, grad = lax.optimization_barrier((across, grad))
    latents = jnp.stack([latent, across])
    pieces = []
    masks = []
    for position, mask in enumerate([0] + rest):
        both = jnp.concatenate([latents, jnp.stack([near[position], got[position]])], axis=1)
        pieces.append(both if mask == 0 else xor_permute(both, "seq", mask))
        masks.append([mask, mask ^ top])
    pieces = pieces + [xor_permute(p, "seq", 1) for p in pieces]
    masks = masks + [[m ^ 1 for m in pair] for pair in masks]
    slot_shape = (slabs, latent_width + chip_channels, frames * rows * width)

    keep, send = pl.pallas_call(
        functools.partial(gradient_kernel, frames, rows, slabs, masks, real_rows, pad_channels),
        out_shape=(
            jax.ShapeDtypeStruct((real_rows, channels), F32),
            jax.ShapeDtypeStruct((real_rows, channels), BF16),
        ),
        in_specs=[smem(), vmem(), vmem()] + [hbm] * len(pieces),
        out_specs=(vmem(), vmem()),
        scratch_shapes=[
            pltpu.VMEM(slot_shape, BF16),
            pltpu.VMEM((frames, 3 * latent_width, (half_rows + 4) * width), BF16),
            pltpu.VMEM((frames, 3 * pad_channels, (half_rows + 4) * width), F32),
            pltpu.VMEM((frames * padded, lanes), BF16),
            pltpu.VMEM((channels, lanes), F32),
            pltpu.VMEM((channels, lanes), F32),
            pltpu.VMEM((channels, lanes), BF16),
            pltpu.VMEM((channels, lanes), BF16),
            pltpu.VMEM((live * padded, channels), F32),
            pltpu.VMEM((channels, LANES), F32),
            pltpu.SemaphoreType.DMA((slabs,)),
        ]
        + weights,
        compiler_params=params(),
        name="gradient",
    )(me, gain, entry, *pieces)
    block = (keep + xor_permute(send, "seq", 1).astype(F32)).astype(BF16)

    columns = [m for m in range(4, slabs, 4)]
    direct = [xor_permute(block, "seq", m) for m in columns]
    beside = xor_permute(block, "seq", 2)
    conv = conv_weight.transpose(1, 2, 3, 0, 4).reshape(27, out_channels, channels)

    held = lax.optimization_barrier((block, *pieces))[1:]
    decoded = pl.pallas_call(
        functools.partial(decode_kernel, frames, rows, slabs, masks),
        out_shape=jax.ShapeDtypeStruct((out_channels, frames, rows, width), BF16),
        in_specs=[smem(), vmem(), vmem(), hbm] + [hbm] * len(pieces),
        out_specs=vmem(),
        scratch_shapes=[
            pltpu.VMEM(slot_shape, BF16),
            pltpu.VMEM((frames, 3 * latent_width, (rows + 4) * width), BF16),
            pltpu.VMEM((channels, (rows + 2) * width), F32),
            pltpu.VMEM((channels, (rows + 2) * width), BF16),
            pltpu.VMEM((frames, 3, channels, (rows + 2) * width), BF16),
            pltpu.VMEM((channels, LANES), F32),
            pltpu.VMEM((live * 9, out_channels, channels), BF16),
            pltpu.SemaphoreType.DMA((slabs,)),
            pltpu.SemaphoreType.DMA(()),
        ]
        + weights,
        compiler_params=params(),
        cost_estimate=cost(
            live * 18 * frames * out_channels * channels * rows * width,
            live * 18 * out_channels * channels,
        ),
        name="decode",
    )(me, gain, entry, conv, *held)
    gated = lax.optimization_barrier((decoded, *direct))
    decoded, direct = gated[0], list(gated[1:])
    across = [xor_permute(piece, "seq", 2) for piece in direct]

    shape = (9, pad_channels, channels)

    def finish(parts, sources, grad):
        return pl.pallas_call(
            functools.partial(finish_kernel, sources),
            out_shape=jax.ShapeDtypeStruct(grad_shape, F32),
            in_specs=[smem()] + [vmem()] * len(parts) + [hbm],
            out_specs=hbm,
            scratch_shapes=[
                pltpu.VMEM((len(parts),) + shape, F32),
                pltpu.SemaphoreType.DMA((len(parts),)),
            ],
            input_output_aliases={len(parts) + 1: 0},
            compiler_params=params(),
            cost_estimate=cost(0, len(parts) * real_rows * channels * 6),
            name="finish",
        )(me, *[p.reshape(shape) for p in parts], grad)

    def both_cores(group):
        parts = [p for p, _ in group] + [xor_permute(p, "seq", 1) for p, _ in group]
        return parts, [m for _, m in group] + [m ^ 1 for _, m in group]

    early = [(block, 0), (beside, 2), (direct[0], columns[0]), (across[0], columns[0] ^ 2)]
    grad = finish(*both_cores(early), grad)
    if columns[1:]:
        gated = lax.optimization_barrier((grad, decoded, *across[1:]))
        grad, decoded, across[1:] = gated[0], gated[1], list(gated[2:])
        late = []
        for position, mask in enumerate(columns[1:]):
            late += [(direct[position + 1], mask), (across[position + 1], mask ^ 2)]
        grad = finish(*both_cores(late), grad)
    if pad_channels != chip_channels:
        grad = grad.reshape(27, chips, pad_channels, channels)[:, :, :chip_channels]
    grad = grad.reshape(3, 3, 3, out_channels, channels).transpose(3, 0, 1, 2, 4)
    return decoded, grad


def solution(mesh):
    return jax.shard_map(
        per_device,
        mesh=mesh,
        in_specs=(
            P(None, "seq", None, "head"),
            P("head", None),
            P(),
            P(),
            P("head", None, None, None, None),
            P("head", None, "seq", None),
        ),
        out_specs=(P("head", None, "seq", None), P("head", None, None, None, None)),
        check_vma=False,
    )
```

```python
import functools

import jax
import jax.numpy as jnp
from jax import lax
from jax.experimental import pallas as pl
from jax.experimental.pallas import tpu as pltpu
from jax.sharding import PartitionSpec as P

LANES = 128
VMEM_LIMIT = 56 * 1024 * 1024
F32 = jnp.float32
BF16 = jnp.bfloat16


def params():
    return pltpu.CompilerParams(vmem_limit_bytes=VMEM_LIMIT)


def cost(flops, size):
    return pl.CostEstimate(flops=flops, transcendentals=0, bytes_accessed=size)


def vmem():
    return pl.BlockSpec(memory_space=pltpu.VMEM)


def smem():
    return pl.BlockSpec(memory_space=pltpu.SMEM)


def xor_permute(x, axis, mask):
    return lax.ppermute(x, axis, [(i, i ^ mask) for i in range(lax.axis_size(axis))])


def dot(a, b):
    return lax.dot_general(a, b, (((1,), (0,)), ((), ())), preferred_element_type=F32)


def dot_t(a, b):
    return lax.dot_general(a, b, (((1,), (1,)), ((), ())), preferred_element_type=F32)


def unpatchify_kernel(frames, tok_rows, tok_cols, own_ref, other_ref, out_ref):
    latent_width = out_ref.shape[0]
    features = (own_ref[...] + other_ref[...]).astype(BF16)
    width = 2 * tok_cols
    span = tok_rows * tok_cols
    source = lax.broadcasted_iota(jnp.int32, (span, tok_rows * width), 0)
    target = lax.broadcasted_iota(jnp.int32, (span, tok_rows * width), 1)
    same_row = source // tok_cols == target // width
    column = source % tok_cols
    even = (same_row & (target % width == 2 * column)).astype(BF16)
    odd = (same_row & (target % width == 2 * column + 1)).astype(BF16)
    for frame in range(frames):
        tokens = features[:, frame * span : (frame + 1) * span]
        left = dot(tokens, even)
        right = dot(tokens, odd)
        for row in range(tok_rows):
            cols = slice(row * width, (row + 1) * width)
            for half in range(2):
                base = half * 2 * latent_width
                cells = (
                    left[base : base + latent_width, cols]
                    + right[base + latent_width : base + 2 * latent_width, cols]
                )
                at = (frame * 2 * tok_rows + 2 * row + half) * width
                out_ref[:, at : at + width] = cells.astype(BF16)


def shifted(tile, shift):
    if shift == 1:
        return tile
    lane = lax.broadcasted_iota(jnp.int32, tile.shape, 1)
    if shift == 0:
        return jnp.where(lane == 0, 0.0, pltpu.roll(tile, 1, 1))
    return jnp.where(lane == LANES - 1, 0.0, pltpu.roll(tile, LANES - 1, 1))


def fetch(piece_refs, mask_lists, slot_ref, sems):
    copies = []
    for index, (piece_ref, masks) in enumerate(zip(piece_refs, mask_lists)):
        for position, mask in enumerate(masks):
            copies.append(
                pltpu.make_async_copy(
                    piece_ref.at[position], slot_ref.at[mask], sems.at[index * len(masks) + position]
                )
            )
    for copy in copies:
        copy.start()
    return copies


def place_latent(slot_ref, stack_ref, me, first_slab, slab_count, frames, rows, slabs):
    latent_width = stack_ref.shape[1] // 3
    for offset in range(-1, slab_count + 1):
        slab = first_slab + offset
        inside = ((slab >= 0) & (slab < slabs)).astype(F32)
        source = jnp.clip(slab, 0, slabs - 1) ^ me
        needed = range(rows)
        if offset == -1:
            needed = range(rows - 2, rows)
        if offset == slab_count:
            needed = range(2)
        for frame in range(frames):
            for row in needed:
                at = (frame * rows + row) * LANES
                tile = slot_ref[source, :latent_width, at : at + LANES].astype(F32)
                if offset in (-1, slab_count):
                    tile = tile * inside
                to = (offset * rows + row + 2) * LANES
                for shift in range(3):
                    stack_ref[
                        frame, shift * latent_width : (shift + 1) * latent_width, to : to + LANES
                    ] = shifted(tile, shift).astype(BF16)


def hidden_rows(stack_ref, weight_ref, frame, first, count):
    pieces = []
    for source in range(max(0, frame - 2), frame + 1):
        for row_tap in range(3):
            at = pl.multiple_of((first + row_tap) * LANES, LANES)
            pieces.append(stack_ref[source, :, pl.ds(at, count * LANES)])
    return dot(weight_ref[...], jnp.concatenate(pieces, axis=0))


def load_entry(entry_ref, gain_ref, weight_refs, wide_gain):
    for weight_ref in weight_refs:
        depth = weight_ref.shape[1]
        start = entry_ref.shape[0] - depth
        weight_ref[...] = jnp.transpose(entry_ref[start:, :].astype(F32)).astype(BF16)
    wide_gain[...] = jnp.transpose(jnp.broadcast_to(0.5 * gain_ref[...], wide_gain.shape[::-1]))


def activate_rows(hidden_ref, gain_ref, act_ref, base, top_row, count, height):
    channels = hidden_ref.shape[0]
    block = 16
    for index in range(count):
        at = pl.multiple_of((base + index) * LANES, LANES)
        hidden = hidden_ref[:, pl.ds(at, LANES)]
        mean = jnp.sum(hidden * hidden, axis=0, keepdims=True) * (1.0 / channels)
        row = top_row + base + index
        inside = ((row >= 0) & (row < height)).astype(F32)
        inverse = jnp.broadcast_to(lax.rsqrt(mean + 1e-6) * inside, (block, LANES))
        for at_channel in range(0, channels, block):
            chunk = slice(at_channel, at_channel + block)
            half = hidden_ref[chunk, pl.ds(at, LANES)] * inverse * gain_ref[chunk, :]
            act_ref[chunk, pl.ds(at, LANES)] = (half + half * jnp.tanh(half)).astype(BF16)


def place_cotangent(
    slot_ref, flat_ref, out_ref, me, first_slab, slab_count, frames, rows, pad_channels, skip
):
    channels = slot_ref.shape[1] - skip
    half_rows = slab_count * rows
    group = 3 * pad_channels
    padded = out_ref.shape[0] // frames
    for frame in range(frames):
        for edge in (0, half_rows + 2):
            flat_ref[frame, :, edge * LANES : (edge + 2) * LANES] = jnp.zeros((group, 2 * LANES), F32)
    for offset in range(slab_count):
        source = (first_slab + offset) ^ me
        for frame in range(frames):
            for row in range(rows):
                at = (frame * rows + row) * LANES
                tile = slot_ref[source, skip:, at : at + LANES].astype(F32)
                if pad_channels != channels:
                    tile = jnp.concatenate(
                        [tile, jnp.zeros((pad_channels - channels, LANES), F32)], axis=0
                    )
                to = (offset * rows + row + 2) * LANES
                for tap in range(3):
                    flat_ref[frame, tap * pad_channels : (tap + 1) * pad_channels, to : to + LANES] = (
                        shifted(tile, 2 - tap)
                    )
    filler = [jnp.zeros((padded - 3 * group, LANES), F32)] if padded != 3 * group else []
    for frame in range(frames):
        for row in range(half_rows + 2):
            taps = [flat_ref[frame, :, (row + 2 - tap) * LANES : (row + 3 - tap) * LANES] for tap in range(3)]
            out_ref[frame * padded : (frame + 1) * padded, row * LANES : (row + 1) * LANES] = (
                jnp.concatenate(taps + filler, axis=0).astype(BF16)
            )


def gradient_kernel(frames, rows, slabs, masks, real_rows, pad_channels, *refs):
    me_ref, gain_ref, entry_ref = refs[:3]
    refs = refs[3:]
    piece_refs, refs = refs[: len(masks)], refs[len(masks) :]
    keep_ref, send_ref, slots, stack_ref, flat_ref, cot_ref = refs[:6]
    hid_a, hid_b, act_a, act_b, sum_ref, wide_gain, sems = refs[6:13]
    weight_refs = refs[13:]
    copies = fetch(piece_refs, masks, slots, sems)
    me = me_ref[0]
    core = me & 1
    slab_count = slabs // 2
    half_rows = slab_count * rows
    height = slabs * rows
    first_slab = core * slab_count
    padded = cot_ref.shape[0] // frames
    top_row = core * half_rows - 1
    ext = half_rows + 2
    count = max(d for d in range(1, 18) if ext % d == 0)
    width = count * LANES
    hidden = (hid_a, hid_b)
    acts = (act_a, act_b)
    load_entry(entry_ref, gain_ref, weight_refs, wide_gain)
    sum_ref[...] = jnp.zeros_like(sum_ref)
    for copy in copies:
        copy.wait()
    place_latent(slots, stack_ref, me, first_slab, slab_count, frames, rows, slabs)
    hid_a[...] = hidden_rows(stack_ref, weight_refs[0], 0, 0, ext)
    place_cotangent(
        slots, flat_ref, cot_ref, me, first_slab, slab_count, frames, rows, pad_channels,
        stack_ref.shape[1] // 3,
    )
    for frame in range(frames):

        def chunk(step, carry):
            at = pl.multiple_of(step * width, LANES)
            if frame + 1 < frames:
                hidden[(frame + 1) % 2][:, pl.ds(at, width)] = hidden_rows(
                    stack_ref, weight_refs[frame + 1], frame + 1, step * count, count
                )
            if frame > 0:
                last = min(frames, frame + 2)
                sum_ref[0 : (last - frame + 1) * padded, :] += dot_t(
                    cot_ref[(frame - 1) * padded : last * padded, pl.ds(at, width)],
                    acts[(frame - 1) % 2][:, pl.ds(at, width)],
                )
            activate_rows(
                hidden[frame % 2], wide_gain, acts[frame % 2], step * count, top_row, count, height
            )
            return carry

        lax.fori_loop(0, ext // count, chunk, 0)
    final = frames - 1
    sum_ref[0:padded, :] += dot_t(cot_ref[final * padded : frames * padded, :], acts[final % 2][...])
    keep_at = pl.multiple_of(core * padded, 16)
    send_at = pl.multiple_of((1 - core) * padded, 16)
    keep_ref[...] = sum_ref[pl.ds(keep_at, padded), :][:real_rows]
    send_ref[...] = sum_ref[pl.ds(send_at, padded), :][:real_rows].astype(BF16)


def decode_kernel(frames, rows, slabs, masks, me_ref, gain_ref, entry_ref, conv_hbm, *refs):
    piece_refs, refs = refs[: len(masks)], refs[len(masks) :]
    out_ref, slots, stack_ref, hid_ref, flat_ref, act_ref, wide_gain, conv_ref, sems, sem = refs[:10]
    weight_refs = refs[10:]
    live = conv_ref.shape[0] // 9
    load = pltpu.make_async_copy(conv_hbm.at[pl.ds((3 - live) * 9, live * 9)], conv_ref, sem)
    load.start()
    copies = fetch(piece_refs, masks, slots, sems)
    me = me_ref[0]
    height = slabs * rows
    load_entry(entry_ref, gain_ref, weight_refs, wide_gain)
    for copy in copies:
        copy.wait()
    place_latent(slots, stack_ref, me, me, 1, frames, rows, slabs)
    ext = rows + 2
    for frame in range(frames):
        hid_ref[...] = hidden_rows(stack_ref, weight_refs[frame], frame, 0, ext)
        activate_rows(hid_ref, wide_gain, flat_ref, 0, me * rows - 1, ext, height)
        for row in range(ext):
            tile = flat_ref[:, row * LANES : (row + 1) * LANES].astype(F32)
            for tap in range(3):
                act_ref[frame, tap, :, row * LANES : (row + 1) * LANES] = shifted(tile, tap).astype(BF16)
    load.wait()
    for frame in range(frames):
        kernels = []
        inputs = []
        for depth in range(max(0, 2 - frame), 3):
            for row_tap in range(3):
                for col_tap in range(3):
                    kernels.append(conv_ref[(depth - (3 - live)) * 9 + row_tap * 3 + col_tap])
                    inputs.append(
                        act_ref[frame + depth - 2, col_tap, :, row_tap * LANES : (row_tap + rows) * LANES]
                    )
        total = dot(jnp.concatenate(kernels, axis=1), jnp.concatenate(inputs, axis=0))
        for row in range(rows):
            out_ref[:, frame, row, :] = total[:, row * LANES : (row + 1) * LANES].astype(BF16)


def blank_kernel(blank, out_hbm, zero_ref, sems):
    zero_ref[...] = jnp.zeros_like(zero_ref)
    copies = [
        pltpu.make_async_copy(zero_ref, out_hbm.at[plane, tap], sems.at[plane * 9 + tap])
        for plane in range(blank)
        for tap in range(9)
    ]
    for copy in copies:
        copy.start()
    for copy in copies:
        copy.wait()


def finish_kernel(pieces, me_ref, *refs):
    count = len(pieces)
    piece_refs = refs[:count]
    out_hbm, wide_ref, sems = refs[count + 1 :]
    me = me_ref[0]
    channels = wide_ref.shape[2]
    copies = []
    for index, mask in enumerate(pieces):
        source = me ^ mask
        wide_ref[index] = piece_refs[index][...].astype(F32)
        at = pl.multiple_of((source >> 1) * channels, 8)
        copy = pltpu.make_async_copy(
            wide_ref.at[index], out_hbm.at[2 - (source & 1), :, pl.ds(at, channels), :], sems.at[index]
        )
        copy.start()
        copies.append(copy)
    for copy in copies:
        copy.wait()


def per_device(attn_out, w_proj, norm_gain, entry_weight, conv_weight, cotangent):
    frames, tok_rows, tok_cols, model_width = attn_out.shape
    latent_width = entry_weight.shape[4]
    channels = entry_weight.shape[0]
    out_channels = conv_weight.shape[0]
    slabs = lax.axis_size("seq")
    heads = lax.axis_size("head")
    chips = slabs // 2
    rows = 2 * tok_rows
    width = 2 * tok_cols
    height = rows * slabs
    half_rows = height // 2
    chip_channels = out_channels // chips
    pad_channels = -(-chip_channels // 8) * 8
    real_rows = 9 * pad_channels
    padded = -(-real_rows // 16) * 16
    lanes = (half_rows + 2) * width
    live = min(3, frames)
    me_index = lax.axis_index("seq")
    me = me_index.astype(jnp.int32).reshape(1)
    top = slabs // 2
    rest = [m for m in range(2, top, 2)]

    flat = cotangent.reshape(chips, chip_channels, frames * rows * width)
    chip = me_index // 2

    def wanted(side):
        return jnp.stack(
            [
                lax.dynamic_index_in_dim(flat, chip ^ ((m ^ side) // 2), 0, keepdims=False)
                for m in [0] + rest
            ]
        )

    near, far = wanted(0), wanted(top)
    got = xor_permute(far, "seq", top)

    attn_out = lax.optimization_barrier((attn_out, far))[0]
    flattened = attn_out.reshape(frames * tok_rows * tok_cols, model_width)
    partial_sum = lax.dot_general(
        w_proj, flattened, (((0,), (1,)), ((), ())), preferred_element_type=F32
    )
    step = heads // 2
    other = jnp.zeros_like(partial_sum)
    while step >= 1:
        other = xor_permute(partial_sum, "head", step)
        if step > 1:
            partial_sum = partial_sum + other
        step //= 2
    entry = entry_weight.transpose(1, 2, 3, 4, 0).reshape(27 * latent_width, channels)
    gain = norm_gain.reshape(1, channels)
    weights = [
        pltpu.VMEM((channels, min(3, f + 1) * 9 * latent_width), BF16) for f in range(frames)
    ]
    latent = pl.pallas_call(
        functools.partial(unpatchify_kernel, frames, tok_rows, tok_cols),
        out_shape=jax.ShapeDtypeStruct((latent_width, frames * rows * width), BF16),
        in_specs=[vmem(), vmem()],
        out_specs=vmem(),
        compiler_params=params(),
        name="unpatchify",
    )(partial_sum, other)

    blank = 3 - live
    hbm = pl.BlockSpec(memory_space=pl.ANY)
    grad_shape = (3, 9, chips * pad_channels, channels)
    grad = pl.pallas_call(
        functools.partial(blank_kernel, blank),
        out_shape=jax.ShapeDtypeStruct(grad_shape, F32),
        out_specs=hbm,
        scratch_shapes=[
            pltpu.VMEM((chips * pad_channels, channels), F32),
            pltpu.SemaphoreType.DMA((max(1, 9 * blank),)),
        ],
        compiler_params=params(),
        cost_estimate=cost(0, blank * 9 * out_channels * channels * 4),
        name="blank",
    )()

    across = xor_permute(latent, "seq", top)
    across, grad = lax.optimization_barrier((across, grad))
    latents = jnp.stack([latent, across])
    pieces = []
    masks = []
    for position, mask in enumerate([0] + rest):
        both = jnp.concatenate([latents, jnp.stack([near[position], got[position]])], axis=1)
        pieces.append(both if mask == 0 else xor_permute(both, "seq", mask))
        masks.append([mask, mask ^ top])
    pieces = pieces + [xor_permute(p, "seq", 1) for p in pieces]
    masks = masks + [[m ^ 1 for m in pair] for pair in masks]
    slot_shape = (slabs, latent_width + chip_channels, frames * rows * width)

    keep, send = pl.pallas_call(
        functools.partial(gradient_kernel, frames, rows, slabs, masks, real_rows, pad_channels),
        out_shape=(
            jax.ShapeDtypeStruct((real_rows, channels), F32),
            jax.ShapeDtypeStruct((real_rows, channels), BF16),
        ),
        in_specs=[smem(), vmem(), vmem()] + [hbm] * len(pieces),
        out_specs=(vmem(), vmem()),
        scratch_shapes=[
            pltpu.VMEM(slot_shape, BF16),
            pltpu.VMEM((frames, 3 * latent_width, (half_rows + 4) * width), BF16),
            pltpu.VMEM((frames, 3 * pad_channels, (half_rows + 4) * width), F32),
            pltpu.VMEM((frames * padded, lanes), BF16),
            pltpu.VMEM((channels, lanes), F32),
            pltpu.VMEM((channels, lanes), F32),
            pltpu.VMEM((channels, lanes), BF16),
            pltpu.VMEM((channels, lanes), BF16),
            pltpu.VMEM((live * padded, channels), F32),
            pltpu.VMEM((channels, LANES), F32),
            pltpu.SemaphoreType.DMA((slabs,)),
        ]
        + weights,
        compiler_params=params(),
        name="gradient",
    )(me, gain, entry, *pieces)
    block = (keep + xor_permute(send, "seq", 1).astype(F32)).astype(BF16)

    columns = [m for m in range(4, slabs, 4)]
    direct = [xor_permute(block, "seq", m) for m in columns]
    beside = xor_permute(block, "seq", 2)
    conv = conv_weight.transpose(1, 2, 3, 0, 4).reshape(27, out_channels, channels)

    held = lax.optimization_barrier((block, direct[0], *pieces))[2:]
    decoded = pl.pallas_call(
        functools.partial(decode_kernel, frames, rows, slabs, masks),
        out_shape=jax.ShapeDtypeStruct((out_channels, frames, rows, width), BF16),
        in_specs=[smem(), vmem(), vmem(), hbm] + [hbm] * len(pieces),
        out_specs=vmem(),
        scratch_shapes=[
            pltpu.VMEM(slot_shape, BF16),
            pltpu.VMEM((frames, 3 * latent_width, (rows + 4) * width), BF16),
            pltpu.VMEM((channels, (rows + 2) * width), F32),
            pltpu.VMEM((channels, (rows + 2) * width), BF16),
            pltpu.VMEM((frames, 3, channels, (rows + 2) * width), BF16),
            pltpu.VMEM((channels, LANES), F32),
            pltpu.VMEM((live * 9, out_channels, channels), BF16),
            pltpu.SemaphoreType.DMA((slabs,)),
            pltpu.SemaphoreType.DMA(()),
        ]
        + weights,
        compiler_params=params(),
        name="decode",
    )(me, gain, entry, conv, *held)
    nearest = xor_permute(direct[0], "seq", 2)
    gated = lax.optimization_barrier((decoded, block, beside, nearest, *direct))
    decoded, block, beside, nearest = gated[:4]
    direct = list(gated[4:])
    across = [nearest] + [xor_permute(piece, "seq", 2) for piece in direct[1:]]

    shape = (9, pad_channels, channels)

    def finish(parts, sources, grad):
        return pl.pallas_call(
            functools.partial(finish_kernel, sources),
            out_shape=jax.ShapeDtypeStruct(grad_shape, F32),
            in_specs=[smem()] + [vmem()] * len(parts) + [hbm],
            out_specs=hbm,
            scratch_shapes=[
                pltpu.VMEM((len(parts),) + shape, F32),
                pltpu.SemaphoreType.DMA((len(parts),)),
            ],
            input_output_aliases={len(parts) + 1: 0},
            compiler_params=params(),
            cost_estimate=cost(0, len(parts) * real_rows * channels * 6),
            name="finish",
        )(me, *[p.reshape(shape) for p in parts], grad)

    def both_cores(group):
        parts = [p for p, _ in group] + [xor_permute(p, "seq", 1) for p, _ in group]
        return parts, [m for _, m in group] + [m ^ 1 for _, m in group]

    early = [(block, 0), (beside, 2), (direct[0], columns[0]), (across[0], columns[0] ^ 2)]
    grad = finish(*both_cores(early), grad)
    if columns[1:]:
        gated = lax.optimization_barrier((grad, decoded, *across[1:]))
        grad, decoded, across[1:] = gated[0], gated[1], list(gated[2:])
        late = []
        for position, mask in enumerate(columns[1:]):
            late += [(direct[position + 1], mask), (across[position + 1], mask ^ 2)]
        grad = finish(*both_cores(late), grad)
    if pad_channels != chip_channels:
        grad = grad.reshape(27, chips, pad_channels, channels)[:, :, :chip_channels]
    grad = grad.reshape(3, 3, 3, out_channels, channels).transpose(3, 0, 1, 2, 4)
    return decoded, grad


def solution(mesh):
    return jax.shard_map(
        per_device,
        mesh=mesh,
        in_specs=(
            P(None, "seq", None, "head"),
            P("head", None),
            P(),
            P(),
            P("head", None, None, None, None),
            P("head", None, "seq", None),
        ),
        out_specs=(P("head", None, "seq", None), P("head", None, None, None, None)),
        check_vma=False,
    )
```

```python
import functools

import jax
import jax.numpy as jnp
from jax import lax
from jax.experimental import pallas as pl
from jax.experimental.pallas import tpu as pltpu
from jax.sharding import PartitionSpec as P

LANES = 128
VMEM_LIMIT = 56 * 1024 * 1024
F32 = jnp.float32
BF16 = jnp.bfloat16


def params():
    return pltpu.CompilerParams(vmem_limit_bytes=VMEM_LIMIT)


def cost(flops, size):
    return pl.CostEstimate(flops=flops, transcendentals=0, bytes_accessed=size)


def vmem():
    return pl.BlockSpec(memory_space=pltpu.VMEM)


def smem():
    return pl.BlockSpec(memory_space=pltpu.SMEM)


def xor_permute(x, axis, mask):
    return lax.ppermute(x, axis, [(i, i ^ mask) for i in range(lax.axis_size(axis))])


def dot(a, b):
    return lax.dot_general(a, b, (((1,), (0,)), ((), ())), preferred_element_type=F32)


def dot_t(a, b):
    return lax.dot_general(a, b, (((1,), (1,)), ((), ())), preferred_element_type=F32)


def unpatchify_kernel(frames, tok_rows, tok_cols, own_ref, other_ref, out_ref):
    latent_width = out_ref.shape[0]
    features = (own_ref[...] + other_ref[...]).astype(BF16)
    width = 2 * tok_cols
    span = tok_rows * tok_cols
    source = lax.broadcasted_iota(jnp.int32, (span, tok_rows * width), 0)
    target = lax.broadcasted_iota(jnp.int32, (span, tok_rows * width), 1)
    same_row = source // tok_cols == target // width
    column = source % tok_cols
    even = (same_row & (target % width == 2 * column)).astype(BF16)
    odd = (same_row & (target % width == 2 * column + 1)).astype(BF16)
    for frame in range(frames):
        tokens = features[:, frame * span : (frame + 1) * span]
        left = dot(tokens, even)
        right = dot(tokens, odd)
        for row in range(tok_rows):
            cols = slice(row * width, (row + 1) * width)
            for half in range(2):
                base = half * 2 * latent_width
                cells = (
                    left[base : base + latent_width, cols]
                    + right[base + latent_width : base + 2 * latent_width, cols]
                )
                at = (frame * 2 * tok_rows + 2 * row + half) * width
                out_ref[:, at : at + width] = cells.astype(BF16)


def shifted(tile, shift):
    if shift == 1:
        return tile
    lane = lax.broadcasted_iota(jnp.int32, tile.shape, 1)
    if shift == 0:
        return jnp.where(lane == 0, 0.0, pltpu.roll(tile, 1, 1))
    return jnp.where(lane == LANES - 1, 0.0, pltpu.roll(tile, LANES - 1, 1))


def fetch(piece_refs, mask_lists, slot_ref, sems):
    count = slot_ref.shape[1]
    copies = []
    for index, (piece_ref, masks) in enumerate(zip(piece_refs, mask_lists)):
        for position, mask in enumerate(masks):
            copies.append(
                pltpu.make_async_copy(
                    piece_ref.at[position, pl.ds(0, count)],
                    slot_ref.at[mask],
                    sems.at[index * len(masks) + position],
                )
            )
    for copy in copies:
        copy.start()
    return copies


def place_latent(slot_ref, stack_ref, me, first_slab, slab_count, frames, rows, slabs):
    latent_width = stack_ref.shape[1] // 3
    for offset in range(-1, slab_count + 1):
        slab = first_slab + offset
        inside = ((slab >= 0) & (slab < slabs)).astype(F32)
        source = jnp.clip(slab, 0, slabs - 1) ^ me
        needed = range(rows)
        if offset == -1:
            needed = range(rows - 2, rows)
        if offset == slab_count:
            needed = range(2)
        for frame in range(frames):
            for row in needed:
                at = (frame * rows + row) * LANES
                tile = slot_ref[source, :latent_width, at : at + LANES].astype(F32)
                if offset in (-1, slab_count):
                    tile = tile * inside
                to = (offset * rows + row + 2) * LANES
                for shift in range(3):
                    stack_ref[
                        frame, shift * latent_width : (shift + 1) * latent_width, to : to + LANES
                    ] = shifted(tile, shift).astype(BF16)


def hidden_rows(stack_ref, weight_ref, frame, first, count):
    pieces = []
    for source in range(max(0, frame - 2), frame + 1):
        for row_tap in range(3):
            at = pl.multiple_of((first + row_tap) * LANES, LANES)
            pieces.append(stack_ref[source, :, pl.ds(at, count * LANES)])
    return dot(weight_ref[...], jnp.concatenate(pieces, axis=0))


def load_entry(entry_ref, gain_ref, weight_refs, wide_gain):
    for weight_ref in weight_refs:
        depth = weight_ref.shape[1]
        start = entry_ref.shape[0] - depth
        weight_ref[...] = jnp.transpose(entry_ref[start:, :].astype(F32)).astype(BF16)
    wide_gain[...] = jnp.transpose(jnp.broadcast_to(0.5 * gain_ref[...], wide_gain.shape[::-1]))


def activate_rows(hidden_ref, gain_ref, act_ref, base, top_row, count, height):
    channels = hidden_ref.shape[0]
    block = 16
    for index in range(count):
        at = pl.multiple_of((base + index) * LANES, LANES)
        hidden = hidden_ref[:, pl.ds(at, LANES)]
        mean = jnp.sum(hidden * hidden, axis=0, keepdims=True) * (1.0 / channels)
        row = top_row + base + index
        inside = ((row >= 0) & (row < height)).astype(F32)
        inverse = jnp.broadcast_to(lax.rsqrt(mean + 1e-6) * inside, (block, LANES))
        for at_channel in range(0, channels, block):
            chunk = slice(at_channel, at_channel + block)
            half = hidden_ref[chunk, pl.ds(at, LANES)] * inverse * gain_ref[chunk, :]
            act_ref[chunk, pl.ds(at, LANES)] = (half + half * jnp.tanh(half)).astype(BF16)


def place_cotangent(
    slot_ref, flat_ref, out_ref, me, first_slab, slab_count, frames, rows, pad_channels, skip
):
    channels = slot_ref.shape[1] - skip
    half_rows = slab_count * rows
    group = 3 * pad_channels
    padded = out_ref.shape[0] // frames
    for frame in range(frames):
        for edge in (0, half_rows + 2):
            flat_ref[frame, :, edge * LANES : (edge + 2) * LANES] = jnp.zeros((group, 2 * LANES), F32)
    for offset in range(slab_count):
        source = (first_slab + offset) ^ me
        for frame in range(frames):
            for row in range(rows):
                at = (frame * rows + row) * LANES
                tile = slot_ref[source, skip:, at : at + LANES].astype(F32)
                if pad_channels != channels:
                    tile = jnp.concatenate(
                        [tile, jnp.zeros((pad_channels - channels, LANES), F32)], axis=0
                    )
                to = (offset * rows + row + 2) * LANES
                for tap in range(3):
                    flat_ref[frame, tap * pad_channels : (tap + 1) * pad_channels, to : to + LANES] = (
                        shifted(tile, 2 - tap)
                    )
    filler = [jnp.zeros((padded - 3 * group, LANES), F32)] if padded != 3 * group else []
    for frame in range(frames):
        for row in range(half_rows + 2):
            taps = [flat_ref[frame, :, (row + 2 - tap) * LANES : (row + 3 - tap) * LANES] for tap in range(3)]
            out_ref[frame * padded : (frame + 1) * padded, row * LANES : (row + 1) * LANES] = (
                jnp.concatenate(taps + filler, axis=0).astype(BF16)
            )


def gradient_kernel(frames, rows, slabs, masks, real_rows, pad_channels, *refs):
    me_ref, gain_ref, entry_ref = refs[:3]
    refs = refs[3:]
    piece_refs, refs = refs[: len(masks)], refs[len(masks) :]
    keep_ref, send_ref, slots, stack_ref, flat_ref, cot_ref = refs[:6]
    hid_a, hid_b, act_a, act_b, sum_ref, wide_gain, sems = refs[6:13]
    weight_refs = refs[13:]
    copies = fetch(piece_refs, masks, slots, sems)
    me = me_ref[0]
    core = me & 1
    slab_count = slabs // 2
    half_rows = slab_count * rows
    height = slabs * rows
    first_slab = core * slab_count
    padded = cot_ref.shape[0] // frames
    top_row = core * half_rows - 1
    ext = half_rows + 2
    count = max(d for d in range(1, 18) if ext % d == 0)
    width = count * LANES
    hidden = (hid_a, hid_b)
    acts = (act_a, act_b)
    load_entry(entry_ref, gain_ref, weight_refs, wide_gain)
    sum_ref[...] = jnp.zeros_like(sum_ref)
    for copy in copies:
        copy.wait()
    place_latent(slots, stack_ref, me, first_slab, slab_count, frames, rows, slabs)
    hid_a[...] = hidden_rows(stack_ref, weight_refs[0], 0, 0, ext)
    place_cotangent(
        slots, flat_ref, cot_ref, me, first_slab, slab_count, frames, rows, pad_channels,
        stack_ref.shape[1] // 3,
    )
    for frame in range(frames):

        def chunk(step, carry):
            at = pl.multiple_of(step * width, LANES)
            if frame + 1 < frames:
                hidden[(frame + 1) % 2][:, pl.ds(at, width)] = hidden_rows(
                    stack_ref, weight_refs[frame + 1], frame + 1, step * count, count
                )
            if frame > 0:
                last = min(frames, frame + 2)
                sum_ref[0 : (last - frame + 1) * padded, :] += dot_t(
                    cot_ref[(frame - 1) * padded : last * padded, pl.ds(at, width)],
                    acts[(frame - 1) % 2][:, pl.ds(at, width)],
                )
            activate_rows(
                hidden[frame % 2], wide_gain, acts[frame % 2], step * count, top_row, count, height
            )
            return carry

        lax.fori_loop(0, ext // count, chunk, 0)
    final = frames - 1
    sum_ref[0:padded, :] += dot_t(cot_ref[final * padded : frames * padded, :], acts[final % 2][...])
    keep_at = pl.multiple_of(core * padded, 16)
    send_at = pl.multiple_of((1 - core) * padded, 16)
    keep_ref[...] = sum_ref[pl.ds(keep_at, padded), :][:real_rows]
    send_ref[...] = sum_ref[pl.ds(send_at, padded), :][:real_rows].astype(BF16)


def decode_kernel(frame, frames, rows, slabs, masks, me_ref, gain_ref, entry_ref, conv_hbm, *refs):
    other_refs, refs = (refs[: frames - 1], refs[frames - 1 :]) if frame == 0 else ((), refs)
    sources = range(max(0, frame - 2), frame + 1)
    piece_refs, refs = refs[: len(masks)], refs[len(masks) :]
    out_ref, slots, stack_ref, hid_ref, flat_ref, act_ref, wide_gain, conv_ref, sems, sem = refs[:10]
    weight_refs = refs[10:]
    taps = conv_ref.shape[0]
    copies = fetch(piece_refs, masks, slots, sems)
    load = pltpu.make_async_copy(conv_hbm.at[pl.ds(27 - taps, taps)], conv_ref, sem)
    load.start()
    me = me_ref[0]
    height = slabs * rows
    load_entry(entry_ref, gain_ref, weight_refs, wide_gain)
    for copy in copies:
        copy.wait()
    place_latent(slots, stack_ref, me, me, 1, frames, rows, slabs)
    ext = rows + 2
    for position, source in enumerate(sources):
        hid_ref[...] = hidden_rows(stack_ref, weight_refs[position], source, 0, ext)
        activate_rows(hid_ref, wide_gain, flat_ref, 0, me * rows - 1, ext, height)
        for row in range(ext):
            tile = flat_ref[:, row * LANES : (row + 1) * LANES].astype(F32)
            for tap in range(3):
                act_ref[position, tap, :, row * LANES : (row + 1) * LANES] = shifted(tile, tap).astype(BF16)
    load.wait()
    kernels = []
    inputs = []
    for position in range(len(sources)):
        for row_tap in range(3):
            for col_tap in range(3):
                kernels.append(conv_ref[position * 9 + row_tap * 3 + col_tap])
                inputs.append(act_ref[position, col_tap, :, row_tap * LANES : (row_tap + rows) * LANES])
    total = dot(jnp.concatenate(kernels, axis=1), jnp.concatenate(inputs, axis=0))
    for row in range(rows):
        tile = total[:, row * LANES : (row + 1) * LANES].astype(BF16)
        if frame == 0:
            out_ref[:, 0, row, :] = tile
        else:
            out_ref[:, row, :] = tile
    for index, other_ref in enumerate(other_refs):
        out_ref[:, index + 1] = other_ref[...]


def blank_kernel(blank, out_hbm, zero_ref, sems):
    zero_ref[...] = jnp.zeros_like(zero_ref)
    copies = [
        pltpu.make_async_copy(zero_ref, out_hbm.at[plane, tap], sems.at[plane * 9 + tap])
        for plane in range(blank)
        for tap in range(9)
    ]
    for copy in copies:
        copy.start()
    for copy in copies:
        copy.wait()


def finish_kernel(pieces, me_ref, *refs):
    count = len(pieces)
    piece_refs = refs[:count]
    out_hbm, narrow_ref, wide_ref, in_sems, out_sems = refs[count + 1 :]
    me = me_ref[0]
    channels = wide_ref.shape[2]
    loads = [
        pltpu.make_async_copy(piece_refs[index], narrow_ref.at[index], in_sems.at[index])
        for index in range(count)
    ]
    for load in loads:
        load.start()
    stores = []
    for index, mask in enumerate(pieces):
        source = me ^ mask
        loads[index].wait()
        wide_ref[index] = narrow_ref[index].astype(F32)
        at = pl.multiple_of((source >> 1) * channels, 8)
        store = pltpu.make_async_copy(
            wide_ref.at[index], out_hbm.at[2 - (source & 1), :, pl.ds(at, channels), :], out_sems.at[index]
        )
        store.start()
        stores.append(store)
    for store in stores:
        store.wait()


def per_device(attn_out, w_proj, norm_gain, entry_weight, conv_weight, cotangent):
    frames, tok_rows, tok_cols, model_width = attn_out.shape
    latent_width = entry_weight.shape[4]
    channels = entry_weight.shape[0]
    out_channels = conv_weight.shape[0]
    slabs = lax.axis_size("seq")
    heads = lax.axis_size("head")
    chips = slabs // 2
    rows = 2 * tok_rows
    width = 2 * tok_cols
    height = rows * slabs
    half_rows = height // 2
    chip_channels = out_channels // chips
    pad_channels = -(-chip_channels // 8) * 8
    real_rows = 9 * pad_channels
    padded = -(-real_rows // 16) * 16
    lanes = (half_rows + 2) * width
    live = min(3, frames)
    me_index = lax.axis_index("seq")
    me = me_index.astype(jnp.int32).reshape(1)
    top = slabs // 2
    rest = [m for m in range(2, top, 2)]

    flat = cotangent.reshape(chips, chip_channels, frames * rows * width)
    chip = me_index // 2

    def wanted(side):
        return jnp.stack(
            [
                lax.dynamic_index_in_dim(flat, chip ^ ((m ^ side) // 2), 0, keepdims=False)
                for m in [0] + rest
            ]
        )

    near, far = wanted(0), wanted(top)
    got = xor_permute(far, "seq", top)

    attn_out = lax.optimization_barrier((attn_out, far))[0]
    flattened = attn_out.reshape(frames * tok_rows * tok_cols, model_width)
    partial_sum = lax.dot_general(
        w_proj, flattened, (((0,), (1,)), ((), ())), preferred_element_type=F32
    )
    step = heads // 2
    other = jnp.zeros_like(partial_sum)
    while step >= 1:
        other = xor_permute(partial_sum, "head", step)
        if step > 1:
            partial_sum = partial_sum + other
        step //= 2
    entry = entry_weight.transpose(1, 2, 3, 4, 0).reshape(27 * latent_width, channels)
    gain = norm_gain.reshape(1, channels)
    weights = [
        pltpu.VMEM((channels, min(3, f + 1) * 9 * latent_width), BF16) for f in range(frames)
    ]
    latent = pl.pallas_call(
        functools.partial(unpatchify_kernel, frames, tok_rows, tok_cols),
        out_shape=jax.ShapeDtypeStruct((latent_width, frames * rows * width), BF16),
        in_specs=[vmem(), vmem()],
        out_specs=vmem(),
        compiler_params=params(),
        name="unpatchify",
    )(partial_sum, other)

    blank = 3 - live
    hbm = pl.BlockSpec(memory_space=pl.ANY)
    grad_shape = (3, 9, chips * pad_channels, channels)
    grad = pl.pallas_call(
        functools.partial(blank_kernel, blank),
        out_shape=jax.ShapeDtypeStruct(grad_shape, F32),
        out_specs=hbm,
        scratch_shapes=[
            pltpu.VMEM((chips * pad_channels, channels), F32),
            pltpu.SemaphoreType.DMA((max(1, 9 * blank),)),
        ],
        compiler_params=params(),
        cost_estimate=cost(0, blank * 9 * out_channels * channels * 4),
        name="blank",
    )()

    across = xor_permute(latent, "seq", top)
    across, grad = lax.optimization_barrier((across, grad))
    latents = jnp.stack([latent, across])
    pieces = []
    masks = []
    for position, mask in enumerate([0] + rest):
        both = jnp.concatenate([latents, jnp.stack([near[position], got[position]])], axis=1)
        pieces.append(both if mask == 0 else xor_permute(both, "seq", mask))
        masks.append([mask, mask ^ top])
    pieces = pieces + [xor_permute(p, "seq", 1) for p in pieces]
    masks = masks + [[m ^ 1 for m in pair] for pair in masks]
    slot_shape = (slabs, latent_width + chip_channels, frames * rows * width)

    keep, send = pl.pallas_call(
        functools.partial(gradient_kernel, frames, rows, slabs, masks, real_rows, pad_channels),
        out_shape=(
            jax.ShapeDtypeStruct((real_rows, channels), F32),
            jax.ShapeDtypeStruct((real_rows, channels), BF16),
        ),
        in_specs=[smem(), vmem(), vmem()] + [hbm] * len(pieces),
        out_specs=(vmem(), vmem()),
        scratch_shapes=[
            pltpu.VMEM(slot_shape, BF16),
            pltpu.VMEM((frames, 3 * latent_width, (half_rows + 4) * width), BF16),
            pltpu.VMEM((frames, 3 * pad_channels, (half_rows + 4) * width), F32),
            pltpu.VMEM((frames * padded, lanes), BF16),
            pltpu.VMEM((channels, lanes), F32),
            pltpu.VMEM((channels, lanes), F32),
            pltpu.VMEM((channels, lanes), BF16),
            pltpu.VMEM((channels, lanes), BF16),
            pltpu.VMEM((live * padded, channels), F32),
            pltpu.VMEM((channels, LANES), F32),
            pltpu.SemaphoreType.DMA((slabs,)),
        ]
        + weights,
        compiler_params=params(),
        name="gradient",
    )(me, gain, entry, *pieces)
    block = (keep + xor_permute(send, "seq", 1).astype(F32)).astype(BF16)

    columns = [m for m in range(4, slabs, 4)]
    direct = [xor_permute(block, "seq", m) for m in columns]
    beside = xor_permute(block, "seq", 2)
    conv = conv_weight.transpose(1, 2, 3, 0, 4).reshape(27, out_channels, channels)

    def decode(frame, held, others=()):
        count = min(3, frame + 1)
        last = (frames,) if frame == 0 else ()
        return pl.pallas_call(
            functools.partial(decode_kernel, frame, frames, rows, slabs, masks),
            out_shape=jax.ShapeDtypeStruct((out_channels,) + last + (rows, width), BF16),
            in_specs=[smem(), vmem(), vmem(), hbm] + [vmem()] * len(others) + [hbm] * len(pieces),
            out_specs=vmem(),
            scratch_shapes=[
                pltpu.VMEM((slabs, latent_width, frames * rows * width), BF16),
                pltpu.VMEM((frames, 3 * latent_width, (rows + 4) * width), BF16),
                pltpu.VMEM((channels, (rows + 2) * width), F32),
                pltpu.VMEM((channels, (rows + 2) * width), BF16),
                pltpu.VMEM((count, 3, channels, (rows + 2) * width), BF16),
                pltpu.VMEM((channels, LANES), F32),
                pltpu.VMEM((count * 9, out_channels, channels), BF16),
                pltpu.SemaphoreType.DMA((slabs,)),
                pltpu.SemaphoreType.DMA(()),
            ]
            + weights[max(0, frame - 2) : frame + 1],
            compiler_params=params(),
            name="decode",
        )(me, gain, entry, conv, *others, *held)

    shape = (9, pad_channels, channels)

    def finish(parts, sources, grad):
        return pl.pallas_call(
            functools.partial(finish_kernel, sources),
            out_shape=jax.ShapeDtypeStruct(grad_shape, F32),
            in_specs=[smem()] + [hbm] * (len(parts) + 1),
            out_specs=hbm,
            scratch_shapes=[
                pltpu.VMEM((len(parts),) + shape, BF16),
                pltpu.VMEM((len(parts),) + shape, F32),
                pltpu.SemaphoreType.DMA((len(parts),)),
                pltpu.SemaphoreType.DMA((len(parts),)),
            ],
            input_output_aliases={len(parts) + 1: 0},
            compiler_params=params(),
            name="finish",
        )(me, *[p.reshape(shape) for p in parts], grad)

    def both_cores(group):
        parts = [p for p, _ in group] + [xor_permute(p, "seq", 1) for p, _ in group]
        return parts, [m for _, m in group] + [m ^ 1 for _, m in group]

    nearest = xor_permute(direct[0], "seq", 2)
    held = lax.optimization_barrier((direct[0], *pieces))[1:]
    decoded = [decode(frame, held) for frame in range(1, frames)]
    gate = decoded[-1] if frames > 1 else block
    half = max(1, len(direct[1:]) // 2)
    gated = lax.optimization_barrier((gate, block, beside, nearest, *direct[: 1 + half]))
    if frames > 1:
        decoded[-1] = gated[0]
    block, beside, nearest = gated[1:4]
    direct[: 1 + half] = gated[4:]
    second = direct[1 : 1 + half]
    across = [xor_permute(piece, "seq", 2) for piece in second]
    grad = finish(
        *both_cores(
            [(block, 0), (beside, 2), (direct[0], columns[0]), (nearest, columns[0] ^ 2)]
        ),
        grad,
    )
    third = list(lax.optimization_barrier((gate, *direct[1 + half :])))[1:]
    across = across + [xor_permute(piece, "seq", 2) for piece in third]
    held = lax.optimization_barrier((grad, *pieces))[1:]
    decoded = decode(0, held, decoded)
    gated = lax.optimization_barrier((decoded, *across))
    decoded, across = gated[0], gated[1:]
    late = []
    for mask, piece, swapped in zip(columns[1:], second + third, across):
        late += [(piece, mask), (swapped, mask ^ 2)]
    if late:
        grad = finish(*both_cores(late), grad)
    if pad_channels != chip_channels:
        grad = grad.reshape(27, chips, pad_channels, channels)[:, :, :chip_channels]
    grad = grad.reshape(3, 3, 3, out_channels, channels).transpose(3, 0, 1, 2, 4)
    return decoded, grad


def solution(mesh):
    return jax.shard_map(
        per_device,
        mesh=mesh,
        in_specs=(
            P(None, "seq", None, "head"),
            P("head", None),
            P(),
            P(),
            P("head", None, None, None, None),
            P("head", None, "seq", None),
        ),
        out_specs=(P("head", None, "seq", None), P("head", None, None, None, None)),
        check_vma=False,
    )
```

```python
import functools

import jax
import jax.numpy as jnp
from jax import lax
from jax.experimental import pallas as pl
from jax.experimental.pallas import tpu as pltpu
from jax.sharding import PartitionSpec as P

LANES = 128
VMEM_LIMIT = 56 * 1024 * 1024
F32 = jnp.float32
BF16 = jnp.bfloat16


def params():
    return pltpu.CompilerParams(vmem_limit_bytes=VMEM_LIMIT)


def cost(flops, size):
    return pl.CostEstimate(flops=flops, transcendentals=0, bytes_accessed=size)


def vmem():
    return pl.BlockSpec(memory_space=pltpu.VMEM)


def smem():
    return pl.BlockSpec(memory_space=pltpu.SMEM)


def xor_permute(x, axis, mask):
    return lax.ppermute(x, axis, [(i, i ^ mask) for i in range(lax.axis_size(axis))])


def dot(a, b):
    return lax.dot_general(a, b, (((1,), (0,)), ((), ())), preferred_element_type=F32)


def dot_t(a, b):
    return lax.dot_general(a, b, (((1,), (1,)), ((), ())), preferred_element_type=F32)


def unpatchify_kernel(frames, tok_rows, tok_cols, own_ref, other_ref, out_ref):
    latent_width = out_ref.shape[0]
    features = (own_ref[...] + other_ref[...]).astype(BF16)
    width = 2 * tok_cols
    span = tok_rows * tok_cols
    source = lax.broadcasted_iota(jnp.int32, (span, tok_rows * width), 0)
    target = lax.broadcasted_iota(jnp.int32, (span, tok_rows * width), 1)
    same_row = source // tok_cols == target // width
    column = source % tok_cols
    even = (same_row & (target % width == 2 * column)).astype(BF16)
    odd = (same_row & (target % width == 2 * column + 1)).astype(BF16)
    for frame in range(frames):
        tokens = features[:, frame * span : (frame + 1) * span]
        left = dot(tokens, even)
        right = dot(tokens, odd)
        for row in range(tok_rows):
            cols = slice(row * width, (row + 1) * width)
            for half in range(2):
                base = half * 2 * latent_width
                cells = (
                    left[base : base + latent_width, cols]
                    + right[base + latent_width : base + 2 * latent_width, cols]
                )
                at = (frame * 2 * tok_rows + 2 * row + half) * width
                out_ref[:, at : at + width] = cells.astype(BF16)


def shifted(tile, shift):
    if shift == 1:
        return tile
    lane = lax.broadcasted_iota(jnp.int32, tile.shape, 1)
    if shift == 0:
        return jnp.where(lane == 0, 0.0, pltpu.roll(tile, 1, 1))
    return jnp.where(lane == LANES - 1, 0.0, pltpu.roll(tile, LANES - 1, 1))


def fetch(mixed_refs, near_refs, masks, lat_slots, cot_slots, sems):
    copies = []

    def load(source, target):
        copies.append(pltpu.make_async_copy(source, target, sems.at[len(copies)]))
        copies[-1].start()

    latent_width = lat_slots.shape[1]
    for mixed_ref, (first, second) in zip(mixed_refs, masks):
        load(mixed_ref.at[pl.ds(0, latent_width)], lat_slots.at[first])
        load(mixed_ref.at[pl.ds(latent_width, latent_width)], lat_slots.at[second])
    for mixed_ref, near_ref, (first, second) in zip(mixed_refs, near_refs, masks):
        channels = cot_slots.shape[1]
        load(near_ref, cot_slots.at[first])
        load(mixed_ref.at[pl.ds(2 * latent_width, channels)], cot_slots.at[second])
    return copies


def place_latent(slot_ref, stack_ref, me, first_slab, slab_count, frames, rows, slabs):
    latent_width = stack_ref.shape[1] // 3
    for offset in range(-1, slab_count + 1):
        slab = first_slab + offset
        inside = ((slab >= 0) & (slab < slabs)).astype(F32)
        source = jnp.clip(slab, 0, slabs - 1) ^ me
        needed = range(rows)
        if offset == -1:
            needed = range(rows - 2, rows)
        if offset == slab_count:
            needed = range(2)
        for frame in range(frames):
            for row in needed:
                at = (frame * rows + row) * LANES
                tile = slot_ref[source, :, at : at + LANES].astype(F32)
                if offset in (-1, slab_count):
                    tile = tile * inside
                to = (offset * rows + row + 2) * LANES
                for shift in range(3):
                    stack_ref[
                        frame, shift * latent_width : (shift + 1) * latent_width, to : to + LANES
                    ] = shifted(tile, shift).astype(BF16)


def hidden_rows(stack_ref, weight_ref, frame, first, count):
    pieces = []
    for source in range(max(0, frame - 2), frame + 1):
        for row_tap in range(3):
            at = pl.multiple_of((first + row_tap) * LANES, LANES)
            pieces.append(stack_ref[source, :, pl.ds(at, count * LANES)])
    return dot(weight_ref[...], jnp.concatenate(pieces, axis=0))


def load_entry(entry_ref, gain_ref, weight_refs, wide_gain):
    for weight_ref in weight_refs:
        depth = weight_ref.shape[1]
        start = entry_ref.shape[0] - depth
        weight_ref[...] = jnp.transpose(entry_ref[start:, :].astype(F32)).astype(BF16)
    wide_gain[...] = jnp.transpose(jnp.broadcast_to(0.5 * gain_ref[...], wide_gain.shape[::-1]))


def activate_rows(hidden_ref, gain_ref, act_ref, base, top_row, count, height):
    channels = hidden_ref.shape[0]
    block = 16
    for index in range(count):
        at = pl.multiple_of((base + index) * LANES, LANES)
        hidden = hidden_ref[:, pl.ds(at, LANES)]
        mean = jnp.sum(hidden * hidden, axis=0, keepdims=True) * (1.0 / channels)
        row = top_row + base + index
        inside = ((row >= 0) & (row < height)).astype(F32)
        inverse = jnp.broadcast_to(lax.rsqrt(mean + 1e-6) * inside, (block, LANES))
        for at_channel in range(0, channels, block):
            chunk = slice(at_channel, at_channel + block)
            half = hidden_ref[chunk, pl.ds(at, LANES)] * inverse * gain_ref[chunk, :]
            act_ref[chunk, pl.ds(at, LANES)] = (half + half * jnp.tanh(half)).astype(BF16)


def place_cotangent(slot_ref, flat_ref, out_ref, me, first_slab, slab_count, frames, rows, pad_channels):
    channels = slot_ref.shape[1]
    half_rows = slab_count * rows
    group = 3 * pad_channels
    padded = out_ref.shape[0] // frames
    for frame in range(frames):
        for edge in (0, half_rows + 2):
            flat_ref[frame, :, edge * LANES : (edge + 2) * LANES] = jnp.zeros((group, 2 * LANES), F32)
    for offset in range(slab_count):
        source = (first_slab + offset) ^ me
        for frame in range(frames):
            for row in range(rows):
                at = (frame * rows + row) * LANES
                tile = slot_ref[source, :, at : at + LANES].astype(F32)
                if pad_channels != channels:
                    tile = jnp.concatenate(
                        [tile, jnp.zeros((pad_channels - channels, LANES), F32)], axis=0
                    )
                to = (offset * rows + row + 2) * LANES
                for tap in range(3):
                    flat_ref[frame, tap * pad_channels : (tap + 1) * pad_channels, to : to + LANES] = (
                        shifted(tile, 2 - tap)
                    )
    filler = [jnp.zeros((padded - 3 * group, LANES), F32)] if padded != 3 * group else []
    for frame in range(frames):
        for row in range(half_rows + 2):
            taps = [flat_ref[frame, :, (row + 2 - tap) * LANES : (row + 3 - tap) * LANES] for tap in range(3)]
            out_ref[frame * padded : (frame + 1) * padded, row * LANES : (row + 1) * LANES] = (
                jnp.concatenate(taps + filler, axis=0).astype(BF16)
            )


def gradient_kernel(frames, rows, slabs, masks, real_rows, pad_channels, *refs):
    me_ref, gain_ref, entry_ref = refs[:3]
    refs = refs[3:]
    count = len(masks)
    mixed_refs, near_refs, refs = refs[:count], refs[count : 2 * count], refs[2 * count :]
    keep_ref, send_ref, lat_slots, cot_slots, stack_ref, flat_ref, cot_ref = refs[:7]
    hid_a, hid_b, act_a, act_b, sum_ref, wide_gain, sems = refs[7:14]
    weight_refs = refs[14:]
    copies = fetch(mixed_refs, near_refs, masks, lat_slots, cot_slots, sems)
    me = me_ref[0]
    core = me & 1
    slab_count = slabs // 2
    half_rows = slab_count * rows
    height = slabs * rows
    first_slab = core * slab_count
    padded = cot_ref.shape[0] // frames
    top_row = core * half_rows - 1
    ext = half_rows + 2
    count = max(d for d in range(1, 18) if ext % d == 0)
    width = count * LANES
    hidden = (hid_a, hid_b)
    acts = (act_a, act_b)
    load_entry(entry_ref, gain_ref, weight_refs, wide_gain)
    sum_ref[...] = jnp.zeros_like(sum_ref)
    for copy in copies[: 2 * count]:
        copy.wait()
    place_latent(lat_slots, stack_ref, me, first_slab, slab_count, frames, rows, slabs)
    for copy in copies[2 * count :]:
        copy.wait()
    hid_a[...] = hidden_rows(stack_ref, weight_refs[0], 0, 0, ext)
    place_cotangent(
        cot_slots, flat_ref, cot_ref, me, first_slab, slab_count, frames, rows, pad_channels
    )
    for frame in range(frames):

        def chunk(step, carry):
            at = pl.multiple_of(step * width, LANES)
            if frame + 1 < frames:
                hidden[(frame + 1) % 2][:, pl.ds(at, width)] = hidden_rows(
                    stack_ref, weight_refs[frame + 1], frame + 1, step * count, count
                )
            if frame > 0:
                last = min(frames, frame + 2)
                sum_ref[0 : (last - frame + 1) * padded, :] += dot_t(
                    cot_ref[(frame - 1) * padded : last * padded, pl.ds(at, width)],
                    acts[(frame - 1) % 2][:, pl.ds(at, width)],
                )
            activate_rows(
                hidden[frame % 2], wide_gain, acts[frame % 2], step * count, top_row, count, height
            )
            return carry

        lax.fori_loop(0, ext // count, chunk, 0)
    final = frames - 1
    sum_ref[0:padded, :] += dot_t(cot_ref[final * padded : frames * padded, :], acts[final % 2][...])
    keep_at = pl.multiple_of(core * padded, 16)
    send_at = pl.multiple_of((1 - core) * padded, 16)
    keep_ref[...] = sum_ref[pl.ds(keep_at, padded), :][:real_rows]
    send_ref[...] = sum_ref[pl.ds(send_at, padded), :][:real_rows].astype(BF16)


def decode_kernel(frames, rows, slabs, masks, me_ref, gain_ref, entry_ref, conv_hbm, *refs):
    piece_refs, refs = refs[: len(masks)], refs[len(masks) :]
    out_ref, slots, stack_ref, hid_ref, flat_ref, act_ref, wide_gain, conv_ref, sems, sem = refs[:10]
    weight_refs = refs[10:]
    live = conv_ref.shape[0] // 9
    load = pltpu.make_async_copy(conv_hbm.at[pl.ds((3 - live) * 9, live * 9)], conv_ref, sem)
    load.start()
    copies = fetch(piece_refs, (), masks, slots, slots, sems)
    me = me_ref[0]
    height = slabs * rows
    load_entry(entry_ref, gain_ref, weight_refs, wide_gain)
    for copy in copies:
        copy.wait()
    place_latent(slots, stack_ref, me, me, 1, frames, rows, slabs)
    ext = rows + 2
    for frame in range(frames):
        hid_ref[...] = hidden_rows(stack_ref, weight_refs[frame], frame, 0, ext)
        activate_rows(hid_ref, wide_gain, flat_ref, 0, me * rows - 1, ext, height)
        for row in range(ext):
            tile = flat_ref[:, row * LANES : (row + 1) * LANES].astype(F32)
            for tap in range(3):
                act_ref[frame, tap, :, row * LANES : (row + 1) * LANES] = shifted(tile, tap).astype(BF16)
    load.wait()
    for frame in range(frames):
        kernels = []
        inputs = []
        for depth in range(max(0, 2 - frame), 3):
            for row_tap in range(3):
                for col_tap in range(3):
                    kernels.append(conv_ref[(depth - (3 - live)) * 9 + row_tap * 3 + col_tap])
                    inputs.append(
                        act_ref[frame + depth - 2, col_tap, :, row_tap * LANES : (row_tap + rows) * LANES]
                    )
        total = dot(jnp.concatenate(kernels, axis=1), jnp.concatenate(inputs, axis=0))
        for row in range(rows):
            out_ref[:, frame, row, :] = total[:, row * LANES : (row + 1) * LANES].astype(BF16)


def blank_kernel(blank, out_hbm, zero_ref, sems):
    zero_ref[...] = jnp.zeros_like(zero_ref)
    copies = [
        pltpu.make_async_copy(zero_ref, out_hbm.at[plane, tap], sems.at[plane * 9 + tap])
        for plane in range(blank)
        for tap in range(9)
    ]
    for copy in copies:
        copy.start()
    for copy in copies:
        copy.wait()


def finish_kernel(pieces, me_ref, *refs):
    count = len(pieces)
    piece_refs = refs[:count]
    out_hbm, narrow_ref, wide_ref, in_sems, out_sems = refs[count + 1 :]
    me = me_ref[0]
    channels = wide_ref.shape[2]
    loads = [
        pltpu.make_async_copy(piece_refs[index], narrow_ref.at[index], in_sems.at[index])
        for index in range(count)
    ]
    for load in loads:
        load.start()
    stores = []
    for index, mask in enumerate(pieces):
        source = me ^ mask
        loads[index].wait()
        wide_ref[index] = narrow_ref[index].astype(F32)
        at = pl.multiple_of((source >> 1) * channels, 8)
        store = pltpu.make_async_copy(
            wide_ref.at[index], out_hbm.at[2 - (source & 1), :, pl.ds(at, channels), :], out_sems.at[index]
        )
        store.start()
        stores.append(store)
    for store in stores:
        store.wait()


def per_device(attn_out, w_proj, norm_gain, entry_weight, conv_weight, cotangent):
    frames, tok_rows, tok_cols, model_width = attn_out.shape
    latent_width = entry_weight.shape[4]
    channels = entry_weight.shape[0]
    out_channels = conv_weight.shape[0]
    slabs = lax.axis_size("seq")
    heads = lax.axis_size("head")
    chips = slabs // 2
    rows = 2 * tok_rows
    width = 2 * tok_cols
    height = rows * slabs
    half_rows = height // 2
    chip_channels = out_channels // chips
    pad_channels = -(-chip_channels // 8) * 8
    real_rows = 9 * pad_channels
    padded = -(-real_rows // 16) * 16
    lanes = (half_rows + 2) * width
    live = min(3, frames)
    me_index = lax.axis_index("seq")
    me = me_index.astype(jnp.int32).reshape(1)
    top = slabs // 2
    rest = [m for m in range(2, top, 2)]

    chip = me_index // 2
    flat = cotangent.reshape(chips, chip_channels, frames * rows * width)

    def wanted(side):
        return [
            lax.dynamic_index_in_dim(flat, chip ^ ((m ^ side) // 2), 0, keepdims=False)
            for m in [0] + rest
        ]

    near, far = wanted(0), jnp.stack(wanted(top))
    got = xor_permute(far, "seq", top)

    attn_out = lax.optimization_barrier((attn_out, far))[0]
    flattened = attn_out.reshape(frames * tok_rows * tok_cols, model_width)
    partial_sum = lax.dot_general(
        w_proj, flattened, (((0,), (1,)), ((), ())), preferred_element_type=F32
    )
    step = heads // 2
    other = jnp.zeros_like(partial_sum)
    while step >= 1:
        other = xor_permute(partial_sum, "head", step)
        if step > 1:
            partial_sum = partial_sum + other
        step //= 2
    entry = entry_weight.transpose(1, 2, 3, 4, 0).reshape(27 * latent_width, channels)
    gain = norm_gain.reshape(1, channels)
    weights = [
        pltpu.VMEM((channels, min(3, f + 1) * 9 * latent_width), BF16) for f in range(frames)
    ]
    latent = pl.pallas_call(
        functools.partial(unpatchify_kernel, frames, tok_rows, tok_cols),
        out_shape=jax.ShapeDtypeStruct((latent_width, frames * rows * width), BF16),
        in_specs=[vmem(), vmem()],
        out_specs=vmem(),
        compiler_params=params(),
        name="unpatchify",
    )(partial_sum, other)

    blank = 3 - live
    hbm = pl.BlockSpec(memory_space=pl.ANY)
    grad_shape = (3, 9, chips * pad_channels, channels)
    grad = pl.pallas_call(
        functools.partial(blank_kernel, blank),
        out_shape=jax.ShapeDtypeStruct(grad_shape, F32),
        out_specs=hbm,
        scratch_shapes=[
            pltpu.VMEM((chips * pad_channels, channels), F32),
            pltpu.SemaphoreType.DMA((max(1, 9 * blank),)),
        ],
        compiler_params=params(),
        cost_estimate=cost(0, blank * 9 * out_channels * channels * 4),
        name="blank",
    )()

    across = xor_permute(latent, "seq", top)
    nears = [near[0]] + [xor_permute(near[i + 1], "seq", m) for i, m in enumerate(rest)]
    across, grad = lax.optimization_barrier((across, grad))
    got, *nears = lax.optimization_barrier((got, *nears))
    latents = jnp.concatenate([latent, across], axis=0)
    mixed = []
    masks = []
    for position, mask in enumerate([0] + rest):
        both = jnp.concatenate([latents, got[position]], axis=0)
        mixed.append(both if mask == 0 else xor_permute(both, "seq", mask))
        masks.append([mask, mask ^ top])
    swapped = xor_permute(jnp.stack(nears), "seq", 1)
    nears = nears + [swapped[i] for i in range(len(nears))]
    mixed = mixed + [xor_permute(p, "seq", 1) for p in mixed]
    masks = masks + [[m ^ 1 for m in pair] for pair in masks]
    lat_slots = (slabs, latent_width, frames * rows * width)
    cot_slots = (slabs, chip_channels, frames * rows * width)

    keep, send = pl.pallas_call(
        functools.partial(gradient_kernel, frames, rows, slabs, masks, real_rows, pad_channels),
        out_shape=(
            jax.ShapeDtypeStruct((real_rows, channels), F32),
            jax.ShapeDtypeStruct((real_rows, channels), BF16),
        ),
        in_specs=[smem(), vmem(), vmem()] + [hbm] * (len(mixed) + len(nears)),
        out_specs=(vmem(), vmem()),
        scratch_shapes=[
            pltpu.VMEM(lat_slots, BF16),
            pltpu.VMEM(cot_slots, BF16),
            pltpu.VMEM((frames, 3 * latent_width, (half_rows + 4) * width), BF16),
            pltpu.VMEM((frames, 3 * pad_channels, (half_rows + 4) * width), F32),
            pltpu.VMEM((frames * padded, lanes), BF16),
            pltpu.VMEM((channels, lanes), F32),
            pltpu.VMEM((channels, lanes), F32),
            pltpu.VMEM((channels, lanes), BF16),
            pltpu.VMEM((channels, lanes), BF16),
            pltpu.VMEM((live * padded, channels), F32),
            pltpu.VMEM((channels, LANES), F32),
            pltpu.SemaphoreType.DMA((2 * slabs,)),
        ]
        + weights,
        compiler_params=params(),
        name="gradient",
    )(me, gain, entry, *mixed, *nears)
    block = (keep + xor_permute(send, "seq", 1).astype(F32)).astype(BF16)

    columns = [m for m in range(4, slabs, 4)]
    direct = [xor_permute(block, "seq", m) for m in columns]
    beside = xor_permute(block, "seq", 2)
    conv = conv_weight.transpose(1, 2, 3, 0, 4).reshape(27, out_channels, channels)

    held = lax.optimization_barrier((block, direct[0], *mixed))[2:]
    decoded = pl.pallas_call(
        functools.partial(decode_kernel, frames, rows, slabs, masks),
        out_shape=jax.ShapeDtypeStruct((out_channels, frames, rows, width), BF16),
        in_specs=[smem(), vmem(), vmem(), hbm] + [hbm] * len(mixed),
        out_specs=vmem(),
        scratch_shapes=[
            pltpu.VMEM(lat_slots, BF16),
            pltpu.VMEM((frames, 3 * latent_width, (rows + 4) * width), BF16),
            pltpu.VMEM((channels, (rows + 2) * width), F32),
            pltpu.VMEM((channels, (rows + 2) * width), BF16),
            pltpu.VMEM((frames, 3, channels, (rows + 2) * width), BF16),
            pltpu.VMEM((channels, LANES), F32),
            pltpu.VMEM((live * 9, out_channels, channels), BF16),
            pltpu.SemaphoreType.DMA((slabs,)),
            pltpu.SemaphoreType.DMA(()),
        ]
        + weights,
        compiler_params=params(),
        name="decode",
    )(me, gain, entry, conv, *held)
    nearest = xor_permute(direct[0], "seq", 2)
    gated = lax.optimization_barrier((decoded, block, beside, nearest, *direct))
    decoded, block, beside, nearest = gated[:4]
    direct = list(gated[4:])
    across = [nearest] + [xor_permute(piece, "seq", 2) for piece in direct[1:]]

    shape = (9, pad_channels, channels)

    def finish(parts, sources, grad):
        return pl.pallas_call(
            functools.partial(finish_kernel, sources),
            out_shape=jax.ShapeDtypeStruct(grad_shape, F32),
            in_specs=[smem()] + [hbm] * (len(parts) + 1),
            out_specs=hbm,
            scratch_shapes=[
                pltpu.VMEM((len(parts),) + shape, BF16),
                pltpu.VMEM((len(parts),) + shape, F32),
                pltpu.SemaphoreType.DMA((len(parts),)),
                pltpu.SemaphoreType.DMA((len(parts),)),
            ],
            input_output_aliases={len(parts) + 1: 0},
            compiler_params=params(),
            name="finish",
        )(me, *[p.reshape(shape) for p in parts], grad)

    def both_cores(group):
        parts = [p for p, _ in group] + [xor_permute(p, "seq", 1) for p, _ in group]
        return parts, [m for _, m in group] + [m ^ 1 for _, m in group]

    early = [(block, 0), (beside, 2), (direct[0], columns[0]), (across[0], columns[0] ^ 2)]
    grad = finish(*both_cores(early), grad)
    if columns[1:]:
        gated = lax.optimization_barrier((grad, decoded, *across[1:]))
        grad, decoded, across[1:] = gated[0], gated[1], list(gated[2:])
        late = []
        for position, mask in enumerate(columns[1:]):
            late += [(direct[position + 1], mask), (across[position + 1], mask ^ 2)]
        grad = finish(*both_cores(late), grad)
    if pad_channels != chip_channels:
        grad = grad.reshape(27, chips, pad_channels, channels)[:, :, :chip_channels]
    grad = grad.reshape(3, 3, 3, out_channels, channels).transpose(3, 0, 1, 2, 4)
    return decoded, grad


def solution(mesh):
    return jax.shard_map(
        per_device,
        mesh=mesh,
        in_specs=(
            P(None, "seq", None, "head"),
            P("head", None),
            P(),
            P(),
            P("head", None, None, None, None),
            P("head", None, "seq", None),
        ),
        out_specs=(P("head", None, "seq", None), P("head", None, None, None, None)),
        check_vma=False,
    )
```

```python
import functools

import jax
import jax.numpy as jnp
from jax import lax
from jax.experimental import pallas as pl
from jax.experimental.pallas import tpu as pltpu
from jax.sharding import PartitionSpec as P

LANES = 128
VMEM_LIMIT = 56 * 1024 * 1024
F32 = jnp.float32
BF16 = jnp.bfloat16


def params():
    return pltpu.CompilerParams(vmem_limit_bytes=VMEM_LIMIT)


def cost(flops, size):
    return pl.CostEstimate(flops=flops, transcendentals=0, bytes_accessed=size)


def vmem():
    return pl.BlockSpec(memory_space=pltpu.VMEM)


def smem():
    return pl.BlockSpec(memory_space=pltpu.SMEM)


def xor_permute(x, axis, mask):
    return lax.ppermute(x, axis, [(i, i ^ mask) for i in range(lax.axis_size(axis))])


def dot(a, b):
    return lax.dot_general(a, b, (((1,), (0,)), ((), ())), preferred_element_type=F32)


def dot_t(a, b):
    return lax.dot_general(a, b, (((1,), (1,)), ((), ())), preferred_element_type=F32)


def shifted(tile, shift):
    if shift == 1:
        return tile
    lane = lax.broadcasted_iota(jnp.int32, tile.shape, 1)
    if shift == 0:
        return jnp.where(lane == 0, 0.0, pltpu.roll(tile, 1, 1))
    return jnp.where(lane == LANES - 1, 0.0, pltpu.roll(tile, LANES - 1, 1))


def fetch(piece_refs, mask_lists, slot_ref, sems):
    count = slot_ref.shape[1]
    copies = []
    for index, (piece_ref, masks) in enumerate(zip(piece_refs, mask_lists)):
        for position, mask in enumerate(masks):
            copies.append(
                pltpu.make_async_copy(
                    piece_ref.at[position, pl.ds(0, count)],
                    slot_ref.at[mask],
                    sems.at[index * len(masks) + position],
                )
            )
    for copy in copies:
        copy.start()
    return copies


def selection(tok_rows, tok_cols):
    span = tok_rows * tok_cols
    width = 2 * tok_cols
    shape = (2 * span, 3 * tok_rows * width)
    source = lax.broadcasted_iota(jnp.int32, shape, 0)
    target = lax.broadcasted_iota(jnp.int32, shape, 1)
    token = source % span
    cell = 2 * (token % tok_cols) + source // span
    shift = target // (tok_rows * width)
    same_row = token // tok_cols == (target // width) % tok_rows
    return (same_row & (target % width + shift - 1 == cell)).astype(F32).astype(BF16)


def place_latent(slot_ref, select, stack_ref, me, first_slab, slab_count, frames, rows, slabs):
    latent_width = stack_ref.shape[1] // 3
    tok_rows = rows // 2
    span = select.shape[0] // 2
    for offset in range(-1, slab_count + 1):
        slab = first_slab + offset
        inside = ((slab >= 0) & (slab < slabs)).astype(F32)
        source = jnp.clip(slab, 0, slabs - 1) ^ me
        blocks = []
        for frame in range(frames):
            for half in range(2):
                sides = [
                    slot_ref[
                        source,
                        :latent_width,
                        ((half * 2 + side) * frames + frame) * span : (
                            (half * 2 + side) * frames + frame + 1
                        )
                        * span,
                    ]
                    for side in range(2)
                ]
                blocks.append(jnp.concatenate(sides, axis=1))
        cells = dot(jnp.concatenate(blocks, axis=0), select)
        if offset in (-1, slab_count):
            cells = cells * inside
        cells = cells.astype(BF16)
        needed = range(rows)
        if offset == -1:
            needed = range(rows - 2, rows)
        if offset == slab_count:
            needed = range(2)
        for frame in range(frames):
            for row in needed:
                at_row = (frame * 2 + row % 2) * latent_width
                to = (offset * rows + row + 2) * LANES
                for shift in range(3):
                    at = (shift * tok_rows + row // 2) * LANES
                    stack_ref[
                        frame, shift * latent_width : (shift + 1) * latent_width, to : to + LANES
                    ] = cells[at_row : at_row + latent_width, at : at + LANES]


def hidden_rows(stack_ref, weight_ref, frame, first, count):
    pieces = []
    for source in range(max(0, frame - 2), frame + 1):
        for row_tap in range(3):
            at = pl.multiple_of((first + row_tap) * LANES, LANES)
            pieces.append(stack_ref[source, :, pl.ds(at, count * LANES)])
    return dot(weight_ref[...], jnp.concatenate(pieces, axis=0))


def load_entry(entry_ref, gain_ref, weight_refs, wide_gain):
    for weight_ref in weight_refs:
        depth = weight_ref.shape[1]
        start = entry_ref.shape[0] - depth
        weight_ref[...] = jnp.transpose(entry_ref[start:, :].astype(F32)).astype(BF16)
    wide_gain[...] = jnp.transpose(jnp.broadcast_to(0.5 * gain_ref[...], wide_gain.shape[::-1]))


def activate_rows(hidden_ref, gain_ref, act_ref, base, top_row, count, height):
    channels = hidden_ref.shape[0]
    block = 16
    for index in range(count):
        at = pl.multiple_of((base + index) * LANES, LANES)
        hidden = hidden_ref[:, pl.ds(at, LANES)]
        mean = jnp.sum(hidden * hidden, axis=0, keepdims=True) * (1.0 / channels)
        row = top_row + base + index
        inside = ((row >= 0) & (row < height)).astype(F32)
        inverse = jnp.broadcast_to(lax.rsqrt(mean + 1e-6) * inside, (block, LANES))
        for at_channel in range(0, channels, block):
            chunk = slice(at_channel, at_channel + block)
            half = hidden_ref[chunk, pl.ds(at, LANES)] * inverse * gain_ref[chunk, :]
            act_ref[chunk, pl.ds(at, LANES)] = (half + half * jnp.tanh(half)).astype(BF16)


def place_cotangent(
    slot_ref, flat_ref, out_ref, me, first_slab, slab_count, frames, rows, pad_channels, skip
):
    channels = slot_ref.shape[1] - skip
    half_rows = slab_count * rows
    group = 3 * pad_channels
    padded = out_ref.shape[0] // frames
    for frame in range(frames):
        for edge in (0, half_rows + 2):
            flat_ref[frame, :, edge * LANES : (edge + 2) * LANES] = jnp.zeros((group, 2 * LANES), F32)
    for offset in range(slab_count):
        source = (first_slab + offset) ^ me
        for frame in range(frames):
            for row in range(rows):
                at = (frame * rows + row) * LANES
                tile = slot_ref[source, skip:, at : at + LANES].astype(F32)
                if pad_channels != channels:
                    tile = jnp.concatenate(
                        [tile, jnp.zeros((pad_channels - channels, LANES), F32)], axis=0
                    )
                to = (offset * rows + row + 2) * LANES
                for tap in range(3):
                    flat_ref[frame, tap * pad_channels : (tap + 1) * pad_channels, to : to + LANES] = (
                        shifted(tile, 2 - tap)
                    )
    filler = [jnp.zeros((padded - 3 * group, LANES), F32)] if padded != 3 * group else []
    for frame in range(frames):
        for row in range(half_rows + 2):
            taps = [flat_ref[frame, :, (row + 2 - tap) * LANES : (row + 3 - tap) * LANES] for tap in range(3)]
            out_ref[frame * padded : (frame + 1) * padded, row * LANES : (row + 1) * LANES] = (
                jnp.concatenate(taps + filler, axis=0).astype(BF16)
            )


def gradient_kernel(frames, rows, slabs, tok_cols, masks, real_rows, pad_channels, *refs):
    me_ref, gain_ref, entry_ref = refs[:3]
    refs = refs[3:]
    piece_refs, refs = refs[: len(masks)], refs[len(masks) :]
    keep_ref, send_ref, slots, stack_ref, flat_ref, cot_ref = refs[:6]
    hid_a, hid_b, act_a, act_b, sum_ref, wide_gain, sems = refs[6:13]
    weight_refs = refs[13:]
    copies = fetch(piece_refs, masks, slots, sems)
    me = me_ref[0]
    core = me & 1
    slab_count = slabs // 2
    half_rows = slab_count * rows
    height = slabs * rows
    first_slab = core * slab_count
    padded = cot_ref.shape[0] // frames
    top_row = core * half_rows - 1
    ext = half_rows + 2
    count = max(d for d in range(1, 18) if ext % d == 0)
    width = count * LANES
    hidden = (hid_a, hid_b)
    acts = (act_a, act_b)
    load_entry(entry_ref, gain_ref, weight_refs, wide_gain)
    select = selection(rows // 2, tok_cols)
    sum_ref[...] = jnp.zeros_like(sum_ref)
    for copy in copies:
        copy.wait()
    place_latent(slots, select, stack_ref, me, first_slab, slab_count, frames, rows, slabs)
    hid_a[...] = hidden_rows(stack_ref, weight_refs[0], 0, 0, ext)
    place_cotangent(
        slots, flat_ref, cot_ref, me, first_slab, slab_count, frames, rows, pad_channels,
        stack_ref.shape[1] // 3,
    )
    for frame in range(frames):

        def chunk(step, carry):
            at = pl.multiple_of(step * width, LANES)
            if frame + 1 < frames:
                hidden[(frame + 1) % 2][:, pl.ds(at, width)] = hidden_rows(
                    stack_ref, weight_refs[frame + 1], frame + 1, step * count, count
                )
            if frame > 0:
                last = min(frames, frame + 2)
                sum_ref[0 : (last - frame + 1) * padded, :] += dot_t(
                    cot_ref[(frame - 1) * padded : last * padded, pl.ds(at, width)],
                    acts[(frame - 1) % 2][:, pl.ds(at, width)],
                )
            activate_rows(
                hidden[frame % 2], wide_gain, acts[frame % 2], step * count, top_row, count, height
            )
            return carry

        lax.fori_loop(0, ext // count, chunk, 0)
    final = frames - 1
    sum_ref[0:padded, :] += dot_t(cot_ref[final * padded : frames * padded, :], acts[final % 2][...])
    keep_at = pl.multiple_of(core * padded, 16)
    send_at = pl.multiple_of((1 - core) * padded, 16)
    keep_ref[...] = sum_ref[pl.ds(keep_at, padded), :][:real_rows]
    send_ref[...] = sum_ref[pl.ds(send_at, padded), :][:real_rows].astype(BF16)


def decode_kernel(frames, rows, slabs, tok_cols, masks, me_ref, gain_ref, entry_ref, conv_hbm, *refs):
    piece_refs, refs = refs[: len(masks)], refs[len(masks) :]
    out_ref, slots, stack_ref, hid_ref, flat_ref, act_ref, wide_gain, conv_ref, sems, sem = refs[:10]
    weight_refs = refs[10:]
    live = conv_ref.shape[0] // 9
    load = pltpu.make_async_copy(conv_hbm.at[pl.ds((3 - live) * 9, live * 9)], conv_ref, sem)
    load.start()
    copies = fetch(piece_refs, masks, slots, sems)
    me = me_ref[0]
    height = slabs * rows
    load_entry(entry_ref, gain_ref, weight_refs, wide_gain)
    select = selection(rows // 2, tok_cols)
    for copy in copies:
        copy.wait()
    place_latent(slots, select, stack_ref, me, me, 1, frames, rows, slabs)
    ext = rows + 2
    for frame in range(frames):
        hid_ref[...] = hidden_rows(stack_ref, weight_refs[frame], frame, 0, ext)
        activate_rows(hid_ref, wide_gain, flat_ref, 0, me * rows - 1, ext, height)
        for row in range(ext):
            tile = flat_ref[:, row * LANES : (row + 1) * LANES].astype(F32)
            for tap in range(3):
                act_ref[frame, tap, :, row * LANES : (row + 1) * LANES] = shifted(tile, tap).astype(BF16)
    load.wait()
    for frame in range(frames):
        kernels = []
        inputs = []
        for depth in range(max(0, 2 - frame), 3):
            for row_tap in range(3):
                for col_tap in range(3):
                    kernels.append(conv_ref[(depth - (3 - live)) * 9 + row_tap * 3 + col_tap])
                    inputs.append(
                        act_ref[frame + depth - 2, col_tap, :, row_tap * LANES : (row_tap + rows) * LANES]
                    )
        total = dot(jnp.concatenate(kernels, axis=1), jnp.concatenate(inputs, axis=0))
        for row in range(rows):
            out_ref[:, frame, row, :] = total[:, row * LANES : (row + 1) * LANES].astype(BF16)


def blank_kernel(blank, out_hbm, zero_ref, sems):
    zero_ref[...] = jnp.zeros_like(zero_ref)
    copies = [
        pltpu.make_async_copy(zero_ref, out_hbm.at[plane, tap], sems.at[plane * 9 + tap])
        for plane in range(blank)
        for tap in range(9)
    ]
    for copy in copies:
        copy.start()
    for copy in copies:
        copy.wait()


def finish_kernel(pieces, me_ref, *refs):
    count = len(pieces)
    piece_refs = refs[:count]
    out_hbm, narrow_ref, wide_ref, in_sems, out_sems = refs[count + 1 :]
    me = me_ref[0]
    channels = wide_ref.shape[2]
    loads = [
        pltpu.make_async_copy(piece_refs[index], narrow_ref.at[index], in_sems.at[index])
        for index in range(count)
    ]
    for load in loads:
        load.start()
    stores = []
    for index, mask in enumerate(pieces):
        source = me ^ mask
        loads[index].wait()
        wide_ref[index] = narrow_ref[index].astype(F32)
        at = pl.multiple_of((source >> 1) * channels, 8)
        store = pltpu.make_async_copy(
            wide_ref.at[index], out_hbm.at[2 - (source & 1), :, pl.ds(at, channels), :], out_sems.at[index]
        )
        store.start()
        stores.append(store)
    for store in stores:
        store.wait()


def per_device(attn_out, w_proj, norm_gain, entry_weight, conv_weight, cotangent):
    frames, tok_rows, tok_cols, model_width = attn_out.shape
    latent_width = entry_weight.shape[4]
    channels = entry_weight.shape[0]
    out_channels = conv_weight.shape[0]
    slabs = lax.axis_size("seq")
    heads = lax.axis_size("head")
    chips = slabs // 2
    rows = 2 * tok_rows
    width = 2 * tok_cols
    height = rows * slabs
    half_rows = height // 2
    chip_channels = out_channels // chips
    pad_channels = -(-chip_channels // 8) * 8
    real_rows = 9 * pad_channels
    padded = -(-real_rows // 16) * 16
    lanes = (half_rows + 2) * width
    live = min(3, frames)
    me_index = lax.axis_index("seq")
    me = me_index.astype(jnp.int32).reshape(1)
    top = slabs // 2
    rest = [m for m in range(2, top, 2)]

    flat = cotangent.reshape(chips, chip_channels, frames * rows * width)
    chip = me_index // 2

    def wanted(side):
        return jnp.stack(
            [
                lax.dynamic_index_in_dim(flat, chip ^ ((m ^ side) // 2), 0, keepdims=False)
                for m in [0] + rest
            ]
        )

    near, far = wanted(0), wanted(top)
    got = xor_permute(far, "seq", top)

    attn_out = lax.optimization_barrier((attn_out, far))[0]
    flattened = attn_out.reshape(frames * tok_rows * tok_cols, model_width)
    partial_sum = lax.dot_general(
        w_proj, flattened, (((0,), (1,)), ((), ())), preferred_element_type=F32
    )
    step = heads // 2
    other = jnp.zeros_like(partial_sum)
    while step >= 1:
        other = xor_permute(partial_sum, "head", step)
        if step > 1:
            partial_sum = partial_sum + other
        step //= 2
    entry = entry_weight.transpose(1, 2, 3, 4, 0).reshape(27 * latent_width, channels)
    gain = norm_gain.reshape(1, channels)
    weights = [
        pltpu.VMEM((channels, min(3, f + 1) * 9 * latent_width), BF16) for f in range(frames)
    ]
    features = (partial_sum + other).astype(BF16)
    latent = jnp.concatenate(
        [features[i * latent_width : (i + 1) * latent_width] for i in range(4)], axis=1
    )

    blank = 3 - live
    hbm = pl.BlockSpec(memory_space=pl.ANY)
    grad_shape = (3, 9, chips * pad_channels, channels)
    grad = pl.pallas_call(
        functools.partial(blank_kernel, blank),
        out_shape=jax.ShapeDtypeStruct(grad_shape, F32),
        out_specs=hbm,
        scratch_shapes=[
            pltpu.VMEM((chips * pad_channels, channels), F32),
            pltpu.SemaphoreType.DMA((max(1, 9 * blank),)),
        ],
        compiler_params=params(),
        cost_estimate=cost(0, blank * 9 * out_channels * channels * 4),
        name="blank",
    )()

    across = xor_permute(latent, "seq", top)
    across, grad = lax.optimization_barrier((across, grad))
    latents = jnp.stack([latent, across])
    pieces = []
    masks = []
    for position, mask in enumerate([0] + rest):
        both = jnp.concatenate([latents, jnp.stack([near[position], got[position]])], axis=1)
        pieces.append(both if mask == 0 else xor_permute(both, "seq", mask))
        masks.append([mask, mask ^ top])
    pieces = pieces + [xor_permute(p, "seq", 1) for p in pieces]
    masks = masks + [[m ^ 1 for m in pair] for pair in masks]
    slot_shape = (slabs, latent_width + chip_channels, frames * rows * width)

    keep, send = pl.pallas_call(
        functools.partial(
            gradient_kernel, frames, rows, slabs, tok_cols, masks, real_rows, pad_channels
        ),
        out_shape=(
            jax.ShapeDtypeStruct((real_rows, channels), F32),
            jax.ShapeDtypeStruct((real_rows, channels), BF16),
        ),
        in_specs=[smem(), vmem(), vmem()] + [hbm] * len(pieces),
        out_specs=(vmem(), vmem()),
        scratch_shapes=[
            pltpu.VMEM(slot_shape, BF16),
            pltpu.VMEM((frames, 3 * latent_width, (half_rows + 4) * width), BF16),
            pltpu.VMEM((frames, 3 * pad_channels, (half_rows + 4) * width), F32),
            pltpu.VMEM((frames * padded, lanes), BF16),
            pltpu.VMEM((channels, lanes), F32),
            pltpu.VMEM((channels, lanes), F32),
            pltpu.VMEM((channels, lanes), BF16),
            pltpu.VMEM((channels, lanes), BF16),
            pltpu.VMEM((live * padded, channels), F32),
            pltpu.VMEM((channels, LANES), F32),
            pltpu.SemaphoreType.DMA((slabs,)),
        ]
        + weights,
        compiler_params=params(),
        name="gradient",
    )(me, gain, entry, *pieces)
    block = (keep + xor_permute(send, "seq", 1).astype(F32)).astype(BF16)

    columns = [m for m in range(4, slabs, 4)]
    direct = [xor_permute(block, "seq", m) for m in columns]
    beside = xor_permute(block, "seq", 2)
    conv = conv_weight.transpose(1, 2, 3, 0, 4).reshape(27, out_channels, channels)

    held = lax.optimization_barrier((block, direct[0], *pieces))[2:]
    decoded = pl.pallas_call(
        functools.partial(decode_kernel, frames, rows, slabs, tok_cols, masks),
        out_shape=jax.ShapeDtypeStruct((out_channels, frames, rows, width), BF16),
        in_specs=[smem(), vmem(), vmem(), hbm] + [hbm] * len(pieces),
        out_specs=vmem(),
        scratch_shapes=[
            pltpu.VMEM((slabs, latent_width, frames * rows * width), BF16),
            pltpu.VMEM((frames, 3 * latent_width, (rows + 4) * width), BF16),
            pltpu.VMEM((channels, (rows + 2) * width), F32),
            pltpu.VMEM((channels, (rows + 2) * width), BF16),
            pltpu.VMEM((frames, 3, channels, (rows + 2) * width), BF16),
            pltpu.VMEM((channels, LANES), F32),
            pltpu.VMEM((live * 9, out_channels, channels), BF16),
            pltpu.SemaphoreType.DMA((slabs,)),
            pltpu.SemaphoreType.DMA(()),
        ]
        + weights,
        compiler_params=params(),
        name="decode",
    )(me, gain, entry, conv, *held)
    nearest = xor_permute(direct[0], "seq", 2)
    gated = lax.optimization_barrier((decoded, block, beside, nearest, *direct))
    decoded, block, beside, nearest = gated[:4]
    direct = list(gated[4:])
    across = [nearest] + [xor_permute(piece, "seq", 2) for piece in direct[1:]]

    shape = (9, pad_channels, channels)

    def finish(parts, sources, grad):
        return pl.pallas_call(
            functools.partial(finish_kernel, sources),
            out_shape=jax.ShapeDtypeStruct(grad_shape, F32),
            in_specs=[smem()] + [hbm] * (len(parts) + 1),
            out_specs=hbm,
            scratch_shapes=[
                pltpu.VMEM((len(parts),) + shape, BF16),
                pltpu.VMEM((len(parts),) + shape, F32),
                pltpu.SemaphoreType.DMA((len(parts),)),
                pltpu.SemaphoreType.DMA((len(parts),)),
            ],
            input_output_aliases={len(parts) + 1: 0},
            compiler_params=params(),
            cost_estimate=cost(0, len(parts) * real_rows * channels * 6),
            name="finish",
        )(me, *[p.reshape(shape) for p in parts], grad)

    def both_cores(group):
        parts = [p for p, _ in group] + [xor_permute(p, "seq", 1) for p, _ in group]
        return parts, [m for _, m in group] + [m ^ 1 for _, m in group]

    early = [(block, 0), (beside, 2), (direct[0], columns[0]), (across[0], columns[0] ^ 2)]
    grad = finish(*both_cores(early), grad)
    if columns[1:]:
        gated = lax.optimization_barrier((grad, decoded, *across[1:]))
        grad, decoded, across[1:] = gated[0], gated[1], list(gated[2:])
        late = []
        for position, mask in enumerate(columns[1:]):
            late += [(direct[position + 1], mask), (across[position + 1], mask ^ 2)]
        grad = finish(*both_cores(late), grad)
    if pad_channels != chip_channels:
        grad = grad.reshape(27, chips, pad_channels, channels)[:, :, :chip_channels]
    grad = grad.reshape(3, 3, 3, out_channels, channels).transpose(3, 0, 1, 2, 4)
    return decoded, grad


def solution(mesh):
    return jax.shard_map(
        per_device,
        mesh=mesh,
        in_specs=(
            P(None, "seq", None, "head"),
            P("head", None),
            P(),
            P(),
            P("head", None, None, None, None),
            P("head", None, "seq", None),
        ),
        out_specs=(P("head", None, "seq", None), P("head", None, None, None, None)),
        check_vma=False,
    )
```

```python
import functools

import jax
import jax.numpy as jnp
from jax import lax
from jax.experimental import pallas as pl
from jax.experimental.pallas import tpu as pltpu
from jax.sharding import PartitionSpec as P

LANES = 128
VMEM_LIMIT = 56 * 1024 * 1024
F32 = jnp.float32
BF16 = jnp.bfloat16


def params():
    return pltpu.CompilerParams(vmem_limit_bytes=VMEM_LIMIT)


def cost(flops, size):
    return pl.CostEstimate(flops=flops, transcendentals=0, bytes_accessed=size)


def vmem():
    return pl.BlockSpec(memory_space=pltpu.VMEM)


def smem():
    return pl.BlockSpec(memory_space=pltpu.SMEM)


def xor_permute(x, axis, mask):
    return lax.ppermute(x, axis, [(i, i ^ mask) for i in range(lax.axis_size(axis))])


def dot(a, b):
    return lax.dot_general(a, b, (((1,), (0,)), ((), ())), preferred_element_type=F32)


def dot_t(a, b):
    return lax.dot_general(a, b, (((1,), (1,)), ((), ())), preferred_element_type=F32)


def unpatchify_kernel(frames, tok_rows, tok_cols, own_ref, other_ref, out_ref):
    latent_width = out_ref.shape[0]
    features = (own_ref[...] + other_ref[...]).astype(BF16)
    width = 2 * tok_cols
    span = tok_rows * tok_cols
    source = lax.broadcasted_iota(jnp.int32, (span, tok_rows * width), 0)
    target = lax.broadcasted_iota(jnp.int32, (span, tok_rows * width), 1)
    same_row = source // tok_cols == target // width
    column = source % tok_cols
    even = (same_row & (target % width == 2 * column)).astype(BF16)
    odd = (same_row & (target % width == 2 * column + 1)).astype(BF16)
    for frame in range(frames):
        tokens = features[:, frame * span : (frame + 1) * span]
        left = dot(tokens, even)
        right = dot(tokens, odd)
        for row in range(tok_rows):
            cols = slice(row * width, (row + 1) * width)
            for half in range(2):
                base = half * 2 * latent_width
                cells = (
                    left[base : base + latent_width, cols]
                    + right[base + latent_width : base + 2 * latent_width, cols]
                )
                at = (frame * 2 * tok_rows + 2 * row + half) * width
                out_ref[:, at : at + width] = cells.astype(BF16)


def shifted(tile, shift):
    if shift == 1:
        return tile
    lane = lax.broadcasted_iota(jnp.int32, tile.shape, 1)
    if shift == 0:
        return jnp.where(lane == 0, 0.0, pltpu.roll(tile, 1, 1))
    return jnp.where(lane == LANES - 1, 0.0, pltpu.roll(tile, LANES - 1, 1))


def fetch(piece_refs, mask_lists, slot_ref, sems):
    count = slot_ref.shape[1]
    copies = []
    for index, (piece_ref, masks) in enumerate(zip(piece_refs, mask_lists)):
        for position, mask in enumerate(masks):
            copies.append(
                pltpu.make_async_copy(
                    piece_ref.at[position, pl.ds(0, count)],
                    slot_ref.at[mask],
                    sems.at[index * len(masks) + position],
                )
            )
    for copy in copies:
        copy.start()
    return copies


def place_latent(slot_ref, stack_ref, me, first_slab, slab_count, frames, rows, slabs):
    latent_width = stack_ref.shape[1] // 3
    for offset in range(-1, slab_count + 1):
        slab = first_slab + offset
        inside = ((slab >= 0) & (slab < slabs)).astype(F32)
        source = jnp.clip(slab, 0, slabs - 1) ^ me
        needed = range(rows)
        if offset == -1:
            needed = range(rows - 2, rows)
        if offset == slab_count:
            needed = range(2)
        for frame in range(frames):
            for row in needed:
                at = (frame * rows + row) * LANES
                tile = slot_ref[source, :latent_width, at : at + LANES].astype(F32)
                if offset in (-1, slab_count):
                    tile = tile * inside
                to = (offset * rows + row + 2) * LANES
                for shift in range(3):
                    stack_ref[
                        frame, shift * latent_width : (shift + 1) * latent_width, to : to + LANES
                    ] = shifted(tile, shift).astype(BF16)


def hidden_rows(stack_ref, weight_ref, frame, first, count):
    pieces = []
    for source in range(max(0, frame - 2), frame + 1):
        for row_tap in range(3):
            at = pl.multiple_of((first + row_tap) * LANES, LANES)
            pieces.append(stack_ref[source, :, pl.ds(at, count * LANES)])
    return dot(weight_ref[...], jnp.concatenate(pieces, axis=0))


def load_entry(entry_ref, gain_ref, weight_refs, wide_gain):
    for weight_ref in weight_refs:
        depth = weight_ref.shape[1]
        start = entry_ref.shape[0] - depth
        weight_ref[...] = jnp.transpose(entry_ref[start:, :].astype(F32)).astype(BF16)
    wide_gain[...] = jnp.transpose(jnp.broadcast_to(0.5 * gain_ref[...], wide_gain.shape[::-1]))


def activate_rows(hidden_ref, gain_ref, act_ref, base, top_row, count, height):
    channels = hidden_ref.shape[0]
    block = 16
    for index in range(count):
        at = pl.multiple_of((base + index) * LANES, LANES)
        hidden = hidden_ref[:, pl.ds(at, LANES)]
        mean = jnp.sum(hidden * hidden, axis=0, keepdims=True) * (1.0 / channels)
        row = top_row + base + index
        inside = ((row >= 0) & (row < height)).astype(F32)
        inverse = jnp.broadcast_to(lax.rsqrt(mean + 1e-6) * inside, (block, LANES))
        for at_channel in range(0, channels, block):
            chunk = slice(at_channel, at_channel + block)
            half = hidden_ref[chunk, pl.ds(at, LANES)] * inverse * gain_ref[chunk, :]
            act_ref[chunk, pl.ds(at, LANES)] = (half + half * jnp.tanh(half)).astype(BF16)


def place_cotangent(
    slot_ref, flat_ref, out_ref, me, first_slab, slab_count, frames, rows, pad_channels, skip
):
    channels = slot_ref.shape[1] - skip
    half_rows = slab_count * rows
    group = 3 * pad_channels
    padded = out_ref.shape[0] // frames
    for frame in range(frames):
        for edge in (0, half_rows + 2):
            flat_ref[frame, :, edge * LANES : (edge + 2) * LANES] = jnp.zeros((group, 2 * LANES), F32)
    for offset in range(slab_count):
        source = (first_slab + offset) ^ me
        for frame in range(frames):
            for row in range(rows):
                at = (frame * rows + row) * LANES
                tile = slot_ref[source, skip:, at : at + LANES].astype(F32)
                if pad_channels != channels:
                    tile = jnp.concatenate(
                        [tile, jnp.zeros((pad_channels - channels, LANES), F32)], axis=0
                    )
                to = (offset * rows + row + 2) * LANES
                for tap in range(3):
                    flat_ref[frame, tap * pad_channels : (tap + 1) * pad_channels, to : to + LANES] = (
                        shifted(tile, 2 - tap)
                    )
    filler = [jnp.zeros((padded - 3 * group, LANES), F32)] if padded != 3 * group else []
    for frame in range(frames):
        for row in range(half_rows + 2):
            taps = [flat_ref[frame, :, (row + 2 - tap) * LANES : (row + 3 - tap) * LANES] for tap in range(3)]
            out_ref[frame * padded : (frame + 1) * padded, row * LANES : (row + 1) * LANES] = (
                jnp.concatenate(taps + filler, axis=0).astype(BF16)
            )


def gradient_kernel(frames, rows, slabs, masks, real_rows, pad_channels, *refs):
    me_ref, gain_ref, entry_ref = refs[:3]
    refs = refs[3:]
    piece_refs, refs = refs[: len(masks)], refs[len(masks) :]
    keep_ref, send_ref, slots, stack_ref, flat_ref, cot_ref = refs[:6]
    hid_a, hid_b, act_a, act_b, sum_ref, wide_gain, sems = refs[6:13]
    weight_refs = refs[13:]
    copies = fetch(piece_refs, masks, slots, sems)
    me = me_ref[0]
    core = me & 1
    slab_count = slabs // 2
    half_rows = slab_count * rows
    height = slabs * rows
    first_slab = core * slab_count
    padded = cot_ref.shape[0] // frames
    top_row = core * half_rows - 1
    ext = half_rows + 2
    count = max(d for d in range(1, 18) if ext % d == 0)
    width = count * LANES
    hidden = (hid_a, hid_b)
    acts = (act_a, act_b)
    load_entry(entry_ref, gain_ref, weight_refs, wide_gain)
    sum_ref[...] = jnp.zeros_like(sum_ref)
    for copy in copies:
        copy.wait()
    place_latent(slots, stack_ref, me, first_slab, slab_count, frames, rows, slabs)
    hid_a[...] = hidden_rows(stack_ref, weight_refs[0], 0, 0, ext)
    place_cotangent(
        slots, flat_ref, cot_ref, me, first_slab, slab_count, frames, rows, pad_channels,
        stack_ref.shape[1] // 3,
    )
    for frame in range(frames):

        def chunk(step, carry):
            at = pl.multiple_of(step * width, LANES)
            if frame + 1 < frames:
                hidden[(frame + 1) % 2][:, pl.ds(at, width)] = hidden_rows(
                    stack_ref, weight_refs[frame + 1], frame + 1, step * count, count
                )
            if frame > 0:
                last = min(frames, frame + 2)
                sum_ref[0 : (last - frame + 1) * padded, :] += dot_t(
                    cot_ref[(frame - 1) * padded : last * padded, pl.ds(at, width)],
                    acts[(frame - 1) % 2][:, pl.ds(at, width)],
                )
            activate_rows(
                hidden[frame % 2], wide_gain, acts[frame % 2], step * count, top_row, count, height
            )
            return carry

        lax.fori_loop(0, ext // count, chunk, 0)
    final = frames - 1
    sum_ref[0:padded, :] += dot_t(cot_ref[final * padded : frames * padded, :], acts[final % 2][...])
    keep_at = pl.multiple_of(core * padded, 16)
    send_at = pl.multiple_of((1 - core) * padded, 16)
    keep_ref[...] = sum_ref[pl.ds(keep_at, padded), :][:real_rows]
    send_ref[...] = sum_ref[pl.ds(send_at, padded), :][:real_rows].astype(BF16)


def decode_kernel(frames, rows, slabs, masks, me_ref, gain_ref, entry_ref, conv_hbm, *refs):
    piece_refs, refs = refs[: len(masks)], refs[len(masks) :]
    out_ref, slots, stack_ref, hid_ref, flat_ref, act_ref, wide_gain, conv_ref, sems, sem = refs[:10]
    weight_refs = refs[10:]
    live = conv_ref.shape[0] // 9
    load = pltpu.make_async_copy(conv_hbm.at[pl.ds((3 - live) * 9, live * 9)], conv_ref, sem)
    load.start()
    copies = fetch(piece_refs, masks, slots, sems)
    me = me_ref[0]
    height = slabs * rows
    load_entry(entry_ref, gain_ref, weight_refs, wide_gain)
    for copy in copies:
        copy.wait()
    place_latent(slots, stack_ref, me, me, 1, frames, rows, slabs)
    ext = rows + 2
    for frame in range(frames):
        hid_ref[...] = hidden_rows(stack_ref, weight_refs[frame], frame, 0, ext)
        activate_rows(hid_ref, wide_gain, flat_ref, 0, me * rows - 1, ext, height)
        for row in range(ext):
            tile = flat_ref[:, row * LANES : (row + 1) * LANES].astype(F32)
            for tap in range(3):
                act_ref[frame, tap, :, row * LANES : (row + 1) * LANES] = shifted(tile, tap).astype(BF16)
    load.wait()
    for frame in range(frames):
        kernels = []
        inputs = []
        for depth in range(max(0, 2 - frame), 3):
            for row_tap in range(3):
                for col_tap in range(3):
                    kernels.append(conv_ref[(depth - (3 - live)) * 9 + row_tap * 3 + col_tap])
                    inputs.append(
                        act_ref[frame + depth - 2, col_tap, :, row_tap * LANES : (row_tap + rows) * LANES]
                    )
        total = dot(jnp.concatenate(kernels, axis=1), jnp.concatenate(inputs, axis=0))
        for row in range(rows):
            out_ref[:, frame, row, :] = total[:, row * LANES : (row + 1) * LANES].astype(BF16)


def blank_kernel(blank, out_hbm, zero_ref, sems):
    zero_ref[...] = jnp.zeros_like(zero_ref)
    copies = [
        pltpu.make_async_copy(zero_ref, out_hbm.at[plane, tap], sems.at[plane * 9 + tap])
        for plane in range(blank)
        for tap in range(9)
    ]
    for copy in copies:
        copy.start()
    for copy in copies:
        copy.wait()


def finish_kernel(pieces, me_ref, *refs):
    count = len(pieces)
    piece_refs = refs[:count]
    out_hbm, narrow_ref, wide_ref, in_sems, out_sems = refs[count + 1 :]
    me = me_ref[0]
    channels = wide_ref.shape[2]
    loads = [
        pltpu.make_async_copy(piece_refs[index], narrow_ref.at[index], in_sems.at[index])
        for index in range(count)
    ]
    for load in loads:
        load.start()
    stores = []
    for index, mask in enumerate(pieces):
        source = me ^ mask
        loads[index].wait()
        wide_ref[index] = narrow_ref[index].astype(F32)
        at = pl.multiple_of((source >> 1) * channels, 8)
        store = pltpu.make_async_copy(
            wide_ref.at[index], out_hbm.at[2 - (source & 1), :, pl.ds(at, channels), :], out_sems.at[index]
        )
        store.start()
        stores.append(store)
    for store in stores:
        store.wait()


def per_device(attn_out, w_proj, norm_gain, entry_weight, conv_weight, cotangent):
    frames, tok_rows, tok_cols, model_width = attn_out.shape
    latent_width = entry_weight.shape[4]
    channels = entry_weight.shape[0]
    out_channels = conv_weight.shape[0]
    slabs = lax.axis_size("seq")
    heads = lax.axis_size("head")
    chips = slabs // 2
    rows = 2 * tok_rows
    width = 2 * tok_cols
    height = rows * slabs
    half_rows = height // 2
    chip_channels = out_channels // chips
    pad_channels = -(-chip_channels // 8) * 8
    real_rows = 9 * pad_channels
    padded = -(-real_rows // 16) * 16
    lanes = (half_rows + 2) * width
    live = min(3, frames)
    me_index = lax.axis_index("seq")
    me = me_index.astype(jnp.int32).reshape(1)
    top = slabs // 2
    rest = [m for m in range(2, top, 2)]

    flat = cotangent.reshape(chips, chip_channels, frames * rows * width)
    chip = me_index // 2

    def wanted(side):
        return jnp.stack(
            [
                lax.dynamic_index_in_dim(flat, chip ^ ((m ^ side) // 2), 0, keepdims=False)
                for m in [0] + rest
            ]
        )

    near, far = wanted(0), wanted(top)
    got = xor_permute(far, "seq", top)

    attn_out = lax.optimization_barrier((attn_out, far))[0]
    flattened = attn_out.reshape(frames * tok_rows * tok_cols, model_width)
    partial_sum = lax.dot_general(
        w_proj, flattened, (((0,), (1,)), ((), ())), preferred_element_type=F32
    )
    step = heads // 2
    other = jnp.zeros_like(partial_sum)
    while step >= 1:
        other = xor_permute(partial_sum, "head", step)
        if step > 1:
            partial_sum = partial_sum + other
        step //= 2
    entry = entry_weight.transpose(1, 2, 3, 4, 0).reshape(27 * latent_width, channels)
    gain = norm_gain.reshape(1, channels)
    weights = [
        pltpu.VMEM((channels, min(3, f + 1) * 9 * latent_width), BF16) for f in range(frames)
    ]
    latent = pl.pallas_call(
        functools.partial(unpatchify_kernel, frames, tok_rows, tok_cols),
        out_shape=jax.ShapeDtypeStruct((latent_width, frames * rows * width), BF16),
        in_specs=[vmem(), vmem()],
        out_specs=vmem(),
        compiler_params=params(),
        name="unpatchify",
    )(partial_sum, other)

    blank = 3 - live
    hbm = pl.BlockSpec(memory_space=pl.ANY)
    grad_shape = (3, 9, chips * pad_channels, channels)
    grad = pl.pallas_call(
        functools.partial(blank_kernel, blank),
        out_shape=jax.ShapeDtypeStruct(grad_shape, F32),
        out_specs=hbm,
        scratch_shapes=[
            pltpu.VMEM((chips * pad_channels, channels), F32),
            pltpu.SemaphoreType.DMA((max(1, 9 * blank),)),
        ],
        compiler_params=params(),
        cost_estimate=cost(0, blank * 9 * out_channels * channels * 4),
        name="blank",
    )()

    across = xor_permute(latent, "seq", top)
    across, grad = lax.optimization_barrier((across, grad))
    latents = jnp.stack([latent, across])
    pieces = []
    masks = []
    for position, mask in enumerate([0] + rest):
        both = jnp.concatenate([latents, jnp.stack([near[position], got[position]])], axis=1)
        pieces.append(both if mask == 0 else xor_permute(both, "seq", mask))
        masks.append([mask, mask ^ top])
    pieces = pieces + [xor_permute(p, "seq", 1) for p in pieces]
    masks = masks + [[m ^ 1 for m in pair] for pair in masks]
    slot_shape = (slabs, latent_width + chip_channels, frames * rows * width)

    keep, send = pl.pallas_call(
        functools.partial(gradient_kernel, frames, rows, slabs, masks, real_rows, pad_channels),
        out_shape=(
            jax.ShapeDtypeStruct((real_rows, channels), F32),
            jax.ShapeDtypeStruct((real_rows, channels), BF16),
        ),
        in_specs=[smem(), vmem(), vmem()] + [hbm] * len(pieces),
        out_specs=(vmem(), vmem()),
        scratch_shapes=[
            pltpu.VMEM(slot_shape, BF16),
            pltpu.VMEM((frames, 3 * latent_width, (half_rows + 4) * width), BF16),
            pltpu.VMEM((frames, 3 * pad_channels, (half_rows + 4) * width), F32),
            pltpu.VMEM((frames * padded, lanes), BF16),
            pltpu.VMEM((channels, lanes), F32),
            pltpu.VMEM((channels, lanes), F32),
            pltpu.VMEM((channels, lanes), BF16),
            pltpu.VMEM((channels, lanes), BF16),
            pltpu.VMEM((live * padded, channels), F32),
            pltpu.VMEM((channels, LANES), F32),
            pltpu.SemaphoreType.DMA((slabs,)),
        ]
        + weights,
        compiler_params=params(),
        name="gradient",
    )(me, gain, entry, *pieces)
    block = (keep + xor_permute(send, "seq", 1).astype(F32)).astype(BF16)

    columns = [m for m in range(4, slabs, 4)]
    direct = [xor_permute(block, "seq", m) for m in columns]
    beside = xor_permute(block, "seq", 2)
    conv = conv_weight.transpose(1, 2, 3, 0, 4).reshape(27, out_channels, channels)

    held = lax.optimization_barrier((block, direct[0], *pieces))[2:]
    decoded = pl.pallas_call(
        functools.partial(decode_kernel, frames, rows, slabs, masks),
        out_shape=jax.ShapeDtypeStruct((out_channels, frames, rows, width), BF16),
        in_specs=[smem(), vmem(), vmem(), hbm] + [hbm] * len(pieces),
        out_specs=vmem(),
        scratch_shapes=[
            pltpu.VMEM((slabs, latent_width, frames * rows * width), BF16),
            pltpu.VMEM((frames, 3 * latent_width, (rows + 4) * width), BF16),
            pltpu.VMEM((channels, (rows + 2) * width), F32),
            pltpu.VMEM((channels, (rows + 2) * width), BF16),
            pltpu.VMEM((frames, 3, channels, (rows + 2) * width), BF16),
            pltpu.VMEM((channels, LANES), F32),
            pltpu.VMEM((live * 9, out_channels, channels), BF16),
            pltpu.SemaphoreType.DMA((slabs,)),
            pltpu.SemaphoreType.DMA(()),
        ]
        + weights,
        compiler_params=params(),
        name="decode",
    )(me, gain, entry, conv, *held)
    nearest = xor_permute(direct[0], "seq", 2)
    gated = lax.optimization_barrier((decoded, block, beside, nearest, *direct))
    decoded, block, beside, nearest = gated[:4]
    direct = list(gated[4:])
    across = [nearest] + [xor_permute(piece, "seq", 2) for piece in direct[1:]]

    shape = (9, pad_channels, channels)

    def finish(parts, sources, grad):
        return pl.pallas_call(
            functools.partial(finish_kernel, sources),
            out_shape=jax.ShapeDtypeStruct(grad_shape, F32),
            in_specs=[smem()] + [hbm] * (len(parts) + 1),
            out_specs=hbm,
            scratch_shapes=[
                pltpu.VMEM((len(parts),) + shape, BF16),
                pltpu.VMEM((len(parts),) + shape, F32),
                pltpu.SemaphoreType.DMA((len(parts),)),
                pltpu.SemaphoreType.DMA((len(parts),)),
            ],
            input_output_aliases={len(parts) + 1: 0},
            compiler_params=params(),
            cost_estimate=cost(0, len(parts) * real_rows * channels * 6),
            name="finish",
        )(me, *[p.reshape(shape) for p in parts], grad)

    def both_cores(group):
        parts = [p for p, _ in group] + [xor_permute(p, "seq", 1) for p, _ in group]
        return parts, [m for _, m in group] + [m ^ 1 for _, m in group]

    early = [(block, 0), (beside, 2), (direct[0], columns[0]), (across[0], columns[0] ^ 2)]
    grad = finish(*both_cores(early), grad)
    if columns[1:]:
        gated = lax.optimization_barrier((grad, decoded, *across[1:]))
        grad, decoded, across[1:] = gated[0], gated[1], list(gated[2:])
        late = []
        for position, mask in enumerate(columns[1:]):
            late += [(direct[position + 1], mask), (across[position + 1], mask ^ 2)]
        grad = finish(*both_cores(late), grad)
    if pad_channels != chip_channels:
        grad = grad.reshape(27, chips, pad_channels, channels)[:, :, :chip_channels]
    grad = grad.reshape(3, 3, 3, out_channels, channels).transpose(3, 0, 1, 2, 4)
    return decoded, grad


def solution(mesh):
    return jax.shard_map(
        per_device,
        mesh=mesh,
        in_specs=(
            P(None, "seq", None, "head"),
            P("head", None),
            P(),
            P(),
            P("head", None, None, None, None),
            P("head", None, "seq", None),
        ),
        out_specs=(P("head", None, "seq", None), P("head", None, None, None, None)),
        check_vma=False,
    )
```

```python
import functools

import jax
import jax.numpy as jnp
from jax import lax
from jax.experimental import pallas as pl
from jax.experimental.pallas import tpu as pltpu
from jax.sharding import PartitionSpec as P

LANES = 128
VMEM_LIMIT = 56 * 1024 * 1024
F32 = jnp.float32
BF16 = jnp.bfloat16


def params():
    return pltpu.CompilerParams(vmem_limit_bytes=VMEM_LIMIT)


def cost(flops, size):
    return pl.CostEstimate(flops=flops, transcendentals=0, bytes_accessed=size)


def vmem():
    return pl.BlockSpec(memory_space=pltpu.VMEM)


def smem():
    return pl.BlockSpec(memory_space=pltpu.SMEM)


def xor_permute(x, axis, mask):
    return lax.ppermute(x, axis, [(i, i ^ mask) for i in range(lax.axis_size(axis))])


def dot(a, b):
    return lax.dot_general(a, b, (((1,), (0,)), ((), ())), preferred_element_type=F32)


def dot_t(a, b):
    return lax.dot_general(a, b, (((1,), (1,)), ((), ())), preferred_element_type=F32)


def unpatchify_kernel(frames, tok_rows, tok_cols, sum_ref, out_ref):
    latent_width = out_ref.shape[0]
    features = sum_ref[...]
    width = 2 * tok_cols
    span = tok_rows * tok_cols
    source = lax.broadcasted_iota(jnp.int32, (span, tok_rows * width), 0)
    target = lax.broadcasted_iota(jnp.int32, (span, tok_rows * width), 1)
    same_row = source // tok_cols == target // width
    column = source % tok_cols
    even = (same_row & (target % width == 2 * column)).astype(BF16)
    odd = (same_row & (target % width == 2 * column + 1)).astype(BF16)
    for frame in range(frames):
        tokens = features[:, frame * span : (frame + 1) * span]
        left = dot(tokens, even)
        right = dot(tokens, odd)
        for row in range(tok_rows):
            cols = slice(row * width, (row + 1) * width)
            for half in range(2):
                base = half * 2 * latent_width
                cells = (
                    left[base : base + latent_width, cols]
                    + right[base + latent_width : base + 2 * latent_width, cols]
                )
                at = (frame * 2 * tok_rows + 2 * row + half) * width
                out_ref[:, at : at + width] = cells.astype(BF16)


def shifted(tile, shift):
    if shift == 1:
        return tile
    lane = lax.broadcasted_iota(jnp.int32, tile.shape, 1)
    if shift == 0:
        return jnp.where(lane == 0, 0.0, pltpu.roll(tile, 1, 1))
    return jnp.where(lane == LANES - 1, 0.0, pltpu.roll(tile, LANES - 1, 1))


def fetch(piece_refs, mask_lists, slot_ref, sems):
    count = slot_ref.shape[1]
    copies = []
    for index, (piece_ref, masks) in enumerate(zip(piece_refs, mask_lists)):
        for position, mask in enumerate(masks):
            copies.append(
                pltpu.make_async_copy(
                    piece_ref.at[position, pl.ds(0, count)],
                    slot_ref.at[mask],
                    sems.at[index * len(masks) + position],
                )
            )
    for copy in copies:
        copy.start()
    return copies


def place_latent(slot_ref, stack_ref, me, first_slab, slab_count, frames, rows, slabs):
    latent_width = stack_ref.shape[1] // 3
    for offset in range(-1, slab_count + 1):
        slab = first_slab + offset
        inside = ((slab >= 0) & (slab < slabs)).astype(F32)
        source = jnp.clip(slab, 0, slabs - 1) ^ me
        needed = range(rows)
        if offset == -1:
            needed = range(rows - 2, rows)
        if offset == slab_count:
            needed = range(2)
        for frame in range(frames):
            for row in needed:
                at = (frame * rows + row) * LANES
                tile = slot_ref[source, :latent_width, at : at + LANES].astype(F32)
                if offset in (-1, slab_count):
                    tile = tile * inside
                to = (offset * rows + row + 2) * LANES
                for shift in range(3):
                    stack_ref[
                        frame, shift * latent_width : (shift + 1) * latent_width, to : to + LANES
                    ] = shifted(tile, shift).astype(BF16)


def hidden_rows(stack_ref, weight_ref, frame, first, count):
    pieces = []
    for source in range(max(0, frame - 2), frame + 1):
        for row_tap in range(3):
            at = pl.multiple_of((first + row_tap) * LANES, LANES)
            pieces.append(stack_ref[source, :, pl.ds(at, count * LANES)])
    return dot(weight_ref[...], jnp.concatenate(pieces, axis=0))


def load_entry(entry_ref, gain_ref, weight_refs, wide_gain):
    for weight_ref in weight_refs:
        depth = weight_ref.shape[1]
        start = entry_ref.shape[0] - depth
        weight_ref[...] = jnp.transpose(entry_ref[start:, :].astype(F32)).astype(BF16)
    wide_gain[...] = jnp.transpose(jnp.broadcast_to(0.5 * gain_ref[...], wide_gain.shape[::-1]))


def activate_rows(hidden_ref, gain_ref, act_ref, base, top_row, count, height):
    channels = hidden_ref.shape[0]
    block = 16
    for index in range(count):
        at = pl.multiple_of((base + index) * LANES, LANES)
        hidden = hidden_ref[:, pl.ds(at, LANES)]
        mean = jnp.sum(hidden * hidden, axis=0, keepdims=True) * (1.0 / channels)
        row = top_row + base + index
        inside = ((row >= 0) & (row < height)).astype(F32)
        inverse = jnp.broadcast_to(lax.rsqrt(mean + 1e-6) * inside, (block, LANES))
        for at_channel in range(0, channels, block):
            chunk = slice(at_channel, at_channel + block)
            half = hidden_ref[chunk, pl.ds(at, LANES)] * inverse * gain_ref[chunk, :]
            act_ref[chunk, pl.ds(at, LANES)] = (half + half * jnp.tanh(half)).astype(BF16)


def place_cotangent(
    slot_ref, flat_ref, out_ref, me, first_slab, slab_count, frames, rows, pad_channels, skip
):
    channels = slot_ref.shape[1] - skip
    half_rows = slab_count * rows
    group = 3 * pad_channels
    padded = out_ref.shape[0] // frames
    for frame in range(frames):
        for edge in (0, half_rows + 2):
            flat_ref[frame, :, edge * LANES : (edge + 2) * LANES] = jnp.zeros((group, 2 * LANES), F32)
    for offset in range(slab_count):
        source = (first_slab + offset) ^ me
        for frame in range(frames):
            for row in range(rows):
                at = (frame * rows + row) * LANES
                tile = slot_ref[source, skip:, at : at + LANES].astype(F32)
                if pad_channels != channels:
                    tile = jnp.concatenate(
                        [tile, jnp.zeros((pad_channels - channels, LANES), F32)], axis=0
                    )
                to = (offset * rows + row + 2) * LANES
                for tap in range(3):
                    flat_ref[frame, tap * pad_channels : (tap + 1) * pad_channels, to : to + LANES] = (
                        shifted(tile, 2 - tap)
                    )
    filler = [jnp.zeros((padded - 3 * group, LANES), F32)] if padded != 3 * group else []
    for frame in range(frames):
        for row in range(half_rows + 2):
            taps = [flat_ref[frame, :, (row + 2 - tap) * LANES : (row + 3 - tap) * LANES] for tap in range(3)]
            out_ref[frame * padded : (frame + 1) * padded, row * LANES : (row + 1) * LANES] = (
                jnp.concatenate(taps + filler, axis=0).astype(BF16)
            )


def gradient_kernel(frames, rows, slabs, masks, real_rows, pad_channels, *refs):
    me_ref, gain_ref, entry_ref = refs[:3]
    refs = refs[3:]
    piece_refs, refs = refs[: len(masks)], refs[len(masks) :]
    keep_ref, send_ref, slots, stack_ref, flat_ref, cot_ref = refs[:6]
    hid_a, hid_b, act_a, act_b, sum_ref, wide_gain, sems = refs[6:13]
    weight_refs = refs[13:]
    copies = fetch(piece_refs, masks, slots, sems)
    me = me_ref[0]
    core = me & 1
    slab_count = slabs // 2
    half_rows = slab_count * rows
    height = slabs * rows
    first_slab = core * slab_count
    padded = cot_ref.shape[0] // frames
    top_row = core * half_rows - 1
    ext = half_rows + 2
    count = max(d for d in range(1, 18) if ext % d == 0)
    width = count * LANES
    hidden = (hid_a, hid_b)
    acts = (act_a, act_b)
    load_entry(entry_ref, gain_ref, weight_refs, wide_gain)
    sum_ref[...] = jnp.zeros_like(sum_ref)
    for copy in copies:
        copy.wait()
    place_latent(slots, stack_ref, me, first_slab, slab_count, frames, rows, slabs)
    hid_a[...] = hidden_rows(stack_ref, weight_refs[0], 0, 0, ext)
    place_cotangent(
        slots, flat_ref, cot_ref, me, first_slab, slab_count, frames, rows, pad_channels,
        stack_ref.shape[1] // 3,
    )
    for frame in range(frames):

        def chunk(step, carry):
            at = pl.multiple_of(step * width, LANES)
            if frame + 1 < frames:
                hidden[(frame + 1) % 2][:, pl.ds(at, width)] = hidden_rows(
                    stack_ref, weight_refs[frame + 1], frame + 1, step * count, count
                )
            if frame > 0:
                last = min(frames, frame + 2)
                sum_ref[0 : (last - frame + 1) * padded, :] += dot_t(
                    cot_ref[(frame - 1) * padded : last * padded, pl.ds(at, width)],
                    acts[(frame - 1) % 2][:, pl.ds(at, width)],
                )
            activate_rows(
                hidden[frame % 2], wide_gain, acts[frame % 2], step * count, top_row, count, height
            )
            return carry

        lax.fori_loop(0, ext // count, chunk, 0)
    final = frames - 1
    sum_ref[0:padded, :] += dot_t(cot_ref[final * padded : frames * padded, :], acts[final % 2][...])
    keep_at = pl.multiple_of(core * padded, 16)
    send_at = pl.multiple_of((1 - core) * padded, 16)
    keep_ref[...] = sum_ref[pl.ds(keep_at, padded), :][:real_rows]
    send_ref[...] = sum_ref[pl.ds(send_at, padded), :][:real_rows].astype(BF16)


def decode_kernel(frames, rows, slabs, masks, me_ref, gain_ref, entry_ref, conv_hbm, *refs):
    piece_refs, refs = refs[: len(masks)], refs[len(masks) :]
    out_ref, slots, stack_ref, hid_ref, flat_ref, act_ref, wide_gain, conv_ref, sems, sem = refs[:10]
    weight_refs = refs[10:]
    live = conv_ref.shape[0] // 9
    load = pltpu.make_async_copy(conv_hbm.at[pl.ds((3 - live) * 9, live * 9)], conv_ref, sem)
    load.start()
    copies = fetch(piece_refs, masks, slots, sems)
    me = me_ref[0]
    height = slabs * rows
    load_entry(entry_ref, gain_ref, weight_refs, wide_gain)
    for copy in copies:
        copy.wait()
    place_latent(slots, stack_ref, me, me, 1, frames, rows, slabs)
    ext = rows + 2
    for frame in range(frames):
        hid_ref[...] = hidden_rows(stack_ref, weight_refs[frame], frame, 0, ext)
        activate_rows(hid_ref, wide_gain, flat_ref, 0, me * rows - 1, ext, height)
        for row in range(ext):
            tile = flat_ref[:, row * LANES : (row + 1) * LANES].astype(F32)
            for tap in range(3):
                act_ref[frame, tap, :, row * LANES : (row + 1) * LANES] = shifted(tile, tap).astype(BF16)
    load.wait()
    for frame in range(frames):
        kernels = []
        inputs = []
        for depth in range(max(0, 2 - frame), 3):
            for row_tap in range(3):
                for col_tap in range(3):
                    kernels.append(conv_ref[(depth - (3 - live)) * 9 + row_tap * 3 + col_tap])
                    inputs.append(
                        act_ref[frame + depth - 2, col_tap, :, row_tap * LANES : (row_tap + rows) * LANES]
                    )
        total = dot(jnp.concatenate(kernels, axis=1), jnp.concatenate(inputs, axis=0))
        for row in range(rows):
            out_ref[:, frame, row, :] = total[:, row * LANES : (row + 1) * LANES].astype(BF16)


def blank_kernel(blank, out_hbm, zero_ref, sems):
    zero_ref[...] = jnp.zeros_like(zero_ref)
    copies = [
        pltpu.make_async_copy(zero_ref, out_hbm.at[plane, tap], sems.at[plane * 9 + tap])
        for plane in range(blank)
        for tap in range(9)
    ]
    for copy in copies:
        copy.start()
    for copy in copies:
        copy.wait()


def finish_kernel(pieces, me_ref, *refs):
    count = len(pieces)
    piece_refs = refs[:count]
    out_hbm, narrow_ref, wide_ref, in_sems, out_sems = refs[count + 1 :]
    me = me_ref[0]
    channels = wide_ref.shape[2]
    loads = [
        pltpu.make_async_copy(piece_refs[index], narrow_ref.at[index], in_sems.at[index])
        for index in range(count)
    ]
    for load in loads:
        load.start()
    stores = []
    for index, mask in enumerate(pieces):
        source = me ^ mask
        loads[index].wait()
        wide_ref[index] = narrow_ref[index].astype(F32)
        at = pl.multiple_of((source >> 1) * channels, 8)
        store = pltpu.make_async_copy(
            wide_ref.at[index], out_hbm.at[2 - (source & 1), :, pl.ds(at, channels), :], out_sems.at[index]
        )
        store.start()
        stores.append(store)
    for store in stores:
        store.wait()


def per_device(attn_out, w_proj, norm_gain, entry_weight, conv_weight, cotangent):
    frames, tok_rows, tok_cols, model_width = attn_out.shape
    latent_width = entry_weight.shape[4]
    channels = entry_weight.shape[0]
    out_channels = conv_weight.shape[0]
    slabs = lax.axis_size("seq")
    heads = lax.axis_size("head")
    chips = slabs // 2
    rows = 2 * tok_rows
    width = 2 * tok_cols
    height = rows * slabs
    half_rows = height // 2
    chip_channels = out_channels // chips
    pad_channels = -(-chip_channels // 8) * 8
    real_rows = 9 * pad_channels
    padded = -(-real_rows // 16) * 16
    lanes = (half_rows + 2) * width
    live = min(3, frames)
    me_index = lax.axis_index("seq")
    me = me_index.astype(jnp.int32).reshape(1)
    top = slabs // 2
    rest = [m for m in range(2, top, 2)]

    flat = cotangent.reshape(chips, chip_channels, frames * rows * width)
    chip = me_index // 2

    def wanted(side):
        return jnp.stack(
            [
                lax.dynamic_index_in_dim(flat, chip ^ ((m ^ side) // 2), 0, keepdims=False)
                for m in [0] + rest
            ]
        )

    near, far = wanted(0), wanted(top)
    got = xor_permute(far, "seq", top)

    attn_out = lax.optimization_barrier((attn_out, far))[0]
    flattened = attn_out.reshape(frames * tok_rows * tok_cols, model_width)
    partial_sum = lax.dot_general(
        w_proj, flattened, (((0,), (1,)), ((), ())), preferred_element_type=F32
    )
    step = heads // 2
    other = jnp.zeros_like(partial_sum)
    while step >= 1:
        other = xor_permute(partial_sum, "head", step)
        if step > 1:
            partial_sum = partial_sum + other
        step //= 2
    entry = entry_weight.transpose(1, 2, 3, 4, 0).reshape(27 * latent_width, channels)
    gain = norm_gain.reshape(1, channels)
    weights = [
        pltpu.VMEM((channels, min(3, f + 1) * 9 * latent_width), BF16) for f in range(frames)
    ]
    latent = pl.pallas_call(
        functools.partial(unpatchify_kernel, frames, tok_rows, tok_cols),
        out_shape=jax.ShapeDtypeStruct((latent_width, frames * rows * width), BF16),
        in_specs=[vmem()],
        out_specs=vmem(),
        compiler_params=params(),
        name="unpatchify",
    )((partial_sum + other).astype(BF16))

    blank = 3 - live
    hbm = pl.BlockSpec(memory_space=pl.ANY)
    grad_shape = (3, 9, chips * pad_channels, channels)
    grad = pl.pallas_call(
        functools.partial(blank_kernel, blank),
        out_shape=jax.ShapeDtypeStruct(grad_shape, F32),
        out_specs=hbm,
        scratch_shapes=[
            pltpu.VMEM((chips * pad_channels, channels), F32),
            pltpu.SemaphoreType.DMA((max(1, 9 * blank),)),
        ],
        compiler_params=params(),
        cost_estimate=cost(0, blank * 9 * out_channels * channels * 4),
        name="blank",
    )()

    across = xor_permute(latent, "seq", top)
    across, grad = lax.optimization_barrier((across, grad))
    latents = jnp.stack([latent, across])
    pieces = []
    masks = []
    for position, mask in enumerate([0] + rest):
        both = jnp.concatenate([latents, jnp.stack([near[position], got[position]])], axis=1)
        pieces.append(both if mask == 0 else xor_permute(both, "seq", mask))
        masks.append([mask, mask ^ top])
    pieces = pieces + [xor_permute(p, "seq", 1) for p in pieces]
    masks = masks + [[m ^ 1 for m in pair] for pair in masks]
    slot_shape = (slabs, latent_width + chip_channels, frames * rows * width)

    keep, send = pl.pallas_call(
        functools.partial(gradient_kernel, frames, rows, slabs, masks, real_rows, pad_channels),
        out_shape=(
            jax.ShapeDtypeStruct((real_rows, channels), F32),
            jax.ShapeDtypeStruct((real_rows, channels), BF16),
        ),
        in_specs=[smem(), vmem(), vmem()] + [hbm] * len(pieces),
        out_specs=(vmem(), vmem()),
        scratch_shapes=[
            pltpu.VMEM(slot_shape, BF16),
            pltpu.VMEM((frames, 3 * latent_width, (half_rows + 4) * width), BF16),
            pltpu.VMEM((frames, 3 * pad_channels, (half_rows + 4) * width), F32),
            pltpu.VMEM((frames * padded, lanes), BF16),
            pltpu.VMEM((channels, lanes), F32),
            pltpu.VMEM((channels, lanes), F32),
            pltpu.VMEM((channels, lanes), BF16),
            pltpu.VMEM((channels, lanes), BF16),
            pltpu.VMEM((live * padded, channels), F32),
            pltpu.VMEM((channels, LANES), F32),
            pltpu.SemaphoreType.DMA((slabs,)),
        ]
        + weights,
        compiler_params=params(),
        name="gradient",
    )(me, gain, entry, *pieces)
    block = (keep + xor_permute(send, "seq", 1).astype(F32)).astype(BF16)

    columns = [m for m in range(4, slabs, 4)]
    direct = [xor_permute(block, "seq", m) for m in columns]
    beside = xor_permute(block, "seq", 2)
    conv = conv_weight.transpose(1, 2, 3, 0, 4).reshape(27, out_channels, channels)

    held = lax.optimization_barrier((block, direct[0], *pieces))[2:]
    decoded = pl.pallas_call(
        functools.partial(decode_kernel, frames, rows, slabs, masks),
        out_shape=jax.ShapeDtypeStruct((out_channels, frames, rows, width), BF16),
        in_specs=[smem(), vmem(), vmem(), hbm] + [hbm] * len(pieces),
        out_specs=vmem(),
        scratch_shapes=[
            pltpu.VMEM((slabs, latent_width, frames * rows * width), BF16),
            pltpu.VMEM((frames, 3 * latent_width, (rows + 4) * width), BF16),
            pltpu.VMEM((channels, (rows + 2) * width), F32),
            pltpu.VMEM((channels, (rows + 2) * width), BF16),
            pltpu.VMEM((frames, 3, channels, (rows + 2) * width), BF16),
            pltpu.VMEM((channels, LANES), F32),
            pltpu.VMEM((live * 9, out_channels, channels), BF16),
            pltpu.SemaphoreType.DMA((slabs,)),
            pltpu.SemaphoreType.DMA(()),
        ]
        + weights,
        compiler_params=params(),
        name="decode",
    )(me, gain, entry, conv, *held)
    nearest = xor_permute(direct[0], "seq", 2)
    gated = lax.optimization_barrier((decoded, block, beside, nearest, *direct))
    decoded, block, beside, nearest = gated[:4]
    direct = list(gated[4:])
    across = [nearest] + [xor_permute(piece, "seq", 2) for piece in direct[1:]]

    shape = (9, pad_channels, channels)

    def finish(parts, sources, grad):
        return pl.pallas_call(
            functools.partial(finish_kernel, sources),
            out_shape=jax.ShapeDtypeStruct(grad_shape, F32),
            in_specs=[smem()] + [hbm] * (len(parts) + 1),
            out_specs=hbm,
            scratch_shapes=[
                pltpu.VMEM((len(parts),) + shape, BF16),
                pltpu.VMEM((len(parts),) + shape, F32),
                pltpu.SemaphoreType.DMA((len(parts),)),
                pltpu.SemaphoreType.DMA((len(parts),)),
            ],
            input_output_aliases={len(parts) + 1: 0},
            compiler_params=params(),
            cost_estimate=cost(0, len(parts) * real_rows * channels * 6),
            name="finish",
        )(me, *[p.reshape(shape) for p in parts], grad)

    def both_cores(group):
        parts = [p for p, _ in group] + [xor_permute(p, "seq", 1) for p, _ in group]
        return parts, [m for _, m in group] + [m ^ 1 for _, m in group]

    early = [(block, 0), (beside, 2), (direct[0], columns[0]), (across[0], columns[0] ^ 2)]
    grad = finish(*both_cores(early), grad)
    if columns[1:]:
        gated = lax.optimization_barrier((grad, decoded, *across[1:]))
        grad, decoded, across[1:] = gated[0], gated[1], list(gated[2:])
        late = []
        for position, mask in enumerate(columns[1:]):
            late += [(direct[position + 1], mask), (across[position + 1], mask ^ 2)]
        grad = finish(*both_cores(late), grad)
    if pad_channels != chip_channels:
        grad = grad.reshape(27, chips, pad_channels, channels)[:, :, :chip_channels]
    grad = grad.reshape(3, 3, 3, out_channels, channels).transpose(3, 0, 1, 2, 4)
    return decoded, grad


def solution(mesh):
    return jax.shard_map(
        per_device,
        mesh=mesh,
        in_specs=(
            P(None, "seq", None, "head"),
            P("head", None),
            P(),
            P(),
            P("head", None, None, None, None),
            P("head", None, "seq", None),
        ),
        out_specs=(P("head", None, "seq", None), P("head", None, None, None, None)),
        check_vma=False,
    )
```
